32 devices in a mesh: dp: 8 (over z, y), fsdp: 4 (over x, core).
Axes of the slice: x: 2, y: 2, z: 4, core: 2. Of those that a mesh axis runs over, the one named last changes fastest.
Arguments:
- tokens: bfloat16 [64, 1024, 768], P(('dp', 'fsdp')), may hold values from -6 to 6
- lengths: int32 [64], replicated, may hold values from 128 to 1024, as said below
- deal_order: int32 [64], replicated, may hold values from 0 to 63, as said below
- qkv_weight: bfloat16 [768, 2304], P(('dp', 'fsdp')), may hold values from -0.21875 to 0.21875
- query_bias: bfloat16 [768], P(('dp', 'fsdp')), may hold values from -3 to 3
- value_bias: bfloat16 [768], P(('dp', 'fsdp')), may hold values from -3 to 3
- out_weight: bfloat16 [768, 768], P(('dp', 'fsdp')), may hold values from -0.875 to 0.875
- out_bias: bfloat16 [768], P(('dp', 'fsdp')), may hold values from -3 to 3
- attn_gain: bfloat16 [768], P(('dp', 'fsdp')), may hold values from 0.5 to 1.5
- attn_shift: bfloat16 [768], P(('dp', 'fsdp')), may hold values from -2 to 2
- up_weight: bfloat16 [768, 3072], P(('dp', 'fsdp')), may hold values from -0.21875 to 0.21875
- up_bias: bfloat16 [3072], P(('dp', 'fsdp')), may hold values from -3 to 3
- down_weight: bfloat16 [3072, 768], P(('dp', 'fsdp')), may hold values from -0.109375 to 0.109375
- down_bias: bfloat16 [768], P(('dp', 'fsdp')), may hold values from -3 to 3
- ffn_gain: bfloat16 [768], P(('dp', 'fsdp')), may hold values from 0.5 to 1.5
- ffn_shift: bfloat16 [768], P(('dp', 'fsdp')), may hold values from -2 to 2
- cotangent: bfloat16 [64, 1024, 768], P(('dp', 'fsdp')), may hold values from -6 to 6
Outputs:
- layer_out: bfloat16 [64, 1024, 768], P(('dp', 'fsdp'))
- input_grad: bfloat16 [64, 1024, 768], P(('dp', 'fsdp'))
- qkvw_grad: float32 [768, 2304], P(('dp', 'fsdp'))
- qbias_grad: float32 [768], P(('dp', 'fsdp'))
- vbias_grad: float32 [768], P(('dp', 'fsdp'))
- outw_grad: float32 [768, 768], P(('dp', 'fsdp'))
- outb_grad: float32 [768], P(('dp', 'fsdp'))
- gaina_grad: float32 [768], P(('dp', 'fsdp'))
- shifta_grad: float32 [768], P(('dp', 'fsdp'))
- upw_grad: float32 [768, 3072], P(('dp', 'fsdp'))
- upb_grad: float32 [3072], P(('dp', 'fsdp'))
- downw_grad: float32 [3072, 768], P(('dp', 'fsdp'))
- downb_grad: float32 [768], P(('dp', 'fsdp'))
- gainf_grad: float32 [768], P(('dp', 'fsdp'))
- shiftf_grad: float32 [768], P(('dp', 'fsdp'))
- branch_rms: float32 [64, 3], P(('dp', 'fsdp'))
The draws below stay inside these ranges and needn't reach their ends.
Inputs may be any that keep to these rules, and one draw needn't show every extreme that they name: `lengths`: some sequence has exactly 1024 valid tokens and some exactly 128. `deal_order`: A permutation of the sequences that maps each aligned block of 8 sequences onto itself; the 2 sequences of an aligned block of 2 go to 2 different aligned blocks of 2.
All inputs are finite; a program needn't handle non-finite values.
Results may differ from the reference program's by a relative error of at most 0.014.
The reference program's roundings to bfloat16 on the way count: a program that leaves them out, or rounds other values in their place, can miss the bound.
Values may be sent and summed in bfloat16 or wider, within the bound.
A program may use at most 448 MiB of HBM per device.

```python
import math
import jax
import jax.numpy as jnp
from jax import lax

D = 768
HEADS = 12
HEAD_DIM = 64
FF = 3072
LEN = 1024
MIN_LEN = 128
BLOCK = 512
SEQ_DEV = 2
SEQS = 64
COLUMN = 8
N_DP = 8
N_FSDP = 4


def draw_lengths(key, part):
    key_one, key_two = jax.random.split(key)
    drawn_lengths = jax.random.randint(key_one, (SEQS,), MIN_LEN, LEN + 1)
    positions = jax.random.permutation(key_two, SEQS)
    drawn_lengths = drawn_lengths.at[positions[0]].set(LEN)
    drawn_lengths = drawn_lengths.at[positions[1]].set(MIN_LEN)
    return drawn_lengths.astype(jnp.int32)


def deal_group(group_key):
    key_one, key_two, key_three = jax.random.split(group_key, 3)
    outer_perm = jax.random.permutation(key_one, N_FSDP)
    inner_perm = jax.random.permutation(key_two, N_FSDP)
    sender = jnp.arange(N_FSDP)[:, None]
    within = jnp.arange(SEQ_DEV)[None, :]
    target = outer_perm[(inner_perm[sender] + within) % N_FSDP]
    orders = jax.vmap(lambda each_key: jax.random.permutation(each_key, SEQ_DEV))(jax.random.split(key_three, N_FSDP))
    landing = orders[target, jnp.broadcast_to(within, target.shape)]
    return (target * SEQ_DEV + landing).reshape(-1)


def draw_deal_order(key, part):
    groups = jax.vmap(deal_group)(jax.random.split(key, N_DP))
    offsets = (jnp.arange(N_DP) * COLUMN)[:, None]
    return (groups + offsets).reshape(-1).astype(jnp.int32)


def strengthened(entries, key, source, target, shards_of, factor):
    owner, partner = [(jnp.arange(entries.shape[dim]) // (entries.shape[dim] // shards_of)).reshape([-1 if axis == dim else 1 for axis in range(entries.ndim)]) for dim in (source, target)]
    chosen = jax.random.permutation(key, shards_of)[partner]
    strong = (owner == chosen) | (owner == (partner + shards_of // 2) % shards_of)
    return jnp.where(strong, factor * entries, entries)


def shard_levels(rng, shape, cuts, least, top_value):
    def one(position, blocks):
        heights = jax.random.uniform(jax.random.fold_in(jax.random.fold_in(rng, 6), position), (blocks,), jnp.float32, least / len(cuts), top_value / len(cuts))
        return jnp.repeat(jnp.exp(heights), shape[position] // blocks).reshape((-1,) + (1,) * (len(shape) - position - 1))

    factor_of = one(*cuts[0])
    for cut in cuts[1:]:
        factor_of = factor_of * one(*cut)
    return factor_of


def normal_values(key, dims, scale, most, cuts=(), held_as=jnp.bfloat16):
    drawn = scale * jax.random.normal(key, dims, jnp.float32)
    if cuts:
        drawn = drawn * shard_levels(key, dims, cuts, -0.22, 0.18)
    return jnp.clip(drawn, -most, most).astype(held_as)


def noise_with(key, shape, scale, limit, cuts, heavy, dtype=jnp.bfloat16):
    values = scale * jax.random.normal(key, shape, jnp.float32)
    if cuts:
        values = values * shard_levels(key, shape, cuts, -0.22, 0.18)
    return jnp.clip(strengthened(values, jax.random.fold_in(key, 3), *heavy), -limit, limit).astype(dtype)


def setup_inputs(seed: int = 0) -> dict:
    key_list = jax.random.split(jax.random.key(seed), 18)
    return {
        "tokens": noise_with(key_list[0], (SEQS, LEN, D), 1.0, 6.0, ((0, 32),), (0, 2, 32, 2.75)),
        "lengths": draw_lengths(jax.random.fold_in(key_list[17], 71), 0),
        "deal_order": draw_deal_order(jax.random.fold_in(key_list[17], 71), 0),
        "qkv_weight": normal_values(key_list[3], (D, 3 * D), D ** -0.5, 0.21875, ((0, 32),)),
        "query_bias": normal_values(key_list[4], (D,), 0.5, 3.0, ((0, 32),)),
        "value_bias": normal_values(key_list[5], (D,), 0.5, 3.0, ((0, 32),)),
        "out_weight": normal_values(key_list[6], (D, D), (D // 16) ** -0.5, 0.875, ((0, 32),)),
        "out_bias": normal_values(key_list[7], (D,), 0.5, 3.0, ((0, 32),)),
        "attn_gain": jnp.clip(1.0 + 0.1 * jax.random.normal(key_list[8], (D,), jnp.float32), 0.5, 1.5).astype(jnp.bfloat16),
        "attn_shift": normal_values(key_list[9], (D,), 0.3, 2.0, ((0, 32),)),
        "up_weight": normal_values(key_list[10], (D, FF), D ** -0.5, 0.21875, ((0, 32),)),
        "up_bias": normal_values(key_list[11], (FF,), 0.5, 3.0, ((0, 32),)),
        "down_weight": normal_values(key_list[12], (FF, D), FF ** -0.5, 0.109375, ((0, 32),)),
        "down_bias": normal_values(key_list[13], (D,), 0.5, 3.0, ((0, 32),)),
        "ffn_gain": jnp.clip(1.0 + 0.1 * jax.random.normal(key_list[14], (D,), jnp.float32), 0.5, 1.5).astype(jnp.bfloat16),
        "ffn_shift": normal_values(key_list[15], (D,), 0.3, 2.0, ((0, 32),)),
        "cotangent": noise_with(key_list[16], (SEQS, LEN, D), 1.0, 6.0, ((0, 32),), (0, 2, 32, 2.75)),
    }


@jax.custom_vjp
def low(v):
    return lax.optimization_barrier(v.astype(jnp.bfloat16)).astype(jnp.float32)

@jax.custom_vjp
def low_back(v):
    return v

def low_keep(v):
    return (low(v), None)

def low_pass(kept, grad):
    return (grad,)

def back_keep(v):
    return (v, None)

def back_low(kept, grad):
    return (low(grad),)
low.defvjp(low_keep, low_pass)
low_back.defvjp(back_keep, back_low)
highest = lax.Precision.HIGHEST
norm_eps = 1e-05
masked_fill = -1e+30

def rounded(values):
    return low_back(low(values))

def matmul(left, right):
    return jnp.dot(left, right, precision=highest, preferred_element_type=jnp.float32)

def layer_norm(values, norm_gain, norm_shift):
    center = values - lax.optimization_barrier(jnp.mean(values, axis=-1, keepdims=True))
    spread = lax.optimization_barrier(jnp.mean(center * center, axis=-1, keepdims=True))
    return center * lax.rsqrt(spread + norm_eps) * norm_gain + norm_shift

def attention(query_rows, key_rows, value_rows, length):
    score_scale = 1.0 / math.sqrt(HEAD_DIM)
    key_heads = key_rows.reshape(LEN, HEADS, HEAD_DIM)
    value_heads = value_rows.reshape(LEN, HEADS, HEAD_DIM)
    usable = jnp.arange(LEN) < length

    def one_block(queries):
        scores = jnp.einsum('qhd,khd->hqk', queries, key_heads, precision=highest) * score_scale
        scores = low_back(scores)
        scores = jnp.where(usable[None, None, :], scores, masked_fill)
        weights = low(jax.nn.softmax(scores, axis=-1))
        return jnp.einsum('hqk,khd->qhd', weights, value_heads, precision=highest)
    blocks = query_rows.reshape(LEN // BLOCK, BLOCK, HEADS, HEAD_DIM)
    return lax.map(jax.checkpoint(one_block), blocks).reshape(LEN, HEADS * HEAD_DIM)

def forward_one(tokens_row, length, params):
    w_qkv, bias_query, bias_value, w_out, bias_out, gain_attn, shift_attn, w_up, bias_up, w_down, bias_down, gain_ffn, shift_ffn = params
    usable = (jnp.arange(LEN) < length).astype(jnp.float32)[:, None]
    projected = matmul(tokens_row, w_qkv)
    query_rows = rounded(projected[:, :D] + bias_query)
    key_rows = rounded(projected[:, D:2 * D])
    value_rows = rounded(projected[:, 2 * D:] + bias_value)
    context = rounded(attention(query_rows, key_rows, value_rows, length))
    branch_attn = low_back(matmul(context, w_out) + bias_out)
    hidden = layer_norm(tokens_row + branch_attn, gain_attn, shift_attn)
    gate_in = low_back(matmul(low(hidden), w_up) + bias_up)
    activated = low(jax.nn.gelu(gate_in, approximate=False))
    branch_ffn = low_back(matmul(activated, w_down) + bias_down)
    result = layer_norm(hidden + branch_ffn, gain_ffn, shift_ffn) * usable
    valid_count = jnp.sum(usable) * D
    summary = jnp.stack([jnp.sqrt(jnp.sum(usable * tokens_row * tokens_row) / valid_count), jnp.sqrt(jnp.sum(usable * branch_attn * branch_attn) / valid_count), jnp.sqrt(jnp.sum(usable * branch_ffn * branch_ffn) / valid_count)])
    return (result, summary)

def forward_all(inputs, lengths, params):
    group_size = math.gcd(SEQS, max(1, 4096 // LEN))
    shaped = inputs.reshape(SEQS // group_size, group_size, LEN, D)
    grouped = lengths.reshape(SEQS // group_size, group_size)

    def one_group(running, element):
        rows_group, counts = element
        results, summary = jax.vmap(lambda one_row, one_count: forward_one(one_row, one_count, params))(rows_group, counts)
        return (running, (results, summary))
    unused, (results, summary) = lax.scan(jax.checkpoint(one_group), jnp.zeros((), jnp.float32), (shaped, grouped))
    return (results.reshape(SEQS, LEN, D), summary.reshape(SEQS, 3))

def reference(tokens, lengths, deal_order, qkv_weight, query_bias, value_bias, out_weight, out_bias, attn_gain, attn_shift, up_weight, up_bias, down_weight, down_bias, ffn_gain, ffn_shift, cotangent):
    params = (qkv_weight.astype(jnp.float32), query_bias.astype(jnp.float32), value_bias.astype(jnp.float32), out_weight.astype(jnp.float32), out_bias.astype(jnp.float32), attn_gain.astype(jnp.float32), attn_shift.astype(jnp.float32), up_weight.astype(jnp.float32), up_bias.astype(jnp.float32), down_weight.astype(jnp.float32), down_bias.astype(jnp.float32), ffn_gain.astype(jnp.float32), ffn_shift.astype(jnp.float32))
    inputs = tokens.astype(jnp.float32)

    def run_layer(values_in, weights_in):
        return forward_all(values_in, lengths, weights_in)
    outputs, pullback, summary = jax.vjp(run_layer, inputs, params, has_aux=True)
    given_cot = cotangent.astype(jnp.float32)[deal_order]
    grad_inputs, grad_params = pullback(given_cot)
    qkvw_grad, qbias_grad, vbias_grad, outw_grad, outb_grad, gaina_grad, shifta_grad, upw_grad, upb_grad, downw_grad, downb_grad, gainf_grad, shiftf_grad = grad_params
    layer_out = jnp.zeros((SEQS, LEN, D), jnp.bfloat16).at[deal_order].set(outputs.astype(jnp.bfloat16))
    branch_rms = jnp.zeros((SEQS, 3), jnp.float32).at[deal_order].set(summary)
    input_grad = grad_inputs.astype(jnp.bfloat16)
    return (layer_out, input_grad, qkvw_grad, qbias_grad, vbias_grad, outw_grad, outb_grad, gaina_grad, shifta_grad, upw_grad, upb_grad, downw_grad, downb_grad, gainf_grad, shiftf_grad, branch_rms)
```

```python
import functools
import math

import jax
import jax.numpy as jnp
from jax import lax
from jax.experimental import pallas as pl
from jax.experimental.pallas import tpu as pltpu
from jax.sharding import PartitionSpec as P

HEADS = 12
HEAD_DIM = 64
PAIR = 2 * HEAD_DIM
PAIRS = HEADS // 2
BLOCK = 256

f32 = jnp.float32
bf16 = jnp.bfloat16
norm_eps = 1e-05
masked_fill = -1e30
BOTH = ("dp", "fsdp")


def nn(left, right):
    return lax.dot_general(left, right, (((1,), (0,)), ((), ())), preferred_element_type=f32)


def nt(left, right):
    return lax.dot_general(left, right, (((1,), (1,)), ((), ())), preferred_element_type=f32)


def tn(left, right):
    return lax.dot_general(left, right, (((0,), (0,)), ((), ())), preferred_element_type=f32)


def block_count(length):
    return (length + (BLOCK - 1)) // BLOCK


def forward_kernel(len_ref, x_ref, w_ref, bias_ref, qkv_ref, ctx_ref, lse_ref):
    seq, pair = pl.program_id(0), pl.program_id(1)
    length = len_ref[seq]
    blocks = block_count(length)
    rows_all, width = x_ref.shape[1], x_ref.shape[2]
    lane = lax.broadcasted_iota(jnp.int32, (1, PAIR), 1)

    @pl.when(pair == 0)
    def _():
        @pl.loop(0, blocks)
        def _(index):
            rows = pl.ds(pl.multiple_of(index * BLOCK, BLOCK), BLOCK)
            tokens = x_ref[0, rows, :]
            for part in range(3):
                cols = slice(part * width, (part + 1) * width)
                projected = nn(tokens, w_ref[:, cols])
                if part != 1:
                    projected = projected + bias_ref[part : part + 1, :].astype(f32)
                projected = projected.astype(bf16)
                if part == 0:
                    projected = projected * jnp.asarray(1.0 / math.sqrt(HEAD_DIM), bf16)
                for head in range(PAIRS):
                    qkv_ref[0, part * PAIRS + head, rows, :] = projected[:, head * PAIR : (head + 1) * PAIR]

    for keys in range(1, rows_all // BLOCK + 1):

        @pl.when(blocks == keys)
        def _(keys=keys):
            count = keys * BLOCK
            query = qkv_ref[0, pair, 0:count, :]
            key = qkv_ref[0, PAIRS + pair, 0:count, :]
            value = qkv_ref[0, 2 * PAIRS + pair, 0:count, :]
            usable = lax.broadcasted_iota(jnp.int32, (1, BLOCK), 1) + (count - BLOCK) < length
            outs = []
            for head in range(2):
                mine = (lane < HEAD_DIM) if head == 0 else (lane >= HEAD_DIM)
                scores = nt(jnp.where(mine, query, jnp.zeros_like(query)), key)
                last = jnp.where(usable, scores[:, count - BLOCK :], masked_fill)
                scores = jnp.concatenate([scores[:, : count - BLOCK], last], axis=1) if keys > 1 else last
                top = jnp.max(scores, axis=1, keepdims=True)
                powers = jnp.exp(scores - top)
                total = jnp.sum(powers, axis=1, keepdims=True)
                outs.append(nn(powers.astype(bf16), value) * (1.0 / total))
                lse_ref[0, 0, 0:count, head : head + 1] = top + jnp.log(total)
            ctx_ref[0, 0:count, :] = jnp.where(lane < HEAD_DIM, outs[0], outs[1]).astype(bf16)


def attention_forward(lengths, tokens, w_qkv, biases):
    seqs, rows, width = tokens.shape
    whole = lambda shape: pl.BlockSpec(shape, lambda s, p, *_: (0,) * len(shape), pipeline_mode=pl.Buffered(1))
    return pl.pallas_call(
        forward_kernel,
        out_shape=(
            jax.ShapeDtypeStruct((seqs, 3 * PAIRS, rows, PAIR), bf16),
            jax.ShapeDtypeStruct((seqs, rows, width), bf16),
            jax.ShapeDtypeStruct((seqs, PAIRS, rows, PAIR), f32),
        ),
        grid_spec=pltpu.PrefetchScalarGridSpec(
            num_scalar_prefetch=1,
            grid=(seqs, PAIRS),
            in_specs=[
                pl.BlockSpec((1, rows, width), lambda s, p, *_: (s, 0, 0)),
                whole(w_qkv.shape),
                whole(biases.shape),
            ],
            out_specs=[
                pl.BlockSpec((1, 3 * PAIRS, rows, PAIR), lambda s, p, *_: (s, 0, 0, 0)),
                pl.BlockSpec((1, rows, PAIR), lambda s, p, *_: (s, 0, p)),
                pl.BlockSpec((1, 1, rows, PAIR), lambda s, p, *_: (s, p, 0, 0)),
            ],
        ),
        compiler_params=pltpu.CompilerParams(vmem_limit_bytes=56 << 20),
        cost_estimate=pl.CostEstimate(
            flops=60_000_000_000, transcendentals=30_000_000, bytes_accessed=30_000_000
        ),
        name="attention_forward",
    )(lengths, tokens, w_qkv, biases)


def normal_tail(values):
    size = jnp.abs(values)
    bell = jnp.exp(-0.5 * values * values)
    t = 1.0 / (1.0 + (0.3275911 / math.sqrt(2.0)) * size)
    poly = t * (
        0.5 * 0.254829592
        + t * (0.5 * -0.284496736 + t * (0.5 * 1.421413741 + t * (0.5 * -1.453152027 + t * (0.5 * 1.061405429))))
    )
    tail = poly * bell
    return jnp.where(values >= 0, 1.0 - tail, tail), bell


def row_mean(values):
    return jnp.mean(values, axis=-1, keepdims=True)


def middle_kernel(
    len_ref, in_slot, out_slot, x_ref, ctx_ref, cot_ref, wo_ref, wu_ref, wd_ref, vec_ref, bu_ref,
    out_ref, gres_ref, gctx_ref, dwo_ref, dwu_ref, dwd_ref, dvec_ref, dbu_ref, sums_ref,
    acc_o, acc_u, acc_d, active, slope, stage, sems,
):
    seq, index = pl.program_id(0), pl.program_id(1)
    first = jnp.logical_and(seq == 0, index == 0)
    final = jnp.logical_and(seq == pl.num_programs(0) - 1, index == pl.num_programs(1) - 1)
    length = len_ref[seq]
    width = x_ref.shape[2]
    chunks = wd_ref.shape[0] // width

    @pl.when(first)
    def _():
        acc_o[...] = jnp.zeros_like(acc_o)
        acc_u[...] = jnp.zeros_like(acc_u)
        acc_d[...] = jnp.zeros_like(acc_d)
        dvec_ref[...] = jnp.zeros_like(dvec_ref)
        dbu_ref[...] = jnp.zeros_like(dbu_ref)

    @pl.when(index == 0)
    def _():
        sums_ref[...] = jnp.zeros_like(sums_ref)

    @pl.when(index * BLOCK >= length)
    def _():
        out_ref[...] = jnp.zeros_like(out_ref)

    @pl.when(index * BLOCK < length)
    def _():
        vec = lambda place: vec_ref[place : place + 1, :].astype(f32)
        bias_out, gain_a, shift_a, bias_down, gain_f, shift_f = (vec(place) for place in range(6))
        valid = (lax.broadcasted_iota(jnp.int32, (BLOCK, 1), 0) + index * BLOCK < length).astype(f32)
        tokens = x_ref[0].astype(f32)
        context = ctx_ref[0]
        branch_a = nn(context, wo_ref[...]) + bias_out
        mixed = tokens + branch_a
        center = mixed - row_mean(mixed)
        scale_a = lax.rsqrt(row_mean(center * center) + norm_eps)
        hat_a = center * scale_a
        hidden = hat_a * gain_a + shift_a
        hidden_low = hidden.astype(bf16)
        branch_f = bias_down
        for chunk in range(chunks):
            cols = slice(chunk * width, (chunk + 1) * width)
            gate = nn(hidden_low, wu_ref[:, cols]) + bu_ref[:, cols].astype(f32)
            share, bell = normal_tail(gate)
            act = (gate * share).astype(bf16)
            active[:, cols] = act
            slope[:, cols] = share + gate * bell * (1.0 / math.sqrt(2.0 * math.pi))
            branch_f = branch_f + nn(act, wd_ref[cols, :])
        mixed_f = hidden + branch_f
        center = mixed_f - row_mean(mixed_f)
        scale_f = lax.rsqrt(row_mean(center * center) + norm_eps)
        hat_f = center * scale_f
        out_ref[0] = ((hat_f * gain_f + shift_f) * valid).astype(bf16)
        g_result = cot_ref[0].astype(f32) * valid
        g_hat = g_result * gain_f
        g_res2 = scale_f * (g_hat - row_mean(g_hat) - hat_f * row_mean(g_hat * hat_f))
        g_ffn = g_res2.astype(bf16)
        g_hidden = g_res2
        for chunk in range(chunks):
            cols = slice(chunk * width, (chunk + 1) * width)
            g_gate = nt(g_ffn, wd_ref[cols, :]) * slope[:, cols]
            g_low = g_gate.astype(bf16)
            acc_d[cols, :] += tn(active[:, cols], g_ffn)
            acc_u[:, cols] += tn(hidden_low, g_low)
            dbu_ref[:, cols] += jnp.sum(g_low.astype(f32), axis=0, keepdims=True)
            g_hidden = g_hidden + nt(g_low, wu_ref[:, cols])
        g_hat = g_hidden * gain_a
        g_res1 = scale_a * (g_hat - row_mean(g_hat) - hat_a * row_mean(g_hat * hat_a))
        g_attn = g_res1.astype(bf16)
        gres_ref[0] = g_res1
        gctx_ref[0] = nt(g_attn, wo_ref[...]).astype(bf16)
        acc_o[...] += tn(context, g_attn)
        column = lambda values: jnp.sum(values, axis=0, keepdims=True)
        dvec_ref[0:1, :] += column(g_attn.astype(f32))
        dvec_ref[1:2, :] += column(g_hidden * hat_a)
        dvec_ref[2:3, :] += column(g_hidden)
        dvec_ref[3:4, :] += column(g_ffn.astype(f32))
        dvec_ref[4:5, :] += column(g_result * hat_f)
        dvec_ref[5:6, :] += column(g_result)
        sums_ref[0, 0:1, :] += column(tokens * tokens * valid)
        sums_ref[0, 1:2, :] += column(branch_a * branch_a * valid)
        sums_ref[0, 2:3, :] += column(branch_f * branch_f * valid)

    @pl.when(final)
    def _():
        pieces = [(acc_o, dwo_ref, slice(None), slice(None))]
        for chunk in range(chunks):
            cols = slice(chunk * width, (chunk + 1) * width)
            pieces.append((acc_u, dwu_ref, slice(None), cols))
            pieces.append((acc_d, dwd_ref, cols, slice(None)))
        copies = []
        for place, (acc, out, rows, cols) in enumerate(pieces):
            slot = place % 2
            if place >= 2:
                copies[place - 2].wait()
            stage[slot] = acc[rows, cols].astype(bf16)
            copies.append(pltpu.make_async_copy(stage.at[slot], out.at[rows, cols], sems.at[slot]))
            copies[-1].start()
        copies[-2].wait()
        copies[-1].wait()


def middle(lengths, in_slot, out_slot, tokens, context, cots, w_out, w_up, w_down, vectors, bias_up):
    seqs, rows, width = tokens.shape
    slots = cots.shape[0]
    hidden = w_up.shape[1]
    whole = lambda shape: pl.BlockSpec(shape, lambda s, i, *_: (0,) * len(shape), pipeline_mode=pl.Buffered(1))
    inside = lambda s, i, lens: jnp.minimum(i, block_count(lens[s]) - 1)
    here = pl.BlockSpec((1, BLOCK, width), lambda s, i, lens, a, b: (s, inside(s, i, lens), 0))
    kept = pl.BlockSpec((1, BLOCK, width), lambda s, i, lens, a, b: (s, inside(s, i, lens), 0))
    total = 2 * seqs * rows * (2 * width * width + 4 * width * hidden) * 2
    return pl.pallas_call(
        middle_kernel,
        out_shape=(
            jax.ShapeDtypeStruct((slots, rows, width), bf16),
            jax.ShapeDtypeStruct((seqs, rows, width), f32),
            jax.ShapeDtypeStruct((seqs, rows, width), bf16),
            jax.ShapeDtypeStruct(w_out.shape, bf16),
            jax.ShapeDtypeStruct(w_up.shape, bf16),
            jax.ShapeDtypeStruct(w_down.shape, bf16),
            jax.ShapeDtypeStruct((8, width), f32),
            jax.ShapeDtypeStruct((1, hidden), f32),
            jax.ShapeDtypeStruct((seqs, 8, width), f32),
        ),
        grid_spec=pltpu.PrefetchScalarGridSpec(
            num_scalar_prefetch=3,
            grid=(seqs, rows // BLOCK),
            in_specs=[
                here,
                here,
                pl.BlockSpec((1, BLOCK, width), lambda s, i, lens, a, b: (a[s], inside(s, i, lens), 0)),
                whole(w_out.shape),
                whole(w_up.shape),
                whole(w_down.shape),
                whole(vectors.shape),
                whole(bias_up.shape),
            ],
            out_specs=[
                pl.BlockSpec((1, BLOCK, width), lambda s, i, lens, a, b: (b[s], i, 0)),
                kept,
                kept,
                pl.BlockSpec(memory_space=pl.ANY),
                pl.BlockSpec(memory_space=pl.ANY),
                pl.BlockSpec(memory_space=pl.ANY),
                whole((8, width)),
                whole((1, hidden)),
                pl.BlockSpec((1, 8, width), lambda s, i, *_: (s, 0, 0)),
            ],
            scratch_shapes=[
                pltpu.VMEM(w_out.shape, f32),
                pltpu.VMEM(w_up.shape, f32),
                pltpu.VMEM(w_down.shape, f32),
                pltpu.VMEM((BLOCK, hidden), bf16),
                pltpu.VMEM((BLOCK, hidden), f32),
                pltpu.VMEM((2, width, width), bf16),
                pltpu.SemaphoreType.DMA((2,)),
            ],
        ),
        compiler_params=pltpu.CompilerParams(vmem_limit_bytes=60 << 20),
        cost_estimate=pl.CostEstimate(flops=total, transcendentals=seqs * rows * hidden, bytes_accessed=60_000_000),
        name="middle",
    )(lengths, in_slot, out_slot, tokens, context, cots, w_out, w_up, w_down, vectors, bias_up)


def backward_kernel(
    len_ref, x_ref, qkv_in, ctx_ref, gctx_ref, lse_ref, gres_ref, w_ref,
    gin_ref, dw_ref, dvec_ref, mixed, acc_w, acc_k, acc_v, stage, sems,
):
    seq, pair = pl.program_id(0), pl.program_id(1)
    length = len_ref[seq]
    blocks = block_count(length)
    rows_all, width = x_ref.shape[1], x_ref.shape[2]
    lane = lax.broadcasted_iota(jnp.int32, (1, PAIR), 1)
    factor = 1.0 / math.sqrt(HEAD_DIM)

    @pl.when(jnp.logical_and(seq == 0, pair == 0))
    def _():
        acc_w[...] = jnp.zeros_like(acc_w)
        dvec_ref[...] = jnp.zeros_like(dvec_ref)

    for keys in range(1, rows_all // BLOCK + 1):

        @pl.when(blocks == keys)
        def _(keys=keys):
            count = keys * BLOCK
            key = qkv_in[0, 1, 0, 0:count, :]
            value = qkv_in[0, 2, 0, 0:count, :]
            usable = lax.broadcasted_iota(jnp.int32, (1, BLOCK), 1) + (count - BLOCK) < length
            acc_k[0:count, :] = jnp.zeros((count, PAIR), f32)
            acc_v[0:count, :] = jnp.zeros((count, PAIR), f32)

            @pl.loop(0, keys)
            def _(index):
                rows = pl.ds(pl.multiple_of(index * BLOCK, BLOCK), BLOCK)
                query = qkv_in[0, 0, 0, rows, :]
                grad = gctx_ref[0, rows, :]
                agree = grad.astype(f32) * ctx_ref[0, rows, :].astype(f32)
                g_query = jnp.zeros((BLOCK, PAIR), f32)
                for head in range(2):
                    mine = (lane < HEAD_DIM) if head == 0 else (lane >= HEAD_DIM)
                    only = lambda values: jnp.where(mine, values, jnp.zeros_like(values))
                    query_h, grad_h, key_h = only(query), only(grad), only(key)
                    delta = jnp.sum(only(agree), axis=1, keepdims=True)
                    scores = nt(query_h, key)
                    last = jnp.where(usable, scores[:, count - BLOCK :], masked_fill)
                    scores = jnp.concatenate([scores[:, : count - BLOCK], last], axis=1) if keys > 1 else last
                    probs = jnp.exp(scores - lse_ref[0, 0, rows, head : head + 1])
                    g_probs = nt(grad_h, value)
                    g_scores = (probs * (g_probs - delta)).astype(bf16)
                    g_query = g_query + nn(g_scores, key_h)
                    acc_k[0:count, :] += tn(g_scores, query_h)
                    acc_v[0:count, :] += tn(probs.astype(bf16), grad_h)
                mixed[pair, rows, :] = (g_query * factor).astype(bf16)

            mixed[PAIRS + pair, 0:count, :] = acc_k[0:count, :].astype(bf16)
            mixed[2 * PAIRS + pair, 0:count, :] = acc_v[0:count, :].astype(bf16)

    @pl.when(pair == PAIRS - 1)
    def _():
        @pl.loop(0, rows_all // BLOCK)
        def _(index):
            rows = pl.ds(pl.multiple_of(index * BLOCK, BLOCK), BLOCK)

            @pl.when(index >= blocks)
            def _():
                gin_ref[0, rows, :] = jnp.zeros((BLOCK, width), bf16)

            @pl.when(index < blocks)
            def _():
                tokens = x_ref[0, rows, :]
                g_in = gres_ref[0, rows, :]
                for part in range(3):
                    cols = slice(part * width, (part + 1) * width)
                    piece = jnp.concatenate([mixed[part * PAIRS + head, rows, :] for head in range(PAIRS)], axis=1)
                    g_in = g_in + nt(piece, w_ref[:, cols])
                    acc_w[:, cols] += tn(tokens, piece)
                    dvec_ref[part : part + 1, :] += jnp.sum(piece.astype(f32), axis=0, keepdims=True)
                gin_ref[0, rows, :] = g_in.astype(bf16)

    @pl.when(jnp.logical_and(seq == pl.num_programs(0) - 1, pair == PAIRS - 1))
    def _():
        copies = []
        for part in range(3):
            cols = slice(part * width, (part + 1) * width)
            slot = part % 2
            if part >= 2:
                copies[part - 2].wait()
            stage[slot] = acc_w[:, cols].astype(bf16)
            copies.append(pltpu.make_async_copy(stage.at[slot], dw_ref.at[:, cols], sems.at[slot]))
            copies[-1].start()
        copies[-2].wait()
        copies[-1].wait()


def attention_backward(lengths, tokens, qkv, context, g_context, lse, g_res1, w_qkv):
    seqs, rows, width = tokens.shape
    whole = lambda shape: pl.BlockSpec(shape, lambda s, p, *_: (0,) * len(shape), pipeline_mode=pl.Buffered(1))
    pair_cols = pl.BlockSpec((1, rows, PAIR), lambda s, p, *_: (s, 0, p))
    seq_rows = pl.BlockSpec((1, rows, width), lambda s, p, *_: (s, 0, 0))
    return pl.pallas_call(
        backward_kernel,
        out_shape=(
            jax.ShapeDtypeStruct((seqs, rows, width), bf16),
            jax.ShapeDtypeStruct(w_qkv.shape, bf16),
            jax.ShapeDtypeStruct((8, width), f32),
        ),
        grid_spec=pltpu.PrefetchScalarGridSpec(
            num_scalar_prefetch=1,
            grid=(seqs, PAIRS),
            in_specs=[
                seq_rows,
                pl.BlockSpec((1, 3, 1, rows, PAIR), lambda s, p, *_: (s, 0, p, 0, 0)),
                pair_cols,
                pair_cols,
                pl.BlockSpec((1, 1, rows, PAIR), lambda s, p, *_: (s, p, 0, 0)),
                seq_rows,
                whole(w_qkv.shape),
            ],
            out_specs=[
                seq_rows,
                pl.BlockSpec(memory_space=pl.ANY),
                whole((8, width)),
            ],
            scratch_shapes=[
                pltpu.VMEM((3 * PAIRS, rows, PAIR), bf16),
                pltpu.VMEM(w_qkv.shape, f32),
                pltpu.VMEM((rows, PAIR), f32),
                pltpu.VMEM((rows, PAIR), f32),
                pltpu.VMEM((2, width, width), bf16),
                pltpu.SemaphoreType.DMA((2,)),
            ],
        ),
        compiler_params=pltpu.CompilerParams(vmem_limit_bytes=60 << 20),
        cost_estimate=pl.CostEstimate(
            flops=120_000_000_000, transcendentals=30_000_000, bytes_accessed=40_000_000
        ),
        name="attention_backward",
    )(lengths, tokens, qkv.reshape(seqs, 3, PAIRS, rows, PAIR), context, g_context, lse, g_res1, w_qkv)


def body(
    tokens, lengths, deal_order, qkv_weight, query_bias, value_bias, out_weight, out_bias, attn_gain, attn_shift,
    up_weight, up_bias, down_weight, down_bias, ffn_gain, ffn_shift, cotangent,
):
    shards = lax.axis_size("fsdp")
    devices = lax.axis_size("dp") * shards
    seqs, rows, width = tokens.shape
    column = shards * seqs
    base = lax.axis_index("dp") * column
    member = lax.axis_index("fsdp")
    order = lax.dynamic_slice_in_dim(deal_order, base, column) - base
    mine = member * seqs
    own_lengths = lax.dynamic_slice_in_dim(lengths, base + mine, seqs)
    target = lax.dynamic_slice_in_dim(order, mine, seqs) // seqs
    dealt_here = mine + jnp.arange(seqs, dtype=jnp.int32)
    matches = order[None, :] == dealt_here[:, None]
    places = jnp.arange(column, dtype=jnp.int32)
    source = jnp.sum(jnp.where(matches, places[None, :], 0), axis=1) // seqs
    peers = jnp.arange(shards, dtype=jnp.int32)

    outgoing = cotangent[0][None]
    for place in range(1, seqs):
        outgoing = jnp.where((source[place] == peers)[:, None, None], cotangent[place][None], outgoing)
    cots = lax.all_to_all(outgoing, "fsdp", split_axis=0, concat_axis=0, tiled=True)

    gather = lambda shard: lax.all_gather(shard, BOTH, axis=0, tiled=True)
    small = jnp.concatenate(
        [query_bias, value_bias, out_bias, attn_gain, attn_shift, down_bias, ffn_gain, ffn_shift, up_bias]
    )
    per = width // devices
    small = lax.all_gather(small, BOTH, axis=0, tiled=False)
    vectors = [small[:, place * per : (place + 1) * per].reshape(1, width) for place in range(8)]
    bias_up = small[:, 8 * per :].reshape(1, -1)
    zero = jnp.zeros((1, width), bf16)
    qkv_bias = jnp.concatenate([vectors[0], zero, vectors[1]] + [zero] * 5, axis=0)
    mid_vectors = jnp.concatenate(vectors[2:] + [zero, zero], axis=0)
    w_qkv, w_out, w_up, w_down = gather(qkv_weight), gather(out_weight), gather(up_weight), gather(down_weight)

    qkv, context, lse = attention_forward(own_lengths, tokens, w_qkv, qkv_bias)
    results, g_res1, g_context, dw_out, dw_up, dw_down, dvec, dbu, sums = middle(
        own_lengths, target, target, tokens, context, cots, w_out, w_up, w_down, mid_vectors, bias_up
    )
    input_grad, dw_qkv, dqv = attention_backward(own_lengths, tokens, qkv, context, g_context, lse, g_res1, w_qkv)

    rms = jnp.sqrt(jnp.sum(sums[:, :3, :], axis=2) / (own_lengths.astype(f32) * width)[:, None])
    rms_out = jnp.sum(jnp.where((target[:, None] == peers[None, :])[:, :, None], rms[:, None, :], 0.0), axis=0)
    rms_here = lax.all_to_all(rms_out, "fsdp", split_axis=0, concat_axis=0, tiled=True)
    arrived = lax.all_to_all(results, "fsdp", split_axis=0, concat_axis=0, tiled=True)
    layer_out = jnp.stack([lax.dynamic_index_in_dim(arrived, source[t], 0, keepdims=False) for t in range(seqs)])
    branch_rms = jnp.stack([lax.dynamic_index_in_dim(rms_here, source[t], 0, keepdims=False) for t in range(seqs)])

    scatter = lambda whole: lax.psum_scatter(whole, BOTH, scatter_dimension=0, tiled=True)
    grads = [dqv[0], dqv[2], dvec[0], dvec[1], dvec[2], dvec[3], dvec[4], dvec[5]]
    packed = jnp.concatenate([vector.reshape(devices, per) for vector in grads] + [dbu.reshape(devices, -1)], axis=1)
    packed = lax.psum_scatter(packed, BOTH, scatter_dimension=0, tiled=True)[0]
    shard = [packed[place * per : (place + 1) * per] for place in range(8)]
    return (
        layer_out, input_grad, scatter(dw_qkv).astype(f32), shard[0], shard[1], scatter(dw_out).astype(f32), shard[2],
        shard[3], shard[4], scatter(dw_up).astype(f32), packed[8 * per :], scatter(dw_down).astype(f32), shard[5],
        shard[6], shard[7], branch_rms,
    )


def solution(mesh):
    rows3, rows2, rows1 = P(BOTH, None, None), P(BOTH, None), P(BOTH)
    in_specs = (
        rows3, P(), P(), rows2, rows1, rows1, rows2, rows1, rows1, rows1, rows2, rows1, rows2, rows1, rows1, rows1, rows3,
    )
    out_specs = (
        rows3, rows3, rows2, rows1, rows1, rows2, rows1, rows1, rows1, rows2, rows1, rows2, rows1, rows1, rows1, rows2,
    )
    return jax.shard_map(body, mesh=mesh, in_specs=in_specs, out_specs=out_specs, check_vma=False)
```

```python
import functools
import math

import jax
import jax.numpy as jnp
from jax import lax
from jax.experimental import pallas as pl
from jax.experimental.pallas import tpu as pltpu
from jax.sharding import PartitionSpec as P

HEADS = 12
HEAD_DIM = 64
PAIR = 2 * HEAD_DIM
PAIRS = HEADS // 2
BLOCK = 256

f32 = jnp.float32
bf16 = jnp.bfloat16
norm_eps = 1e-05
masked_fill = -1e30
BOTH = ("dp", "fsdp")
MESH = pl.DeviceIdType.MESH


def nn(left, right):
    return lax.dot_general(left, right, (((1,), (0,)), ((), ())), preferred_element_type=f32)


def nt(left, right):
    return lax.dot_general(left, right, (((1,), (1,)), ((), ())), preferred_element_type=f32)


def tn(left, right):
    return lax.dot_general(left, right, (((0,), (0,)), ((), ())), preferred_element_type=f32)


def block_count(length):
    return (length + (BLOCK - 1)) // BLOCK


def forward_kernel(len_ref, x_ref, w_ref, bias_ref, qkv_ref, ctx_ref, lse_ref):
    seq, pair = pl.program_id(0), pl.program_id(1)
    length = len_ref[seq]
    blocks = block_count(length)
    rows_all, width = x_ref.shape[1], x_ref.shape[2]
    lane = lax.broadcasted_iota(jnp.int32, (1, PAIR), 1)

    @pl.when(pair == 0)
    def _():
        @pl.loop(0, blocks)
        def _(index):
            rows = pl.ds(pl.multiple_of(index * BLOCK, BLOCK), BLOCK)
            tokens = x_ref[0, rows, :]
            for part in range(3):
                cols = slice(part * width, (part + 1) * width)
                projected = nn(tokens, w_ref[:, cols])
                if part != 1:
                    projected = projected + bias_ref[part // 2 : part // 2 + 1, :].astype(f32)
                projected = projected.astype(bf16)
                if part == 0:
                    projected = projected * jnp.asarray(1.0 / math.sqrt(HEAD_DIM), bf16)
                for head in range(PAIRS):
                    qkv_ref[0, part * PAIRS + head, rows, :] = projected[:, head * PAIR : (head + 1) * PAIR]

    for keys in range(1, rows_all // BLOCK + 1):

        @pl.when(blocks == keys)
        def _(keys=keys):
            count = keys * BLOCK
            query = qkv_ref[0, pair, 0:count, :]
            key = qkv_ref[0, PAIRS + pair, 0:count, :]
            value = qkv_ref[0, 2 * PAIRS + pair, 0:count, :]
            usable = lax.broadcasted_iota(jnp.int32, (1, BLOCK), 1) + (count - BLOCK) < length
            outs = []
            for head in range(2):
                mine = (lane < HEAD_DIM) if head == 0 else (lane >= HEAD_DIM)
                scores = nt(jnp.where(mine, query, jnp.zeros_like(query)), key)
                last = jnp.where(usable, scores[:, count - BLOCK :], masked_fill)
                scores = jnp.concatenate([scores[:, : count - BLOCK], last], axis=1) if keys > 1 else last
                top = jnp.max(scores, axis=1, keepdims=True)
                powers = jnp.exp(scores - top)
                total = jnp.sum(powers, axis=1, keepdims=True)
                outs.append(nn(powers.astype(bf16), value) * (1.0 / total))
                lse_ref[0, 0, 0:count, head : head + 1] = top + jnp.log(total)
            ctx_ref[0, 0:count, :] = jnp.where(lane < HEAD_DIM, outs[0], outs[1]).astype(bf16)


def attention_forward(lengths, tokens, w_qkv, biases):
    seqs, rows, width = tokens.shape
    whole = lambda shape: pl.BlockSpec(shape, lambda s, p, *_: (0,) * len(shape), pipeline_mode=pl.Buffered(1))
    return pl.pallas_call(
        forward_kernel,
        out_shape=(
            jax.ShapeDtypeStruct((seqs, 3 * PAIRS, rows, PAIR), bf16),
            jax.ShapeDtypeStruct((seqs, rows, width), bf16),
            jax.ShapeDtypeStruct((seqs, PAIRS, rows, PAIR), f32),
        ),
        grid_spec=pltpu.PrefetchScalarGridSpec(
            num_scalar_prefetch=1,
            grid=(seqs, PAIRS),
            in_specs=[
                pl.BlockSpec((1, rows, width), lambda s, p, *_: (s, 0, 0)),
                whole(w_qkv.shape),
                whole(biases.shape),
            ],
            out_specs=[
                pl.BlockSpec((1, 3 * PAIRS, rows, PAIR), lambda s, p, *_: (s, 0, 0, 0)),
                pl.BlockSpec((1, rows, PAIR), lambda s, p, *_: (s, 0, p)),
                pl.BlockSpec((1, 1, rows, PAIR), lambda s, p, *_: (s, p, 0, 0)),
            ],
        ),
        compiler_params=pltpu.CompilerParams(vmem_limit_bytes=56 << 20),
        cost_estimate=pl.CostEstimate(
            flops=60_000_000_000, transcendentals=30_000_000, bytes_accessed=30_000_000
        ),
        name="attention_forward",
    )(lengths, tokens, w_qkv, biases)


def normal_tail(values):
    size = jnp.abs(values)
    bell = jnp.exp(-0.5 * values * values)
    t = 1.0 / (1.0 + (0.3275911 / math.sqrt(2.0)) * size)
    poly = t * (
        0.5 * 0.254829592
        + t * (0.5 * -0.284496736 + t * (0.5 * 1.421413741 + t * (0.5 * -1.453152027 + t * (0.5 * 1.061405429))))
    )
    tail = poly * bell
    return jnp.where(values >= 0, 1.0 - tail, tail), bell


def row_mean(values):
    return jnp.mean(values, axis=-1, keepdims=True)


def middle_kernel(
    len_ref, in_slot, out_slot, x_ref, ctx_ref, cot_ref, w_ref, vec_ref, bu_ref,
    out_ref, gres_ref, gctx_ref, dw_ref, dvec_ref, dbu_ref, rms_ref,
    acc, active, slope, sums, stage, sems,
):
    seq, index = pl.program_id(0), pl.program_id(1)
    first = jnp.logical_and(seq == 0, index == 0)
    final = jnp.logical_and(seq == pl.num_programs(0) - 1, index == pl.num_programs(1) - 1)
    length = len_ref[seq]
    width = x_ref.shape[2]
    chunks = bu_ref.shape[1] // width
    tile = lambda place: slice(place * width, (place + 1) * width)
    up = lambda chunk: tile(1 + chunk)
    down = lambda chunk: tile(1 + chunks + chunk)

    @pl.when(first)
    def _():
        acc[...] = jnp.zeros_like(acc)
        dvec_ref[...] = jnp.zeros_like(dvec_ref)
        dbu_ref[...] = jnp.zeros_like(dbu_ref)

    @pl.when(index == 0)
    def _():
        sums[...] = jnp.zeros_like(sums)

    @pl.when(index * BLOCK >= length)
    def _():
        out_ref[...] = jnp.zeros_like(out_ref)

    @pl.when(index * BLOCK < length)
    def _():
        vec = lambda place: vec_ref[place : place + 1, :].astype(f32)
        bias_out, gain_a, shift_a, bias_down, gain_f, shift_f = (vec(place) for place in range(2, 8))
        valid = (lax.broadcasted_iota(jnp.int32, (BLOCK, 1), 0) + index * BLOCK < length).astype(f32)
        tokens = x_ref[0].astype(f32)
        context = ctx_ref[0]
        branch_a = nn(context, w_ref[:, tile(0)]) + bias_out
        mixed = tokens + branch_a
        center = mixed - row_mean(mixed)
        scale_a = lax.rsqrt(row_mean(center * center) + norm_eps)
        hat_a = center * scale_a
        hidden = hat_a * gain_a + shift_a
        hidden_low = hidden.astype(bf16)
        branch_f = bias_down
        for chunk in range(chunks):
            cols = tile(chunk)
            gate = nn(hidden_low, w_ref[:, up(chunk)]) + bu_ref[:, cols].astype(f32)
            share, bell = normal_tail(gate)
            act = (gate * share).astype(bf16)
            active[:, cols] = act
            slope[:, cols] = share + gate * bell * (1.0 / math.sqrt(2.0 * math.pi))
            branch_f = branch_f + nn(act, w_ref[:, down(chunk)])
        mixed_f = hidden + branch_f
        center = mixed_f - row_mean(mixed_f)
        scale_f = lax.rsqrt(row_mean(center * center) + norm_eps)
        hat_f = center * scale_f
        out_ref[0] = ((hat_f * gain_f + shift_f) * valid).astype(bf16)
        g_result = cot_ref[0].astype(f32) * valid
        g_hat = g_result * gain_f
        g_res2 = scale_f * (g_hat - row_mean(g_hat) - hat_f * row_mean(g_hat * hat_f))
        g_ffn = g_res2.astype(bf16)
        g_hidden = g_res2
        for chunk in range(chunks):
            cols = tile(chunk)
            g_gate = nt(g_ffn, w_ref[:, down(chunk)]) * slope[:, cols]
            g_low = g_gate.astype(bf16)
            acc[:, down(chunk)] += tn(active[:, cols], g_ffn)
            acc[:, up(chunk)] += tn(hidden_low, g_low)
            dbu_ref[:, cols] += jnp.sum(g_low.astype(f32), axis=0, keepdims=True)
            g_hidden = g_hidden + nt(g_low, w_ref[:, up(chunk)])
        g_hat = g_hidden * gain_a
        g_res1 = scale_a * (g_hat - row_mean(g_hat) - hat_a * row_mean(g_hat * hat_a))
        g_attn = g_res1.astype(bf16)
        gres_ref[0] = g_res1
        gctx_ref[0] = nt(g_attn, w_ref[:, tile(0)]).astype(bf16)
        acc[:, tile(0)] += tn(context, g_attn)
        column = lambda values: jnp.sum(values, axis=0, keepdims=True)
        dvec_ref[2:3, :] += column(g_attn.astype(f32))
        dvec_ref[3:4, :] += column(g_hidden * hat_a)
        dvec_ref[4:5, :] += column(g_hidden)
        dvec_ref[5:6, :] += column(g_ffn.astype(f32))
        dvec_ref[6:7, :] += column(g_result * hat_f)
        dvec_ref[7:8, :] += column(g_result)
        sums[0:1, :] += column(tokens * tokens * valid)
        sums[1:2, :] += column(branch_a * branch_a * valid)
        sums[2:3, :] += column(branch_f * branch_f * valid)

    @pl.when(index == pl.num_programs(1) - 1)
    def _():
        mean = jnp.sum(sums[...], axis=1, keepdims=True) / (length * width).astype(f32)
        rms_ref[0] = jnp.broadcast_to(jnp.sqrt(mean), rms_ref.shape[1:])

    @pl.when(final)
    def _():
        copies = []
        for place in range(1 + 2 * chunks):
            slot = place % 2
            if place >= 2:
                copies[place - 2].wait()
            stage[slot] = acc[:, tile(place)].astype(bf16)
            copies.append(pltpu.make_async_copy(stage.at[slot], dw_ref.at[:, tile(place)], sems.at[slot]))
            copies[-1].start()
        copies[-2].wait()
        copies[-1].wait()


def middle(lengths, in_slot, out_slot, tokens, context, cots, weights, vectors, bias_up):
    seqs, rows, width = tokens.shape
    slots = cots.shape[0]
    hidden = bias_up.shape[1]
    whole = lambda shape: pl.BlockSpec(shape, lambda s, i, *_: (0,) * len(shape), pipeline_mode=pl.Buffered(1))
    inside = lambda s, i, lens: jnp.minimum(i, block_count(lens[s]) - 1)
    here = pl.BlockSpec((1, BLOCK, width), lambda s, i, lens, a, b: (s, inside(s, i, lens), 0))
    flops = 6 * seqs * rows * (width * width + 2 * width * hidden)
    return pl.pallas_call(
        middle_kernel,
        out_shape=(
            jax.ShapeDtypeStruct((slots, rows, width), bf16),
            jax.ShapeDtypeStruct((seqs, rows, width), f32),
            jax.ShapeDtypeStruct((seqs, rows, width), bf16),
            jax.ShapeDtypeStruct(weights.shape, bf16),
            jax.ShapeDtypeStruct((8, width), f32),
            jax.ShapeDtypeStruct((1, hidden), f32),
            jax.ShapeDtypeStruct((seqs, 8, 128), f32),
        ),
        grid_spec=pltpu.PrefetchScalarGridSpec(
            num_scalar_prefetch=3,
            grid=(seqs, rows // BLOCK),
            in_specs=[
                here,
                here,
                pl.BlockSpec((1, BLOCK, width), lambda s, i, lens, a, b: (a[s], inside(s, i, lens), 0)),
                whole(weights.shape),
                whole(vectors.shape),
                whole(bias_up.shape),
            ],
            out_specs=[
                pl.BlockSpec((1, BLOCK, width), lambda s, i, lens, a, b: (b[s], i, 0)),
                here,
                here,
                pl.BlockSpec(memory_space=pl.ANY),
                whole((8, width)),
                whole((1, hidden)),
                pl.BlockSpec((1, 8, 128), lambda s, i, *_: (s, 0, 0)),
            ],
            scratch_shapes=[
                pltpu.VMEM(weights.shape, f32),
                pltpu.VMEM((BLOCK, hidden), bf16),
                pltpu.VMEM((BLOCK, hidden), f32),
                pltpu.VMEM((8, width), f32),
                pltpu.VMEM((2, width, width), bf16),
                pltpu.SemaphoreType.DMA((2,)),
            ],
        ),
        compiler_params=pltpu.CompilerParams(vmem_limit_bytes=60 << 20),
        cost_estimate=pl.CostEstimate(flops=flops, transcendentals=seqs * rows * hidden, bytes_accessed=60_000_000),
        name="middle",
    )(lengths, in_slot, out_slot, tokens, context, cots, weights, vectors, bias_up)


def backward_kernel(
    len_ref, x_ref, qkv_in, ctx_ref, gctx_ref, lse_ref, gres_ref, w_ref,
    gin_ref, dw_ref, dvec_ref, mixed, acc_w, acc_k, acc_v, stage, sems,
):
    seq, pair = pl.program_id(0), pl.program_id(1)
    length = len_ref[seq]
    blocks = block_count(length)
    rows_all, width = x_ref.shape[1], x_ref.shape[2]
    lane = lax.broadcasted_iota(jnp.int32, (1, PAIR), 1)
    factor = 1.0 / math.sqrt(HEAD_DIM)

    @pl.when(jnp.logical_and(seq == 0, pair == 0))
    def _():
        acc_w[...] = jnp.zeros_like(acc_w)
        dvec_ref[...] = jnp.zeros_like(dvec_ref)

    for keys in range(1, rows_all // BLOCK + 1):

        @pl.when(blocks == keys)
        def _(keys=keys):
            count = keys * BLOCK
            key = qkv_in[0, 1, 0, 0:count, :]
            value = qkv_in[0, 2, 0, 0:count, :]
            usable = lax.broadcasted_iota(jnp.int32, (1, BLOCK), 1) + (count - BLOCK) < length
            acc_k[0:count, :] = jnp.zeros((count, PAIR), f32)
            acc_v[0:count, :] = jnp.zeros((count, PAIR), f32)

            @pl.loop(0, keys)
            def _(index):
                rows = pl.ds(pl.multiple_of(index * BLOCK, BLOCK), BLOCK)
                query = qkv_in[0, 0, 0, rows, :]
                grad = gctx_ref[0, rows, :]
                agree = grad.astype(f32) * ctx_ref[0, rows, :].astype(f32)
                g_query = jnp.zeros((BLOCK, PAIR), f32)
                for head in range(2):
                    mine = (lane < HEAD_DIM) if head == 0 else (lane >= HEAD_DIM)
                    only = lambda values: jnp.where(mine, values, jnp.zeros_like(values))
                    query_h, grad_h, key_h = only(query), only(grad), only(key)
                    delta = jnp.sum(only(agree), axis=1, keepdims=True)
                    scores = nt(query_h, key)
                    last = jnp.where(usable, scores[:, count - BLOCK :], masked_fill)
                    scores = jnp.concatenate([scores[:, : count - BLOCK], last], axis=1) if keys > 1 else last
                    probs = jnp.exp(scores - lse_ref[0, 0, rows, head : head + 1])
                    g_probs = nt(grad_h, value)
                    g_scores = (probs * (g_probs - delta)).astype(bf16)
                    g_query = g_query + nn(g_scores, key_h)
                    acc_k[0:count, :] += tn(g_scores, query_h)
                    acc_v[0:count, :] += tn(probs.astype(bf16), grad_h)
                mixed[pair, rows, :] = (g_query * factor).astype(bf16)

            mixed[PAIRS + pair, 0:count, :] = acc_k[0:count, :].astype(bf16)
            mixed[2 * PAIRS + pair, 0:count, :] = acc_v[0:count, :].astype(bf16)

    @pl.when(pair == PAIRS - 1)
    def _():
        @pl.loop(0, rows_all // BLOCK)
        def _(index):
            rows = pl.ds(pl.multiple_of(index * BLOCK, BLOCK), BLOCK)

            @pl.when(index >= blocks)
            def _():
                gin_ref[0, rows, :] = jnp.zeros((BLOCK, width), bf16)

            @pl.when(index < blocks)
            def _():
                tokens = x_ref[0, rows, :]
                g_in = gres_ref[0, rows, :]
                for part in range(3):
                    cols = slice(part * width, (part + 1) * width)
                    piece = jnp.concatenate([mixed[part * PAIRS + head, rows, :] for head in range(PAIRS)], axis=1)
                    g_in = g_in + nt(piece, w_ref[:, cols])
                    acc_w[:, cols] += tn(tokens, piece)
                    if part != 1:
                        dvec_ref[part // 2 : part // 2 + 1, :] += jnp.sum(piece.astype(f32), axis=0, keepdims=True)
                gin_ref[0, rows, :] = g_in.astype(bf16)

    @pl.when(jnp.logical_and(seq == pl.num_programs(0) - 1, pair == PAIRS - 1))
    def _():
        copies = []
        for part in range(3):
            cols = slice(part * width, (part + 1) * width)
            slot = part % 2
            if part >= 2:
                copies[part - 2].wait()
            stage[slot] = acc_w[:, cols].astype(bf16)
            copies.append(pltpu.make_async_copy(stage.at[slot], dw_ref.at[:, cols], sems.at[slot]))
            copies[-1].start()
        copies[-2].wait()
        copies[-1].wait()


def attention_backward(lengths, tokens, qkv, context, g_context, lse, g_res1, w_qkv):
    seqs, rows, width = tokens.shape
    whole = lambda shape: pl.BlockSpec(shape, lambda s, p, *_: (0,) * len(shape), pipeline_mode=pl.Buffered(1))
    pair_cols = pl.BlockSpec((1, rows, PAIR), lambda s, p, *_: (s, 0, p))
    seq_rows = pl.BlockSpec((1, rows, width), lambda s, p, *_: (s, 0, 0))
    return pl.pallas_call(
        backward_kernel,
        out_shape=(
            jax.ShapeDtypeStruct((seqs, rows, width), bf16),
            jax.ShapeDtypeStruct(w_qkv.shape, bf16),
            jax.ShapeDtypeStruct((8, width), f32),
        ),
        grid_spec=pltpu.PrefetchScalarGridSpec(
            num_scalar_prefetch=1,
            grid=(seqs, PAIRS),
            in_specs=[
                seq_rows,
                pl.BlockSpec((1, 3, 1, rows, PAIR), lambda s, p, *_: (s, 0, p, 0, 0)),
                pair_cols,
                pair_cols,
                pl.BlockSpec((1, 1, rows, PAIR), lambda s, p, *_: (s, p, 0, 0)),
                seq_rows,
                whole(w_qkv.shape),
            ],
            out_specs=[
                seq_rows,
                pl.BlockSpec(memory_space=pl.ANY),
                whole((8, width)),
            ],
            scratch_shapes=[
                pltpu.VMEM((3 * PAIRS, rows, PAIR), bf16),
                pltpu.VMEM(w_qkv.shape, f32),
                pltpu.VMEM((rows, PAIR), f32),
                pltpu.VMEM((rows, PAIR), f32),
                pltpu.VMEM((2, width, width), bf16),
                pltpu.SemaphoreType.DMA((2,)),
            ],
        ),
        compiler_params=pltpu.CompilerParams(vmem_limit_bytes=60 << 20),
        cost_estimate=pl.CostEstimate(
            flops=120_000_000_000, transcendentals=30_000_000, bytes_accessed=40_000_000
        ),
        name="attention_backward",
    )(lengths, tokens, qkv.reshape(seqs, 3, PAIRS, rows, PAIR), context, g_context, lse, g_res1, w_qkv)


def mesh_axes(dp, fsdp):
    if (dp, fsdp) == (8, 4):
        return (("dp", 2, 4), ("dp", 1, 2), ("fsdp", 2, 2), ("fsdp", 1, 2))
    return None


class Place:
    def __init__(self, axes):
        self.axes = axes
        self.at = {name: lax.axis_index(name) for name in BOTH}
        self.own = [lax.rem(self.at[name] // stride, size) for name, stride, size in axes]

    def shifted(self, dim, step):
        size = self.axes[dim][2]
        return lax.rem(self.own[dim] + step + size, size)

    def device(self, dim, step):
        name, stride, _ = self.axes[dim]
        moved = self.at[name] + (self.shifted(dim, step) - self.own[dim]) * stride
        return tuple(moved if name == axis else self.at[axis] for axis in BOTH)

    def steps(self, dim):
        return range(1, self.axes[dim][2])


def meet(place, others=()):
    barrier = pltpu.get_barrier_semaphore()
    peers = [place.device(dim, step) for dim in range(len(place.axes)) for step in place.steps(dim)] + list(others)
    for peer in peers:
        pl.semaphore_signal(barrier, inc=1, device_id=peer, device_id_type=MESH)
    pl.semaphore_wait(barrier, len(peers))


def gather_kernel(axes, parts, waves, count, *refs):
    shards, outs = refs[:count], refs[count : 2 * count]
    send, recv, core_send, core_recv, local = refs[2 * count :]
    place = Place(axes)
    own = place.own
    core = len(axes) - 1
    meet(place)
    mine = [pltpu.make_async_copy(shards[i], outs[i].at[tuple(own)], local.at[i]) for i in range(count)]
    for copy in mine:
        copy.start()
    sent, crossed = [], []
    spots = [list(own) for _ in parts]
    arriving = [[] for _ in parts]
    pieces = [0] * len(parts)
    used = [0] * len(parts)

    def cross(number, spot, source=None):
        array, cols, _ = parts[number]
        there = outs[array].at[tuple(spot) + (slice(None), cols)]
        copy = pltpu.make_async_remote_copy(
            there if source is None else source,
            there,
            core_send.at[number, pieces[number]],
            core_recv.at[number, pieces[number]],
            device_id=place.device(core, 1),
            device_id_type=MESH,
        )
        pieces[number] += 1
        copy.start()
        sent.append(copy)
        crossed.append(copy)

    stages = core
    waiting = list(mine)
    for time in range(max(waves) + stages + 1):
        for number, (array, cols, order) in enumerate(parts):
            stage = time - waves[number]
            if not 0 <= stage <= stages:
                continue
            spot = spots[number]
            fresh = []
            if stage == 0:
                source = shards[array].at[:, cols]
            else:
                while waiting:
                    waiting.pop().wait()
                dim = order[stage - 1]
                for step, copy in enumerate(arriving[number], 1):
                    copy.wait_recv()
                    fresh.append(spot[:dim] + [place.shifted(dim, -step)] + spot[dim + 1 :])
                spot[dim] = slice(None)
                source = outs[array].at[tuple(spot) + (slice(None), cols)]
            if stage < stages:
                dim = order[stage]
                arriving[number] = []
                for step in place.steps(dim):
                    copy = pltpu.make_async_remote_copy(
                        source,
                        outs[array].at[tuple(spot) + (slice(None), cols)],
                        send.at[number, used[number]],
                        recv.at[number, used[number]],
                        device_id=place.device(dim, step),
                        device_id_type=MESH,
                    )
                    used[number] += 1
                    copy.start()
                    sent.append(copy)
                    arriving[number].append(copy)
            if stage == 0:
                cross(number, own, source)
            for block in fresh:
                cross(number, block)
    for copy in crossed:
        copy.wait_recv()
    for copy in sent:
        copy.wait_send()


def gather_blocks(axes, parts, waves, shards):
    sizes = tuple(size for _, _, size in axes)
    hops = sum(size - 1 for size in sizes[:-1])
    count = len(shards)
    sems = lambda *shape: pltpu.SemaphoreType.DMA(shape)
    return pl.pallas_call(
        functools.partial(gather_kernel, axes, parts, waves, count),
        out_shape=tuple(jax.ShapeDtypeStruct(sizes + shard.shape, shard.dtype) for shard in shards),
        in_specs=[pl.BlockSpec(memory_space=pl.ANY)] * count,
        out_specs=tuple([pl.BlockSpec(memory_space=pl.ANY)] * count),
        scratch_shapes=[
            sems(len(parts), hops),
            sems(len(parts), hops),
            sems(len(parts), hops + 1),
            sems(len(parts), hops + 1),
            sems(count),
        ],
        compiler_params=pltpu.CompilerParams(collective_id=1, has_side_effects=True),
        name="gather_blocks",
    )(*shards)


def scatter_kernel(axes, parts, waves, count, *refs):
    grads, note, outs, notes = refs[:count], refs[count], refs[count + 1 : 2 * count + 1], refs[2 * count + 1]
    bufs, small, (send, recv, local, note_send, note_recv) = refs[-15:-10], refs[-10:-5], refs[-5:]
    place = Place(axes)
    own = place.own
    depth = axes[0][2]
    core = len(axes) - 1
    shards = notes.shape[0]
    member = place.at["fsdp"]
    friends = [lax.rem(member + step, shards) for step in range(1, shards)]
    meet(place, [(place.at["dp"], friend) for friend in friends])
    sent, told = [], []
    live = [{} for _ in parts]
    for step, friend in enumerate(friends):
        copy = pltpu.make_async_remote_copy(
            note,
            notes.at[member],
            note_send.at[step],
            note_recv.at[step],
            device_id=(place.at["dp"], friend),
            device_id_type=MESH,
        )
        copy.start()
        sent.append(copy)
        told.append(copy)
    notes[member] = note[...]

    def buffers(number):
        if parts[number][1] is None:
            return small
        return [buf.at[number] for buf in bufs]

    def push(number, piece, source, target, dim, step):
        copy = pltpu.make_async_remote_copy(
            source,
            target,
            send.at[number, piece],
            recv.at[number, piece],
            device_id=place.device(dim, step),
            device_id_type=MESH,
        )
        copy.start()
        sent.append(copy)
        return copy

    def plus(acc, spot, extra):
        acc[spot] = (acc[spot].astype(f32) + extra.astype(f32)).astype(acc.dtype)

    def advance(number, stage):
        array, cols, (one, two) = parts[number]
        acc, from_core, from_one, from_two, from_z = buffers(number)
        state = live[number]
        own_one, own_two = own[one], own[two]
        peer_one, peer_two = place.shifted(one, 1), place.shifted(two, 1)

        def spot(first, second, z):
            index = [z, None, None]
            index[one], index[two] = first, second
            return tuple(index)

        if stage == 0:
            rows = (slice(None),) * core
            last = (slice(None), slice(None) if cols is None else cols)
            state["core"] = push(number, 0, grads[array].at[rows + (place.shifted(core, 1),) + last], from_core, core, 1)
            state["own"] = pltpu.make_async_copy(grads[array].at[rows + (own[core],) + last], acc, local.at[number])
            state["own"].start()
        elif stage == 1:
            state["own"].wait()
            state["core"].wait_recv()
            for first in (peer_one, own_one):

                def both(z, carry, first=first):
                    for second in range(axes[two][2]):
                        plus(acc, spot(first, second, z), from_core[spot(first, second, z)])
                    return carry

                lax.fori_loop(0, depth, both, 0)
                if first is peer_one:
                    state["one"] = push(number, 1, acc.at[spot(peer_one, slice(None), slice(None))], from_one, one, 1)
        elif stage == 2:
            state["one"].wait_recv()
            for second in (peer_two, own_two):

                def single(z, carry, second=second):
                    plus(acc, spot(own_one, second, z), from_one[z, second])
                    return carry

                lax.fori_loop(0, depth, single, 0)
                if second is peer_two:
                    state["two"] = push(number, 2, acc.at[spot(own_one, peer_two, slice(None))], from_two, two, 1)
        elif stage == 3:
            state["two"].wait_recv()
            state["z"] = []
            for step in list(range(1, depth)) + [0]:
                z = place.shifted(0, step)
                plus(acc, spot(own_one, own_two, z), from_two[z])
                if step:
                    source = acc.at[spot(own_one, own_two, z)]
                    state["z"].append(push(number, 2 + step, source, from_z.at[step - 1], 0, step))
        else:
            total = acc[spot(own_one, own_two, own[0])].astype(f32)
            for step, copy in enumerate(state["z"]):
                copy.wait_recv()
                total = total + from_z[step].astype(f32)
            if cols is None:
                outs[array][...] = total
            else:
                outs[array][:, cols] = total

    for time in range(max(waves) + 5):
        for number in range(len(parts)):
            if 0 <= time - waves[number] <= 4:
                advance(number, time - waves[number])
    for copy in told:
        copy.wait_recv()
    for copy in sent:
        copy.wait_send()


def scatter_sums(axes, parts, waves, grads, note):
    sizes = tuple(size for _, _, size in axes)
    depth, across, along, _ = sizes
    blocks = [grad.reshape(sizes + (-1, grad.shape[1])) for grad in grads]
    tiles = sum(1 for part in parts if part[1] is not None)
    rows, width = blocks[0].shape[4], parts[0][1].size
    shards = along * sizes[3]
    big = lambda *lead: pltpu.VMEM((tiles,) + lead + (rows, width), bf16)
    tiny = lambda *lead: pltpu.VMEM(lead + blocks[-1].shape[4:], f32)
    sems = lambda *shape: pltpu.SemaphoreType.DMA(shape)
    vmem = pl.BlockSpec(memory_space=pltpu.VMEM)
    leads = ((depth, across, along), (depth, across, along), (depth, 2), (depth,), (depth - 1,))
    return pl.pallas_call(
        functools.partial(scatter_kernel, axes, parts, waves, len(grads)),
        out_shape=tuple(jax.ShapeDtypeStruct(block.shape[4:], f32) for block in blocks)
        + (jax.ShapeDtypeStruct((shards,) + note.shape, f32),),
        in_specs=[pl.BlockSpec(memory_space=pl.ANY)] * len(grads) + [vmem],
        out_specs=tuple([vmem] * (len(grads) + 1)),
        scratch_shapes=[big(*lead) for lead in leads]
        + [tiny(*lead) for lead in leads]
        + [
            sems(len(parts), 2 + depth),
            sems(len(parts), 2 + depth),
            sems(len(parts)),
            sems(shards - 1),
            sems(shards - 1),
        ],
        compiler_params=pltpu.CompilerParams(collective_id=2, has_side_effects=True, vmem_limit_bytes=56 << 20),
        name="scatter_sums",
    )(*blocks, note)


def body(
    tokens, lengths, deal_order, qkv_weight, query_bias, value_bias, out_weight, out_bias, attn_gain, attn_shift,
    up_weight, up_bias, down_weight, down_bias, ffn_gain, ffn_shift, cotangent,
):
    shards = lax.axis_size("fsdp")
    axes = mesh_axes(lax.axis_size("dp"), shards)
    devices = lax.axis_size("dp") * shards
    seqs, rows, width = tokens.shape
    hidden = up_weight.shape[1]
    chunks = hidden // width
    per = width // devices
    column = shards * seqs
    base = lax.axis_index("dp") * column
    member = lax.axis_index("fsdp")
    order = lax.dynamic_slice_in_dim(deal_order, base, column) - base
    mine = member * seqs
    own_lengths = lax.dynamic_slice_in_dim(lengths, base + mine, seqs)
    target = lax.dynamic_slice_in_dim(order, mine, seqs) // seqs
    dealt_here = mine + jnp.arange(seqs, dtype=jnp.int32)
    matches = order[None, :] == dealt_here[:, None]
    source = jnp.sum(jnp.where(matches, jnp.arange(column, dtype=jnp.int32)[None, :], 0), axis=1)
    peers = jnp.arange(shards, dtype=jnp.int32)

    up_mixed = up_weight.reshape(per, width, chunks).transpose(0, 2, 1).reshape(per, hidden)
    rest = jnp.concatenate([out_weight, up_mixed, down_weight.reshape(per, hidden)], axis=1)
    weights = lax.all_gather(rest, BOTH, axis=0, tiled=True)

    outgoing = cotangent[0][None]
    for place in range(1, seqs):
        outgoing = jnp.where((source[place] // seqs == peers)[:, None, None], cotangent[place][None], outgoing)
    cots = lax.all_to_all(outgoing, "fsdp", split_axis=0, concat_axis=0, tiled=True)

    small = jnp.concatenate(
        [query_bias, value_bias, out_bias, attn_gain, attn_shift, down_bias, ffn_gain, ffn_shift, up_bias]
    )
    small = jnp.pad(small, (0, 8 * 128 - small.shape[0])).reshape(8, 128)
    if axes is None:
        w_qkv = lax.all_gather(qkv_weight, BOTH, axis=0, tiled=True)
        small = lax.all_gather(small, BOTH, axis=0, tiled=False)
    else:
        cut = qkv_weight.shape[1] // 6
        orders = ((0, 2, 1), (0, 2, 1), (1, 0, 2))
        parts = [(1, slice(None), orders[0])] + [(0, pl.ds(i * cut, cut), orders[i % 3]) for i in range(6)]
        w_qkv, small = gather_blocks(axes, parts, [0] * 7, [qkv_weight, small])
        w_qkv = w_qkv.reshape(width, -1)
    small = small.reshape(devices, -1)
    vectors = small[:, : 8 * per].reshape(devices, 8, per).transpose(1, 0, 2).reshape(8, width)
    bias_up = small[:, 8 * per : 8 * per + chunks * per].reshape(width, chunks).T.reshape(1, hidden)

    qkv, context, lse = attention_forward(own_lengths, tokens, w_qkv, vectors)
    results, g_res1, g_context, dw_rest, dvec, dbu, rms = middle(
        own_lengths, target, target, tokens, context, cots, weights, vectors, bias_up
    )
    arrived = lax.all_to_all(results, "fsdp", split_axis=0, concat_axis=0, tiled=True)
    input_grad, dw_qkv, dqv = attention_backward(own_lengths, tokens, qkv, context, g_context, lse, g_res1, w_qkv)
    layer_out = jnp.stack(
        [lax.dynamic_index_in_dim(arrived, source[t] // seqs, 0, keepdims=False) for t in range(seqs)]
    )

    dvec = (dvec + dqv).reshape(8, devices, per).transpose(1, 0, 2).reshape(devices, 8 * per)
    dbu = dbu.reshape(chunks, devices, per).transpose(1, 2, 0).reshape(devices, chunks * per)
    packed = jnp.pad(jnp.concatenate([dvec, dbu], axis=1), ((0, 0), (0, 8 * 128 - (8 + chunks) * per)))
    rms = rms.reshape(seqs * 8, 128)
    if axes is None:
        scatter = lambda whole: lax.psum_scatter(whole, BOTH, scatter_dimension=0, tiled=True)
        qkvw_grad, rest_grad = scatter(dw_qkv).astype(f32), scatter(dw_rest).astype(f32)
        packed = scatter(packed)
        rms = lax.all_gather(rms, "fsdp", axis=0, tiled=False)
    else:
        parts = [
            (array, pl.ds(place, width), ((2, 1), (1, 2))[place // width % 2])
            for array, grad in enumerate((dw_qkv, dw_rest))
            for place in range(0, grad.shape[1], width)
        ]
        waves = [place // 4 for place in range(len(parts))] + [0]
        parts.append((2, None, (2, 1)))
        qkvw_grad, rest_grad, packed, rms = scatter_sums(
            axes, parts, waves, [dw_qkv, dw_rest, packed.reshape(devices * 8, 128)], rms
        )
    packed = packed.reshape(-1)
    vector = [packed[place * per : (place + 1) * per] for place in range(8)]
    rms = rms.reshape(column, 8, 128)[:, :3, 0]
    branch_rms = jnp.sum(jnp.where((source[:, None] == jnp.arange(column))[:, :, None], rms[None], 0.0), axis=1)
    outw_grad = rest_grad[:, :width]
    upw_grad = rest_grad[:, width : width + hidden].reshape(per, chunks, width).transpose(0, 2, 1).reshape(per, hidden)
    downw_grad = rest_grad[:, width + hidden :].reshape(per * chunks, width)
    return (
        layer_out, input_grad, qkvw_grad, vector[0], vector[1], outw_grad, vector[2], vector[3], vector[4], upw_grad,
        packed[8 * per : 8 * per + chunks * per], downw_grad, vector[5], vector[6], vector[7], branch_rms,
    )


def solution(mesh):
    rows3, rows2, rows1 = P(BOTH, None, None), P(BOTH, None), P(BOTH)
    in_specs = (
        rows3, P(), P(), rows2, rows1, rows1, rows2, rows1, rows1, rows1, rows2, rows1, rows2, rows1, rows1, rows1, rows3,
    )
    out_specs = (
        rows3, rows3, rows2, rows1, rows1, rows2, rows1, rows1, rows1, rows2, rows1, rows2, rows1, rows1, rows1, rows2,
    )
    return jax.shard_map(body, mesh=mesh, in_specs=in_specs, out_specs=out_specs, check_vma=False)
```

```python
import functools
import math

import jax
import jax.numpy as jnp
from jax import lax
from jax.experimental import pallas as pl
from jax.experimental.pallas import tpu as pltpu
from jax.sharding import PartitionSpec as P

HEADS = 12
HEAD_DIM = 64
PAIR = 2 * HEAD_DIM
PAIRS = HEADS // 2
BLOCK = 256
ROWS = 512
PIECES = 8

f32 = jnp.float32
bf16 = jnp.bfloat16
norm_eps = 1e-05
masked_fill = -1e30
BOTH = ("dp", "fsdp")
MESH = pl.DeviceIdType.MESH


def nn(left, right):
    return lax.dot_general(left, right, (((1,), (0,)), ((), ())), preferred_element_type=f32)


def nt(left, right):
    return lax.dot_general(left, right, (((1,), (1,)), ((), ())), preferred_element_type=f32)


def tn(left, right):
    return lax.dot_general(left, right, (((0,), (0,)), ((), ())), preferred_element_type=f32)


def block_count(length):
    return (length + (BLOCK - 1)) // BLOCK


def whole(shape):
    return pl.BlockSpec(shape, lambda *_: (0,) * len(shape), pipeline_mode=pl.Buffered(1))


def sems(*shape):
    return pltpu.SemaphoreType.DMA(shape)


ANY = pl.BlockSpec(memory_space=pl.ANY)
VMEM = pl.BlockSpec(memory_space=pltpu.VMEM)


def mesh_axes(dp, fsdp):
    if (dp, fsdp) == (8, 4):
        return (("dp", 2, 4), ("dp", 1, 2), ("fsdp", 2, 2), ("fsdp", 1, 2))
    return None


class Place:
    def __init__(self, axes):
        self.axes = axes
        self.core = len(axes) - 1
        self.at = {name: lax.axis_index(name) for name in BOTH}
        self.own = [lax.rem(self.at[name] // stride, size) for name, stride, size in axes]

    def shifted(self, dim, step):
        size = self.axes[dim][2]
        return lax.rem(self.own[dim] + step + size, size)

    def device(self, dim, step):
        name, stride, _ = self.axes[dim]
        moved = self.at[name] + (self.shifted(dim, step) - self.own[dim]) * stride
        return tuple(moved if name == axis else self.at[axis] for axis in BOTH)

    def steps(self, dim):
        return range(1, self.axes[dim][2])

    def friends(self, count):
        member = self.at["fsdp"]
        return [lax.rem(member + step, count) for step in range(1, count)]


def meet(place, friends=()):
    barrier = pltpu.get_barrier_semaphore()
    peers = [place.device(dim, step) for dim in range(len(place.axes)) for step in place.steps(dim)]
    peers += [(place.at["dp"], friend) for friend in friends]
    for peer in peers:
        pl.semaphore_signal(barrier, inc=1, device_id=peer, device_id_type=MESH)
    pl.semaphore_wait(barrier, len(peers))


def push(source, target, send, recv, device):
    return pltpu.make_async_remote_copy(source, target, send, recv, device_id=device, device_id_type=MESH)


class Exchange:
    def __init__(self, place, mine, theirs, pieces, send, recv, local):
        self.place, self.mine, self.theirs, self.pieces = place, mine, theirs, pieces
        self.send, self.recv, self.local = send, recv, local

    def copies(self, piece):
        member = self.place.at["fsdp"]
        height = self.mine.shape[1] // self.pieces
        rows = pl.ds(piece * height, height)
        made = [
            push(
                self.mine.at[friend, rows],
                self.theirs.at[member, rows],
                self.send.at[step, piece],
                self.recv.at[step, piece],
                (self.place.at["dp"], friend),
            )
            for step, friend in enumerate(self.place.friends(self.mine.shape[0]))
        ]
        return made + [pltpu.make_async_copy(self.mine.at[member, rows], self.theirs.at[member, rows], self.local.at[piece])]

    def start(self, piece):
        for copy in self.copies(piece):
            copy.start()

    def wait(self):
        for piece in range(self.pieces):
            for copy in self.copies(piece):
                copy.wait()


def exchange_sems(friends):
    return [sems(friends, PIECES), sems(friends, PIECES), sems(PIECES)]


class Gather:
    def __init__(self, place, parts, shards, outs, send, recv, core_send, core_recv, local):
        self.place, self.parts, self.shards, self.outs = place, parts, shards, outs
        self.sems = send, recv
        self.core_sems = core_send, core_recv
        self.mine = [
            pltpu.make_async_copy(shard, out.at[tuple(place.own)], local.at[i])
            for i, (shard, out) in enumerate(zip(shards, outs))
        ]

    def start(self):
        for copy in self.mine:
            copy.start()

    def local(self):
        for copy in self.mine:
            copy.wait()

    def view(self, number, spot):
        array, cols, _ = self.parts[number]
        return self.outs[array].at[tuple(spot) + (slice(None), cols)]

    def shard(self, number):
        array, cols, _ = self.parts[number]
        return self.shards[array].at[:, cols]

    def known(self, number, stage):
        order = self.parts[number][2]
        return [slice(None) if dim in order[:stage] else own for dim, own in enumerate(self.place.own)]

    def link(self, number, stage):
        order = self.parts[number][2]
        spot = self.known(number, stage)
        source = self.view(number, spot) if stage else self.shard(number)
        first = sum(self.place.axes[dim][2] - 1 for dim in order[:stage])
        send, recv = self.sems
        return [
            push(
                source,
                self.view(number, spot),
                send.at[number, first + step - 1],
                recv.at[number, first + step - 1],
                self.place.device(order[stage], step),
            )
            for step in self.place.steps(order[stage])
        ]

    def across(self, number, stage):
        order = self.parts[number][2]
        core_send, core_recv = self.core_sems
        peer = self.place.device(self.place.core, 1)
        if stage == 0:
            spot = self.known(number, 0)
            return [push(self.shard(number), self.view(number, spot), core_send.at[number, 0], core_recv.at[number, 0], peer)]
        first = sum(self.place.axes[dim][2] - 1 for dim in order[: stage - 1])
        dim = order[stage - 1]
        copies = []
        for step in self.place.steps(dim):
            spot = self.known(number, stage - 1)
            spot[dim] = self.place.shifted(dim, -step)
            view, piece = self.view(number, spot), first + step
            copies.append(push(view, view, core_send.at[number, piece], core_recv.at[number, piece], peer))
        return copies

    def advance(self, number, stage):
        if stage:
            for copy in self.link(number, stage - 1):
                copy.wait_recv()
        if stage < self.place.core:
            for copy in self.link(number, stage):
                copy.start()
        for copy in self.across(number, stage):
            copy.start()

    def finish(self, number):
        for stage in range(self.place.core + 1):
            if stage < self.place.core:
                for copy in self.link(number, stage):
                    copy.wait_send()
            for copy in self.across(number, stage):
                copy.wait()


def gather_sems(axes, parts, count):
    hops = sum(size - 1 for _, _, size in axes[:-1])
    shapes = (len(parts), hops), (len(parts), hops), (len(parts), hops + 1), (len(parts), hops + 1), (count,)
    return [sems(*shape) for shape in shapes]


class Scatter:
    def __init__(self, place, parts, grads, outs, bufs, send, recv, local):
        self.place, self.parts, self.grads, self.outs = place, parts, grads, outs
        self.bufs = bufs
        self.send, self.recv, self.local = send, recv, local

    def refs(self, number):
        _, _, order, slot = self.parts[number]
        own, *came = self.bufs[order if self.parts[number][1] is not None else None]
        held = own.shape[0]
        return [own.at[slot % held]] + [buf.at[slot] for buf in came]

    def first(self, number, stage):
        order = self.parts[number][2]
        return 1 + sum(self.place.axes[dim][2] - 1 for dim in order[:stage])

    def block(self, number, core):
        array, cols, _, _ = self.parts[number]
        lead = (slice(None),) * self.place.core + (core,)
        return self.grads[array].at[lead + (slice(None), slice(None) if cols is None else cols)]

    def across(self, number):
        place = self.place
        return push(
            self.block(number, place.shifted(place.core, 1)),
            self.refs(number)[1],
            self.send.at[number, 0],
            self.recv.at[number, 0],
            place.device(place.core, 1),
        )

    def own(self, number):
        return pltpu.make_async_copy(
            self.block(number, self.place.own[self.place.core]), self.refs(number)[0], self.local.at[number]
        )

    def spot(self, number, stage, at):
        order = self.parts[number][2]
        dims = [slice(None)] * self.place.core
        for dim in order[:stage]:
            dims[dim] = self.place.own[dim]
        if at is not None:
            dims[order[stage]] = at
        return dims

    def link(self, number, stage, step):
        dim = self.parts[number][2][stage]
        place, refs = self.place, self.refs(number)
        piece = self.first(number, stage) + step - 1
        return push(
            refs[0].at[tuple(self.spot(number, stage, place.shifted(dim, step)))],
            refs[2 + stage].at[step - 1],
            self.send.at[number, piece],
            self.recv.at[number, piece],
            place.device(dim, step),
        )

    def add(self, number, spot, extras):
        acc = self.refs(number)[0]
        free = [dim for dim, index in enumerate(spot) if isinstance(index, slice)]
        sizes = [self.place.axes[dim][2] for dim in free]
        total = math.prod(sizes)

        def one(place, carry):
            index, where = list(spot), []
            rest = place
            for dim, size in zip(reversed(free), reversed(sizes)):
                index[dim] = lax.rem(rest, size)
                where.insert(0, index[dim])
                rest = rest // size
            index = tuple(index)
            value = acc[index].astype(f32)
            for extra in extras:
                value = value + extra[tuple(where)].astype(f32)
            acc[index] = value.astype(acc.dtype)
            return carry

        if total == 1:
            one(0, 0)
        else:
            lax.fori_loop(0, total, one, 0)

    def advance(self, number, stage):
        array, cols, order, _ = self.parts[number]
        place, refs = self.place, self.refs(number)
        if stage == 0:
            self.across(number).start()
            self.own(number).start()
            return
        if stage == 1:
            self.own(number).wait()
            self.across(number).wait_recv()
            came = [refs[1]]
        else:
            dim = order[stage - 2]
            for step in place.steps(dim):
                self.link(number, stage - 2, step).wait_recv()
            came = [refs[stage].at[step - 1] for step in place.steps(dim)]
        if stage <= place.core:
            dim = order[stage - 1]
            for step in list(place.steps(dim)) + [0]:
                at = place.shifted(dim, step)
                spot = self.spot(number, stage - 1, at)
                where = self.within(number, stage - 1, at)
                self.add(number, spot, [extra.at[where] for extra in came])
                if step:
                    self.link(number, stage - 1, step).start()
        else:
            total = refs[0][tuple(place.own[:-1])].astype(f32)
            for extra in came:
                total = total + extra[...].astype(f32)
            if cols is None:
                self.outs[array][...] = total
            else:
                self.outs[array][:, cols] = total

    def within(self, number, stage, at):
        order = self.parts[number][2]
        rest = [dim for dim in range(self.place.core) if dim not in order[:stage]]
        return tuple(at if dim == order[stage] else slice(None) for dim in rest)

    def finish(self, number):
        self.across(number).wait_send()
        order = self.parts[number][2]
        for stage, dim in enumerate(order):
            for step in self.place.steps(dim):
                self.link(number, stage, step).wait_send()


def scatter_buffers(axes, order, tiles, held, block, dtype):
    sizes = [size for _, _, size in axes[:-1]]
    leads = [(held,) + tuple(sizes), (tiles,) + tuple(sizes)]
    left = list(range(len(sizes)))
    for dim in order:
        left.remove(dim)
        leads.append((tiles, sizes[dim] - 1) + tuple(sizes[other] for other in left))
    return [pltpu.VMEM(lead + tuple(block), dtype) for lead in leads]


def scatter_sems(axes, count):
    hops = 1 + sum(size - 1 for _, _, size in axes[:-1])
    return [sems(count, hops), sems(count, hops), sems(count)]


def run_steps(mover, exchange, plan, time, steps):
    for step in range(steps):
        todo = [(part, stage) for part, row in enumerate(plan) for stage, at in enumerate(row) if at == step]

        @pl.when(time == step)
        def _(todo=todo, step=step):
            for part, stage in todo:
                mover.advance(part, stage)
            if 1 <= step <= PIECES:
                exchange.start(step - 1)


def run_rest(mover, exchange, plan, steps):
    for part, row in enumerate(plan):
        for stage, at in enumerate(row):
            if at >= steps:
                mover.advance(part, stage)
    for part in range(len(plan)):
        mover.finish(part)
    exchange.wait()


def forward_kernel(axes, seqs, parts, plan, len_ref, x_ref, w_ref, bias_ref, *refs):
    if axes is None:
        qkv_ref, ctx_ref, probs_ref = refs
    else:
        rest_ref, cot_ref, qkv_ref, ctx_ref, probs_ref, weights_ref, cots_ref = refs[:7]
        place = Place(axes)
        gather = Gather(place, parts, [rest_ref], [weights_ref], *refs[7:12])
        exchange = Exchange(place, cot_ref, cots_ref, PIECES, *refs[12:15])
    seq, pair = pl.program_id(0), pl.program_id(1)
    time = seq * PAIRS + pair
    steps = seqs * PAIRS
    length = len_ref[seq]
    count, width = x_ref.shape[1], x_ref.shape[2]
    lane = lax.broadcasted_iota(jnp.int32, (1, PAIR), 1)

    if axes is not None:

        @pl.when(time == 0)
        def _():
            meet(place, place.friends(cot_ref.shape[0]))
            gather.start()
            gather.local()

        run_steps(gather, exchange, plan, time, steps)

    @pl.when(pair == 0)
    def _():
        tokens = x_ref[0]
        step = 2 * PAIR
        for start in range(0, 3 * width, step):
            part = start // width
            projected = nn(tokens, w_ref[:, start : start + step])
            if part != 1:
                cols = slice(start - part * width, start - part * width + step)
                projected = projected + bias_ref[part // 2 : part // 2 + 1, cols].astype(f32)
            projected = projected.astype(bf16)
            if part == 0:
                projected = projected * jnp.asarray(1.0 / math.sqrt(HEAD_DIM), bf16)
            for half in range(2):
                qkv_ref[0, start // PAIR + half] = projected[:, half * PAIR : (half + 1) * PAIR]

    key = qkv_ref[0, PAIRS + pair]
    value = qkv_ref[0, 2 * PAIRS + pair]
    unusable = lax.broadcasted_iota(jnp.int32, (count, 1), 0) >= length
    mask = jnp.where(unusable, masked_fill, 0.0).astype(bf16)
    keys = [jnp.where(lane == spare, mask, key) for spare in (PAIR - 1, 0)]
    for start in range(0, count, ROWS):
        rows = slice(start, start + ROWS)
        query = qkv_ref[0, pair, rows, :]
        outs = []
        for head in range(2):
            mine = (lane < HEAD_DIM) if head == 0 else (lane >= HEAD_DIM)
            spare = jnp.where(lane == (PAIR - 1 if head == 0 else 0), 1.0, 0.0).astype(bf16)
            scores = nt(jnp.where(mine, query, spare), keys[head])
            top = jnp.max(scores, axis=1, keepdims=True)
            powers = jnp.exp(scores - top)
            total = jnp.sum(powers, axis=1, keepdims=True)
            probs = (powers * (1.0 / total)).astype(bf16)
            probs_ref[0, 0, head, rows, :] = probs
            outs.append(nn(probs, value))
        ctx_ref[0, rows, :] = jnp.where(lane < HEAD_DIM, outs[0], outs[1]).astype(bf16)

    if axes is not None:

        @pl.when(time == steps - 1)
        def _():
            run_rest(gather, exchange, plan, steps)


def attention_forward(axes, lengths, tokens, w_qkv, biases, rest, outgoing):
    seqs, rows, width = tokens.shape
    out_shape = [
        jax.ShapeDtypeStruct((seqs, 3 * PAIRS, rows, PAIR), bf16),
        jax.ShapeDtypeStruct((seqs, rows, width), bf16),
        jax.ShapeDtypeStruct((seqs, PAIRS, 2, rows, rows), bf16),
    ]
    in_specs = [pl.BlockSpec((1, rows, width), lambda s, p, *_: (s, 0, 0)), whole(w_qkv.shape), whole(biases.shape)]
    out_specs = [
        pl.BlockSpec((1, 3 * PAIRS, rows, PAIR), lambda s, p, *_: (s, 0, 0, 0)),
        pl.BlockSpec((1, rows, PAIR), lambda s, p, *_: (s, 0, p)),
        pl.BlockSpec((1, 1, 2, rows, rows), lambda s, p, *_: (s, p, 0, 0, 0)),
    ]
    scratch, extra, parts, plan, talk = [], [], [], [], {}
    if axes is not None:
        parts = [(0, pl.ds(start, width), (2, 0, 1)) for start in range(0, rest.shape[1], width)]
        plan = [[0] + [2 * stage - 1 + max(0, place - 2) for stage in range(1, 4)] for place in range(len(parts))]
        extra = [rest, outgoing]
        in_specs += [ANY, ANY]
        sizes = tuple(size for _, _, size in axes)
        out_shape += [jax.ShapeDtypeStruct(sizes + rest.shape, bf16), jax.ShapeDtypeStruct(outgoing.shape, bf16)]
        out_specs += [ANY, ANY]
        friends = outgoing.shape[0] - 1
        scratch = gather_sems(axes, parts, 1) + exchange_sems(friends)
        talk = {"collective_id": 3, "has_side_effects": True}
    return pl.pallas_call(
        functools.partial(forward_kernel, axes, seqs, parts, plan),
        out_shape=tuple(out_shape),
        grid_spec=pltpu.PrefetchScalarGridSpec(
            num_scalar_prefetch=1,
            grid=(seqs, PAIRS),
            in_specs=in_specs,
            out_specs=tuple(out_specs),
            scratch_shapes=scratch,
        ),
        compiler_params=pltpu.CompilerParams(vmem_limit_bytes=58 << 20, **talk),
        cost_estimate=pl.CostEstimate(flops=60_000_000_000, transcendentals=30_000_000, bytes_accessed=80_000_000),
        name="attention_forward",
    )(lengths, tokens, w_qkv, biases, *extra)


def normal_tail(values):
    size = jnp.abs(values)
    bell = jnp.exp(-0.5 * values * values)
    t = 1.0 / (1.0 + (0.3275911 / math.sqrt(2.0)) * size)
    poly = t * (
        0.5 * 0.254829592
        + t * (0.5 * -0.284496736 + t * (0.5 * 1.421413741 + t * (0.5 * -1.453152027 + t * (0.5 * 1.061405429))))
    )
    tail = poly * bell
    return jnp.where(values >= 0, 1.0 - tail, tail), bell


def row_mean(values):
    return jnp.mean(values, axis=-1, keepdims=True)


def middle_kernel(
    len_ref, in_slot, out_slot, x_ref, ctx_ref, cot_ref, w_ref, vec_ref, bu_ref,
    out_ref, gres_ref, gctx_ref, dw_ref, dvec_ref, dbu_ref, rms_ref,
    acc, active, slope, sums, stage, sems,
):
    seq, index = pl.program_id(0), pl.program_id(1)
    first = jnp.logical_and(seq == 0, index == 0)
    final = jnp.logical_and(seq == pl.num_programs(0) - 1, index == pl.num_programs(1) - 1)
    length = len_ref[seq]
    width = x_ref.shape[2]
    chunks = bu_ref.shape[1] // width
    tile = lambda place: slice(place * width, (place + 1) * width)
    up = lambda chunk: tile(1 + chunk)
    down = lambda chunk: tile(1 + chunks + chunk)

    @pl.when(first)
    def _():
        acc[...] = jnp.zeros_like(acc)
        dvec_ref[...] = jnp.zeros_like(dvec_ref)
        dbu_ref[...] = jnp.zeros_like(dbu_ref)

    @pl.when(index == 0)
    def _():
        sums[...] = jnp.zeros_like(sums)

    @pl.when(index * BLOCK >= length)
    def _():
        out_ref[...] = jnp.zeros_like(out_ref)
        gres_ref[...] = jnp.zeros_like(gres_ref)
        gctx_ref[...] = jnp.zeros_like(gctx_ref)

    @pl.when(index * BLOCK < length)
    def _():
        vec = lambda place: vec_ref[place : place + 1, :].astype(f32)
        bias_out, gain_a, shift_a, bias_down, gain_f, shift_f = (vec(place) for place in range(2, 8))
        valid = (lax.broadcasted_iota(jnp.int32, (BLOCK, 1), 0) + index * BLOCK < length).astype(f32)
        tokens = x_ref[0].astype(f32)
        context = ctx_ref[0]
        branch_a = nn(context, w_ref[:, tile(0)]) + bias_out
        mixed = tokens + branch_a
        center = mixed - row_mean(mixed)
        scale_a = lax.rsqrt(row_mean(center * center) + norm_eps)
        hat_a = center * scale_a
        hidden = hat_a * gain_a + shift_a
        hidden_low = hidden.astype(bf16)
        branch_f = bias_down
        for chunk in range(chunks):
            cols = tile(chunk)
            gate = nn(hidden_low, w_ref[:, up(chunk)]) + bu_ref[:, cols].astype(f32)
            share, bell = normal_tail(gate)
            act = (gate * share).astype(bf16)
            active[:, cols] = act
            slope[:, cols] = share + gate * bell * (1.0 / math.sqrt(2.0 * math.pi))
            branch_f = branch_f + nn(act, w_ref[:, down(chunk)])
        mixed_f = hidden + branch_f
        center = mixed_f - row_mean(mixed_f)
        scale_f = lax.rsqrt(row_mean(center * center) + norm_eps)
        hat_f = center * scale_f
        out_ref[0] = ((hat_f * gain_f + shift_f) * valid).astype(bf16)
        g_result = cot_ref[0].astype(f32) * valid
        g_hat = g_result * gain_f
        g_res2 = scale_f * (g_hat - row_mean(g_hat) - hat_f * row_mean(g_hat * hat_f))
        g_ffn = g_res2.astype(bf16)
        g_hidden = g_res2
        for chunk in range(chunks):
            cols = tile(chunk)
            g_gate = nt(g_ffn, w_ref[:, down(chunk)]) * slope[:, cols]
            g_low = g_gate.astype(bf16)
            acc[:, down(chunk)] += tn(active[:, cols], g_ffn)
            acc[:, up(chunk)] += tn(hidden_low, g_low)
            dbu_ref[:, cols] += jnp.sum(g_low.astype(f32), axis=0, keepdims=True)
            g_hidden = g_hidden + nt(g_low, w_ref[:, up(chunk)])
        g_hat = g_hidden * gain_a
        g_res1 = scale_a * (g_hat - row_mean(g_hat) - hat_a * row_mean(g_hat * hat_a))
        g_attn = g_res1.astype(bf16)
        gres_ref[0] = g_res1
        gctx_ref[0] = nt(g_attn, w_ref[:, tile(0)]).astype(bf16)
        acc[:, tile(0)] += tn(context, g_attn)
        column = lambda values: jnp.sum(values, axis=0, keepdims=True)
        dvec_ref[2:3, :] += column(g_attn.astype(f32))
        dvec_ref[3:4, :] += column(g_hidden * hat_a)
        dvec_ref[4:5, :] += column(g_hidden)
        dvec_ref[5:6, :] += column(g_ffn.astype(f32))
        dvec_ref[6:7, :] += column(g_result * hat_f)
        dvec_ref[7:8, :] += column(g_result)
        sums[0:1, :] += column(tokens * tokens * valid)
        sums[1:2, :] += column(branch_a * branch_a * valid)
        sums[2:3, :] += column(branch_f * branch_f * valid)

    @pl.when(index == pl.num_programs(1) - 1)
    def _():
        mean = jnp.sum(sums[...], axis=1, keepdims=True) / (length * width).astype(f32)
        rms_ref[0] = jnp.broadcast_to(jnp.sqrt(mean), rms_ref.shape[1:])

    @pl.when(final)
    def _():
        copies = []
        for place in range(1 + 2 * chunks):
            slot = place % 2
            if place >= 2:
                copies[place - 2].wait()
            stage[slot] = acc[:, tile(place)].astype(bf16)
            copies.append(pltpu.make_async_copy(stage.at[slot], dw_ref.at[:, tile(place)], sems.at[slot]))
            copies[-1].start()
        copies[-2].wait()
        copies[-1].wait()


def middle(lengths, in_slot, out_slot, tokens, context, cots, weights, vectors, bias_up):
    seqs, rows, width = tokens.shape
    slots = cots.shape[0]
    hidden = bias_up.shape[1]
    inside = lambda s, i, lens: jnp.minimum(i, block_count(lens[s]) - 1)
    here = pl.BlockSpec((1, BLOCK, width), lambda s, i, lens, a, b: (s, inside(s, i, lens), 0))
    there = pl.BlockSpec((1, BLOCK, width), lambda s, i, *_: (s, i, 0))
    flops = 6 * seqs * rows * (width * width + 2 * width * hidden)
    return pl.pallas_call(
        middle_kernel,
        out_shape=(
            jax.ShapeDtypeStruct((slots, rows, width), bf16),
            jax.ShapeDtypeStruct((seqs, rows, width), f32),
            jax.ShapeDtypeStruct((seqs, rows, width), bf16),
            jax.ShapeDtypeStruct(weights.shape, bf16),
            jax.ShapeDtypeStruct((8, width), f32),
            jax.ShapeDtypeStruct((1, hidden), f32),
            jax.ShapeDtypeStruct((seqs, 8, 128), f32),
        ),
        grid_spec=pltpu.PrefetchScalarGridSpec(
            num_scalar_prefetch=3,
            grid=(seqs, rows // BLOCK),
            in_specs=[
                here,
                here,
                pl.BlockSpec((1, BLOCK, width), lambda s, i, lens, a, b: (a[s], inside(s, i, lens), 0)),
                whole(weights.shape),
                whole(vectors.shape),
                whole(bias_up.shape),
            ],
            out_specs=[
                pl.BlockSpec((1, BLOCK, width), lambda s, i, lens, a, b: (b[s], i, 0)),
                there,
                there,
                pl.BlockSpec(memory_space=pl.ANY),
                whole((8, width)),
                whole((1, hidden)),
                pl.BlockSpec((1, 8, 128), lambda s, i, *_: (s, 0, 0)),
            ],
            scratch_shapes=[
                pltpu.VMEM(weights.shape, f32),
                pltpu.VMEM((BLOCK, hidden), bf16),
                pltpu.VMEM((BLOCK, hidden), f32),
                pltpu.VMEM((8, width), f32),
                pltpu.VMEM((2, width, width), bf16),
                pltpu.SemaphoreType.DMA((2,)),
            ],
        ),
        compiler_params=pltpu.CompilerParams(vmem_limit_bytes=60 << 20),
        cost_estimate=pl.CostEstimate(flops=flops, transcendentals=seqs * rows * hidden, bytes_accessed=60_000_000),
        name="middle",
    )(lengths, in_slot, out_slot, tokens, context, cots, weights, vectors, bias_up)


def backward_kernel(axes, seqs, parts, plan, x_ref, qkv_in, ctx_ref, gctx_ref, probs_ref, gres_ref, w_ref, *refs):
    if axes is None:
        gin_ref, dw_ref, dvec_ref = refs[:3]
        mixed, acc_w, stage, copy_sems = refs[3:]
    else:
        grad_ref, result_ref, gin_ref, dw_ref, dvec_ref, sum_ref, arrived_ref = refs[:7]
        mixed, acc_w, stage, copy_sems = refs[7:11]
        place = Place(axes)
        bufs = {parts[0][2]: refs[11:16]}
        scatter = Scatter(place, parts, [grad_ref], [sum_ref], bufs, *refs[16:19])
        exchange = Exchange(place, result_ref, arrived_ref, PIECES, *refs[19:22])
    seq, pair = pl.program_id(0), pl.program_id(1)
    time = seq * PAIRS + pair
    steps = seqs * PAIRS
    count, width = x_ref.shape[1], x_ref.shape[2]
    lane = lax.broadcasted_iota(jnp.int32, (1, PAIR), 1)

    if axes is not None:

        @pl.when(time == 0)
        def _():
            meet(place, place.friends(result_ref.shape[0]))

        run_steps(scatter, exchange, plan, time, steps)

    @pl.when(time == 0)
    def _():
        acc_w[...] = jnp.zeros_like(acc_w)
        dvec_ref[...] = jnp.zeros_like(dvec_ref)

    key = qkv_in[0, 1, 0]
    value = qkv_in[0, 2, 0]
    g_key, g_value = [0.0, 0.0], [0.0, 0.0]
    for start in range(0, count, ROWS):
        rows = slice(start, start + ROWS)
        query = qkv_in[0, 0, 0, rows, :]
        grad = gctx_ref[0, rows, :]
        agree = grad.astype(f32) * ctx_ref[0, rows, :].astype(f32)
        query_t, grad_t = query.T, grad.T
        g_query = jnp.zeros((ROWS, PAIR), f32)
        for head in range(2):
            mine = (lane < HEAD_DIM) if head == 0 else (lane >= HEAD_DIM)
            only = lambda values: jnp.where(mine, values, jnp.zeros_like(values))
            lanes = slice(head * HEAD_DIM, (head + 1) * HEAD_DIM)
            delta = jnp.sum(only(agree), axis=1, keepdims=True)
            probs = probs_ref[0, 0, head, rows, :]
            g_probs = nt(only(grad), value)
            g_scores = (probs.astype(f32) * (g_probs - delta)).astype(bf16)
            g_query = g_query + nn(g_scores, only(key))
            g_key[head] = g_key[head] + nn(query_t[lanes], g_scores)
            g_value[head] = g_value[head] + nn(grad_t[lanes], probs)
        mixed[pair, rows, :] = (g_query * (1.0 / math.sqrt(HEAD_DIM))).astype(bf16)
    mixed[PAIRS + pair] = jnp.concatenate(g_key, axis=0).T.astype(bf16)
    mixed[2 * PAIRS + pair] = jnp.concatenate(g_value, axis=0).T.astype(bf16)

    @pl.when(pair == PAIRS - 1)
    def _():
        @pl.loop(0, count // BLOCK)
        def _(index):
            rows = pl.ds(pl.multiple_of(index * BLOCK, BLOCK), BLOCK)
            tokens = x_ref[0, rows, :]
            g_in = gres_ref[0, rows, :]
            for part in range(3):
                cols = slice(part * width, (part + 1) * width)
                piece = jnp.concatenate([mixed[part * PAIRS + head, rows, :] for head in range(PAIRS)], axis=1)
                g_in = g_in + nt(piece, w_ref[:, cols])
                acc_w[:, cols] += tn(tokens, piece)
                if part != 1:
                    dvec_ref[part // 2 : part // 2 + 1, :] += jnp.sum(piece.astype(f32), axis=0, keepdims=True)
            gin_ref[0, rows, :] = g_in.astype(bf16)

    @pl.when(time == steps - 1)
    def _():
        copies = []
        for part in range(3):
            cols = slice(part * width, (part + 1) * width)
            slot = part % 2
            if part >= 2:
                copies[part - 2].wait()
            stage[slot] = acc_w[:, cols].astype(bf16)
            copies.append(pltpu.make_async_copy(stage.at[slot], dw_ref.at[:, cols], copy_sems.at[slot]))
            copies[-1].start()
        copies[-2].wait()
        copies[-1].wait()
        if axes is not None:
            run_rest(scatter, exchange, plan, steps)


def attention_backward(axes, tokens, qkv, context, g_context, probs, g_res1, w_qkv, dw_rest, results):
    seqs, rows, width = tokens.shape
    pair_cols = pl.BlockSpec((1, rows, PAIR), lambda s, p: (s, 0, p))
    seq_rows = pl.BlockSpec((1, rows, width), lambda s, p: (s, 0, 0))
    in_specs = [
        seq_rows,
        pl.BlockSpec((1, 3, 1, rows, PAIR), lambda s, p: (s, 0, p, 0, 0)),
        pair_cols,
        pair_cols,
        pl.BlockSpec((1, 1, 2, rows, rows), lambda s, p: (s, p, 0, 0, 0)),
        seq_rows,
        whole(w_qkv.shape),
    ]
    out_shape = [
        jax.ShapeDtypeStruct((seqs, rows, width), bf16),
        jax.ShapeDtypeStruct(w_qkv.shape, bf16),
        jax.ShapeDtypeStruct((8, width), f32),
    ]
    out_specs = [seq_rows, ANY, whole((8, width))]
    scratch = [
        pltpu.VMEM((3 * PAIRS, rows, PAIR), bf16),
        pltpu.VMEM(w_qkv.shape, f32),
        pltpu.VMEM((2, width, width), bf16),
        sems(2),
    ]
    extra, parts, plan, talk = [], [], [], {}
    if axes is not None:
        sizes = tuple(size for _, _, size in axes)
        order = (1, 0, 2)
        grads = dw_rest.reshape(sizes + (-1, dw_rest.shape[1]))
        block = grads.shape[4:]
        parts = [(0, pl.ds(start, width), order, start // width) for start in range(0, block[1], width)]
        plan = [
            [max(0, place - 2)] + [2 * stage - 1 + max(0, place - 2) for stage in range(1, 5)] for place in range(len(parts))
        ]
        extra = [grads, results]
        in_specs += [ANY, ANY]
        out_shape += [jax.ShapeDtypeStruct(block, f32), jax.ShapeDtypeStruct(results.shape, bf16)]
        out_specs += [whole(block), ANY]
        friends = results.shape[0] - 1
        scratch += scatter_buffers(axes, order, len(parts), len(parts), (block[0], width), bf16)
        scratch += scatter_sems(axes, len(parts)) + exchange_sems(friends)
        talk = {"collective_id": 4, "has_side_effects": True}
    return pl.pallas_call(
        functools.partial(backward_kernel, axes, seqs, parts, plan),
        out_shape=tuple(out_shape),
        grid_spec=pltpu.PrefetchScalarGridSpec(
            num_scalar_prefetch=0,
            grid=(seqs, PAIRS),
            in_specs=in_specs,
            out_specs=tuple(out_specs),
            scratch_shapes=scratch,
        ),
        compiler_params=pltpu.CompilerParams(vmem_limit_bytes=62 << 20, **talk),
        cost_estimate=pl.CostEstimate(flops=120_000_000_000, transcendentals=1, bytes_accessed=100_000_000),
        name="attention_backward",
    )(tokens, qkv.reshape(seqs, 3, PAIRS, rows, PAIR), context, g_context, probs, g_res1, w_qkv, *extra)


def gather_kernel(axes, parts, count, *refs):
    place = Place(axes)
    gather = Gather(place, parts, refs[:count], refs[count : 2 * count], *refs[2 * count :])
    meet(place)
    gather.start()
    for stage in range(place.core + 1):
        if stage == 1:
            gather.local()
        for part in range(len(parts)):
            gather.advance(part, stage)
    for part in range(len(parts)):
        gather.finish(part)


def gather_blocks(axes, parts, shards):
    sizes = tuple(size for _, _, size in axes)
    return pl.pallas_call(
        functools.partial(gather_kernel, axes, parts, len(shards)),
        out_shape=tuple(jax.ShapeDtypeStruct(sizes + shard.shape, shard.dtype) for shard in shards),
        in_specs=[ANY] * len(shards),
        out_specs=tuple([ANY] * len(shards)),
        scratch_shapes=gather_sems(axes, parts, len(shards)),
        compiler_params=pltpu.CompilerParams(collective_id=1, has_side_effects=True),
        name="gather_blocks",
    )(*shards)


def scatter_kernel(axes, parts, orders, *refs):
    grad_ref, small_ref, note_ref, out_ref, out_small, notes_ref = refs[:6]
    place = Place(axes)
    member = place.at["fsdp"]
    friends = place.friends(notes_ref.shape[0])
    bufs = {order: refs[6 + 5 * i : 11 + 5 * i] for i, order in enumerate(orders + (None,))}
    rest = refs[6 + 5 * (len(orders) + 1) :]
    scatter = Scatter(place, parts, [grad_ref, small_ref], [out_ref, out_small], bufs, *rest[:3])
    meet(place, friends)
    told = [
        push(note_ref, notes_ref.at[member], rest[3].at[step], rest[4].at[step], (place.at["dp"], friend))
        for step, friend in enumerate(friends)
    ]
    for copy in told:
        copy.start()
    notes_ref[member] = note_ref[...]
    for stage in range(place.core + 2):
        for part in range(len(parts)):
            scatter.advance(part, stage)
    for copy in told:
        copy.wait()
    for part in range(len(parts)):
        scatter.finish(part)


def scatter_sums(axes, grad, small, note, shards):
    sizes = tuple(size for _, _, size in axes)
    grad = grad.reshape(sizes + (-1, grad.shape[1]))
    small = small.reshape(sizes + (-1, small.shape[1]))
    block = grad.shape[4:]
    orders = ((2, 1, 0), (1, 2, 0))
    cut = block[1] // 6
    parts = [(0, pl.ds(place * cut, cut), orders[place % 2], place // 2) for place in range(6)]
    parts.insert(0, (1, None, orders[0], 0))
    bufs = [buf for order in orders for buf in scatter_buffers(axes, order, 3, 3, (block[0], cut), bf16)]
    bufs += scatter_buffers(axes, orders[0], 1, 1, small.shape[4:], f32)
    return pl.pallas_call(
        functools.partial(scatter_kernel, axes, parts, orders),
        out_shape=(
            jax.ShapeDtypeStruct(block, f32),
            jax.ShapeDtypeStruct(small.shape[4:], f32),
            jax.ShapeDtypeStruct((shards,) + note.shape, f32),
        ),
        in_specs=[ANY, ANY, VMEM],
        out_specs=(VMEM, VMEM, VMEM),
        scratch_shapes=bufs + scatter_sems(axes, len(parts)) + [sems(shards - 1), sems(shards - 1)],
        compiler_params=pltpu.CompilerParams(collective_id=2, has_side_effects=True, vmem_limit_bytes=56 << 20),
        name="scatter_sums",
    )(grad, small, note)


def body(
    tokens, lengths, deal_order, qkv_weight, query_bias, value_bias, out_weight, out_bias, attn_gain, attn_shift,
    up_weight, up_bias, down_weight, down_bias, ffn_gain, ffn_shift, cotangent,
):
    shards = lax.axis_size("fsdp")
    axes = mesh_axes(lax.axis_size("dp"), shards)
    devices = lax.axis_size("dp") * shards
    seqs, rows, width = tokens.shape
    hidden = up_weight.shape[1]
    chunks = hidden // width
    per = width // devices
    column = shards * seqs
    base = lax.axis_index("dp") * column
    member = lax.axis_index("fsdp")
    order = lax.dynamic_slice_in_dim(deal_order, base, column) - base
    mine = member * seqs
    own_lengths = lax.dynamic_slice_in_dim(lengths, base + mine, seqs)
    target = lax.dynamic_slice_in_dim(order, mine, seqs) // seqs
    dealt_here = mine + jnp.arange(seqs, dtype=jnp.int32)
    matches = order[None, :] == dealt_here[:, None]
    source = jnp.sum(jnp.where(matches, jnp.arange(column, dtype=jnp.int32)[None, :], 0), axis=1)
    peers = jnp.arange(shards, dtype=jnp.int32)

    up_mixed = up_weight.reshape(per, width, chunks).transpose(0, 2, 1).reshape(per, hidden)
    rest = jnp.concatenate([out_weight, up_mixed, down_weight.reshape(per, hidden)], axis=1)
    outgoing = cotangent[0][None]
    for place in range(1, seqs):
        outgoing = jnp.where((source[place] // seqs == peers)[:, None, None], cotangent[place][None], outgoing)
    small = jnp.concatenate(
        [query_bias, value_bias, out_bias, attn_gain, attn_shift, down_bias, ffn_gain, ffn_shift, up_bias]
    )
    small = jnp.pad(small, (0, 8 * 128 - small.shape[0])).reshape(8, 128)
    if axes is None:
        w_qkv = lax.all_gather(qkv_weight, BOTH, axis=0, tiled=True)
        small = lax.all_gather(small, BOTH, axis=0, tiled=False)
    else:
        cut = qkv_weight.shape[1] // 6
        orders = ((0, 2, 1), (0, 2, 1), (1, 0, 2))
        parts = [(1, slice(None), orders[0])] + [(0, pl.ds(i * cut, cut), orders[i % 3]) for i in range(6)]
        w_qkv, small = gather_blocks(axes, parts, [qkv_weight, small])
        w_qkv = w_qkv.reshape(width, -1)
    small = small.reshape(devices, -1)
    vectors = small[:, : 8 * per].reshape(devices, 8, per).transpose(1, 0, 2).reshape(8, width)
    bias_up = small[:, 8 * per : 8 * per + chunks * per].reshape(width, chunks).T.reshape(1, hidden)

    if axes is None:
        weights = lax.all_gather(rest, BOTH, axis=0, tiled=True)
        cots = lax.all_to_all(outgoing, "fsdp", split_axis=0, concat_axis=0, tiled=True)
        qkv, context, probs = attention_forward(axes, own_lengths, tokens, w_qkv, vectors, rest, outgoing)
    else:
        qkv, context, probs, weights, cots = attention_forward(
            axes, own_lengths, tokens, w_qkv, vectors, rest, outgoing
        )
        weights = weights.reshape(width, -1)
    results, g_res1, g_context, dw_rest, dvec, dbu, rms = middle(
        own_lengths, target, target, tokens, context, cots, weights, vectors, bias_up
    )
    outs = attention_backward(axes, tokens, qkv, context, g_context, probs, g_res1, w_qkv, dw_rest, results)
    input_grad, dw_qkv, dqv = outs[:3]
    if axes is None:
        arrived = lax.all_to_all(results, "fsdp", split_axis=0, concat_axis=0, tiled=True)
    else:
        rest_grad, arrived = outs[3:]
    layer_out = jnp.stack(
        [lax.dynamic_index_in_dim(arrived, source[t] // seqs, 0, keepdims=False) for t in range(seqs)]
    )

    dvec = (dvec + dqv).reshape(8, devices, per).transpose(1, 0, 2).reshape(devices, 8 * per)
    dbu = dbu.reshape(chunks, devices, per).transpose(1, 2, 0).reshape(devices, chunks * per)
    packed = jnp.pad(jnp.concatenate([dvec, dbu], axis=1), ((0, 0), (0, 8 * 128 - (8 + chunks) * per)))
    rms = rms.reshape(seqs * 8, 128)
    if axes is None:
        scatter = lambda whole: lax.psum_scatter(whole, BOTH, scatter_dimension=0, tiled=True)
        qkvw_grad, rest_grad = scatter(dw_qkv).astype(f32), scatter(dw_rest).astype(f32)
        packed = scatter(packed)
        rms = lax.all_gather(rms, "fsdp", axis=0, tiled=False)
    else:
        qkvw_grad, packed, rms = scatter_sums(axes, dw_qkv, packed.reshape(devices * 8, 128), rms, shards)
    packed = packed.reshape(-1)
    vector = [packed[place * per : (place + 1) * per] for place in range(8)]
    rms = rms.reshape(column, 8, 128)[:, :3, 0]
    branch_rms = jnp.sum(jnp.where((source[:, None] == jnp.arange(column))[:, :, None], rms[None], 0.0), axis=1)
    outw_grad = rest_grad[:, :width]
    upw_grad = rest_grad[:, width : width + hidden].reshape(per, chunks, width).transpose(0, 2, 1).reshape(per, hidden)
    downw_grad = rest_grad[:, width + hidden :].reshape(per * chunks, width)
    return (
        layer_out, input_grad, qkvw_grad, vector[0], vector[1], outw_grad, vector[2], vector[3], vector[4], upw_grad,
        packed[8 * per : 8 * per + chunks * per], downw_grad, vector[5], vector[6], vector[7], branch_rms,
    )


def solution(mesh):
    rows3, rows2, rows1 = P(BOTH, None, None), P(BOTH, None), P(BOTH)
    in_specs = (
        rows3, P(), P(), rows2, rows1, rows1, rows2, rows1, rows1, rows1, rows2, rows1, rows2, rows1, rows1, rows1, rows3,
    )
    out_specs = (
        rows3, rows3, rows2, rows1, rows1, rows2, rows1, rows1, rows1, rows2, rows1, rows2, rows1, rows1, rows1, rows2,
    )
    return jax.shard_map(body, mesh=mesh, in_specs=in_specs, out_specs=out_specs, check_vma=False)
```

```python
import functools
import math

import jax
import jax.numpy as jnp
from jax import lax
from jax.experimental import pallas as pl
from jax.experimental.pallas import tpu as pltpu
from jax.sharding import PartitionSpec as P

HEADS = 12
HEAD_DIM = 64
PAIR = 2 * HEAD_DIM
PAIRS = HEADS // 2
BLOCK = 256
ROWS = 512
PIECES = 8
ALL = slice(None)
EVERY = (ALL, ALL)

f32 = jnp.float32
bf16 = jnp.bfloat16
norm_eps = 1e-05
masked_fill = -1e30
BOTH = ("dp", "fsdp")
MESH = pl.DeviceIdType.MESH


def nn(left, right):
    return lax.dot_general(left, right, (((1,), (0,)), ((), ())), preferred_element_type=f32)


def nt(left, right):
    return lax.dot_general(left, right, (((1,), (1,)), ((), ())), preferred_element_type=f32)


def tn(left, right):
    return lax.dot_general(left, right, (((0,), (0,)), ((), ())), preferred_element_type=f32)


def block_count(length):
    return (length + (BLOCK - 1)) // BLOCK


def whole(shape):
    return pl.BlockSpec(shape, lambda *_: (0,) * len(shape), pipeline_mode=pl.Buffered(1))


def sems(*shape):
    return pltpu.SemaphoreType.DMA(shape)


def tiles(shape, block):
    return [
        (pl.ds(top, block[0]), pl.ds(left, block[1]))
        for top in range(0, shape[0], block[0])
        for left in range(0, shape[1], block[1])
    ]


ANY = pl.BlockSpec(memory_space=pl.ANY)
VMEM = pl.BlockSpec(memory_space=pltpu.VMEM)


def mesh_axes(dp, fsdp):
    if (dp, fsdp) == (8, 4):
        return (("dp", 2, 4), ("dp", 1, 2), ("fsdp", 2, 2), ("fsdp", 1, 2))
    return None


class Place:
    def __init__(self, axes):
        self.axes = axes
        self.core = len(axes) - 1
        self.at = {name: lax.axis_index(name) for name in BOTH}
        self.own = [lax.rem(self.at[name] // stride, size) for name, stride, size in axes]

    def shifted(self, dim, step):
        size = self.axes[dim][2]
        return lax.rem(self.own[dim] + step + size, size)

    def device(self, dim, step):
        name, stride, _ = self.axes[dim]
        moved = self.at[name] + (self.shifted(dim, step) - self.own[dim]) * stride
        return tuple(moved if name == axis else self.at[axis] for axis in BOTH)

    def steps(self, dim):
        return range(1, self.axes[dim][2])

    def friends(self, count):
        member = self.at["fsdp"]
        return [lax.rem(member + step, count) for step in range(1, count)]


def meet(place, friends=()):
    barrier = pltpu.get_barrier_semaphore()
    peers = [place.device(dim, step) for dim in range(len(place.axes)) for step in place.steps(dim)]
    peers += [(place.at["dp"], friend) for friend in friends]
    for peer in peers:
        pl.semaphore_signal(barrier, inc=1, device_id=peer, device_id_type=MESH)
    pl.semaphore_wait(barrier, len(peers))


def push(source, target, send, recv, device):
    return pltpu.make_async_remote_copy(source, target, send, recv, device_id=device, device_id_type=MESH)


class Exchange:
    def __init__(self, place, mine, theirs, pieces, send, recv, local):
        self.place, self.mine, self.theirs, self.pieces = place, mine, theirs, pieces
        self.send, self.recv, self.local = send, recv, local

    def copies(self, piece):
        member = self.place.at["fsdp"]
        height = self.mine.shape[1] // self.pieces
        rows = pl.ds(piece * height, height)
        made = [
            push(
                self.mine.at[friend, rows],
                self.theirs.at[member, rows],
                self.send.at[step, piece],
                self.recv.at[step, piece],
                (self.place.at["dp"], friend),
            )
            for step, friend in enumerate(self.place.friends(self.mine.shape[0]))
        ]
        return made + [pltpu.make_async_copy(self.mine.at[member, rows], self.theirs.at[member, rows], self.local.at[piece])]

    def start(self, piece):
        for copy in self.copies(piece):
            copy.start()

    def fill(self, source, choice):
        for slot in range(self.mine.shape[0]):
            self.mine[slot] = source[choice[slot]]

    def wait(self):
        for piece in range(self.pieces):
            for copy in self.copies(piece):
                copy.wait()


def exchange_sems(friends):
    return [sems(friends, PIECES), sems(friends, PIECES), sems(PIECES)]


class Gather:
    def __init__(self, place, parts, shards, outs, send, recv, core_send, core_recv, local):
        self.place, self.parts, self.shards, self.outs = place, parts, shards, outs
        self.sems = send, recv
        self.core_sems = core_send, core_recv
        self.mine = [
            pltpu.make_async_copy(shard, out.at[tuple(place.own)], local.at[i])
            for i, (shard, out) in enumerate(zip(shards, outs))
        ]

    def start(self):
        for copy in self.mine:
            copy.start()

    def local(self):
        for copy in self.mine:
            copy.wait()

    def view(self, number, spot):
        array, cut, _ = self.parts[number]
        return self.outs[array].at[tuple(spot) + cut]

    def shard(self, number):
        array, cut, _ = self.parts[number]
        return self.shards[array].at[cut]

    def known(self, number, stage):
        order = self.parts[number][2]
        return [slice(None) if dim in order[:stage] else own for dim, own in enumerate(self.place.own)]

    def link(self, number, stage):
        order = self.parts[number][2]
        spot = self.known(number, stage)
        source = self.view(number, spot) if stage else self.shard(number)
        first = sum(self.place.axes[dim][2] - 1 for dim in order[:stage])
        send, recv = self.sems
        return [
            push(
                source,
                self.view(number, spot),
                send.at[number, first + step - 1],
                recv.at[number, first + step - 1],
                self.place.device(order[stage], step),
            )
            for step in self.place.steps(order[stage])
        ]

    def across(self, number, stage):
        order = self.parts[number][2]
        core_send, core_recv = self.core_sems
        peer = self.place.device(self.place.core, 1)
        if stage == 0:
            spot = self.known(number, 0)
            return [push(self.shard(number), self.view(number, spot), core_send.at[number, 0], core_recv.at[number, 0], peer)]
        first = sum(self.place.axes[dim][2] - 1 for dim in order[: stage - 1])
        dim = order[stage - 1]
        copies = []
        for step in self.place.steps(dim):
            spot = self.known(number, stage - 1)
            spot[dim] = self.place.shifted(dim, -step)
            view, piece = self.view(number, spot), first + step
            copies.append(push(view, view, core_send.at[number, piece], core_recv.at[number, piece], peer))
        return copies

    def advance(self, number, stage):
        if stage:
            for copy in self.link(number, stage - 1):
                copy.wait_recv()
        if stage < self.place.core:
            for copy in self.link(number, stage):
                copy.start()
        for copy in self.across(number, stage):
            copy.start()

    def finish(self, number):
        for stage in range(self.place.core + 1):
            if stage < self.place.core:
                for copy in self.link(number, stage):
                    copy.wait_send()
            for copy in self.across(number, stage):
                copy.wait()


def gather_sems(axes, parts, count):
    hops = sum(size - 1 for _, _, size in axes[:-1])
    shapes = (len(parts), hops), (len(parts), hops), (len(parts), hops + 1), (len(parts), hops + 1), (count,)
    return [sems(*shape) for shape in shapes]


class Scatter:
    def __init__(self, place, parts, grads, outs, bufs, send, recv, local):
        self.place, self.parts, self.grads, self.outs = place, parts, grads, outs
        self.bufs = bufs
        self.send, self.recv, self.local = send, recv, local

    def refs(self, number):
        _, _, order, slot = self.parts[number]
        own, *came = self.bufs[order if self.parts[number][1] is not None else None]
        held = own.shape[0]
        return [own.at[slot % held]] + [buf.at[slot] for buf in came]

    def first(self, number, stage):
        order = self.parts[number][2]
        return 1 + sum(self.place.axes[dim][2] - 1 for dim in order[:stage])

    def block(self, number, core):
        array, cut, _, _ = self.parts[number]
        lead = (slice(None),) * self.place.core + (core,)
        return self.grads[array].at[lead + (EVERY if cut is None else cut)]

    def across(self, number):
        place = self.place
        return push(
            self.block(number, place.shifted(place.core, 1)),
            self.refs(number)[1],
            self.send.at[number, 0],
            self.recv.at[number, 0],
            place.device(place.core, 1),
        )

    def own(self, number):
        return pltpu.make_async_copy(
            self.block(number, self.place.own[self.place.core]), self.refs(number)[0], self.local.at[number]
        )

    def spot(self, number, stage, at):
        order = self.parts[number][2]
        dims = [slice(None)] * self.place.core
        for dim in order[:stage]:
            dims[dim] = self.place.own[dim]
        if at is not None:
            dims[order[stage]] = at
        return dims

    def link(self, number, stage, step):
        dim = self.parts[number][2][stage]
        place, refs = self.place, self.refs(number)
        piece = self.first(number, stage) + step - 1
        return push(
            refs[0].at[tuple(self.spot(number, stage, place.shifted(dim, step)))],
            refs[2 + stage].at[step - 1],
            self.send.at[number, piece],
            self.recv.at[number, piece],
            place.device(dim, step),
        )

    def add(self, number, spot, extras):
        acc = self.refs(number)[0]
        free = [dim for dim, index in enumerate(spot) if isinstance(index, slice)]
        sizes = [self.place.axes[dim][2] for dim in free]
        total = math.prod(sizes)

        def one(place, carry):
            index, where = list(spot), []
            rest = place
            for dim, size in zip(reversed(free), reversed(sizes)):
                index[dim] = lax.rem(rest, size)
                where.insert(0, index[dim])
                rest = rest // size
            index = tuple(index)
            value = acc[index].astype(f32)
            for extra in extras:
                value = value + extra[tuple(where)].astype(f32)
            acc[index] = value.astype(acc.dtype)
            return carry

        if total == 1:
            one(0, 0)
        else:
            lax.fori_loop(0, total, one, 0)

    def advance(self, number, stage):
        array, cut, order, _ = self.parts[number]
        place, refs = self.place, self.refs(number)
        if stage == 0:
            self.across(number).start()
            self.own(number).start()
            return
        if stage == 1:
            self.own(number).wait()
            self.across(number).wait_recv()
            came = [refs[1]]
        else:
            dim = order[stage - 2]
            for step in place.steps(dim):
                self.link(number, stage - 2, step).wait_recv()
            came = [refs[stage].at[step - 1] for step in place.steps(dim)]
        if stage <= place.core:
            dim = order[stage - 1]
            for step in list(place.steps(dim)) + [0]:
                at = place.shifted(dim, step)
                spot = self.spot(number, stage - 1, at)
                where = self.within(number, stage - 1, at)
                self.add(number, spot, [extra.at[where] for extra in came])
                if step:
                    self.link(number, stage - 1, step).start()
        else:
            total = refs[0][tuple(place.own[:-1])].astype(f32)
            for extra in came:
                total = total + extra[...].astype(f32)
            self.outs[array][EVERY if cut is None else cut] = total

    def within(self, number, stage, at):
        order = self.parts[number][2]
        rest = [dim for dim in range(self.place.core) if dim not in order[:stage]]
        return tuple(at if dim == order[stage] else slice(None) for dim in rest)

    def finish(self, number):
        self.across(number).wait_send()
        order = self.parts[number][2]
        for stage, dim in enumerate(order):
            for step in self.place.steps(dim):
                self.link(number, stage, step).wait_send()


def scatter_buffers(axes, order, tiles, held, block, dtype):
    sizes = [size for _, _, size in axes[:-1]]
    leads = [(held,) + tuple(sizes), (tiles,) + tuple(sizes)]
    left = list(range(len(sizes)))
    for dim in order:
        left.remove(dim)
        leads.append((tiles, sizes[dim] - 1) + tuple(sizes[other] for other in left))
    return [pltpu.VMEM(lead + tuple(block), dtype) for lead in leads]


def scatter_sems(axes, count):
    hops = 1 + sum(size - 1 for _, _, size in axes[:-1])
    return [sems(count, hops), sems(count, hops), sems(count)]


def run_steps(mover, exchange, plan, dealt, time, steps, first=0):
    for step in range(first, steps):
        todo = [(part, stage) for part, row in plan.items() for stage, at in enumerate(row) if at == step]
        pieces = [piece for piece, at in enumerate(dealt) if at == step]

        @pl.when(time == step)
        def _(todo=todo, pieces=pieces):
            for part, stage in todo:
                mover.advance(part, stage)
            for piece in pieces:
                exchange.start(piece)


def run_rest(mover, exchange, plan, steps):
    for part, row in plan.items():
        for stage, at in enumerate(row):
            if at >= steps:
                mover.advance(part, stage)
    for part in plan:
        mover.finish(part)
    exchange.wait()


def forward_kernel(axes, seqs, parts, early, plan, dealt, len_ref, choice_ref, x_ref, *refs):
    seq, pair = pl.program_id(0), pl.program_id(1)
    time = seq * PAIRS + pair
    steps = seqs * PAIRS
    length = len_ref[seq]
    count, width = x_ref.shape[1], x_ref.shape[2]
    lane = lax.broadcasted_iota(jnp.int32, (1, PAIR), 1)
    if axes is None:
        w_ref, vec_ref, qkv_ref, ctx_ref, probs_ref = refs
    else:
        shards, cot_ref, qkv_ref, ctx_ref, probs_ref = refs[:5], refs[5], refs[6], refs[7], refs[8]
        gathered, cots_ref, vec_ref = refs[9:14], refs[14], refs[15]
        w_ref, raw_ref, small_ref, held_ref, going_ref, copy_sems = refs[16:22]
        place = Place(axes)
        gather = Gather(place, parts, shards, gathered, *refs[22:27])
        exchange = Exchange(place, going_ref, cots_ref, PIECES, *refs[27:30])

        @pl.when(time == 0)
        def _():
            now = [
                pltpu.make_async_copy(cot_ref, held_ref, copy_sems.at[0]),
                pltpu.make_async_copy(gathered[0], raw_ref, copy_sems.at[1]),
                pltpu.make_async_copy(gathered[1], small_ref, copy_sems.at[2]),
            ]
            now[0].start()
            meet(place, place.friends(cots_ref.shape[0]))
            gather.start()
            for part in list(early) + list(plan):
                gather.advance(part, 0)
            now[0].wait()
            exchange.fill(held_ref, choice_ref)
            gather.local()
            for stage in range(1, place.core + 1):
                for part in early:
                    gather.advance(part, stage)
                for part, row in plan.items():
                    if stage == 1 and row[1] == 0:
                        gather.advance(part, 1)
                for piece, at in enumerate(dealt):
                    if stage == 2 and at == 0:
                        exchange.start(piece)
            for part in early:
                gather.finish(part)
            for copy in now[1:]:
                copy.start()
            for copy in now[1:]:
                copy.wait()
            depth, across, along, _ = raw_ref.shape[:4]
            height = 2 * raw_ref.shape[4]

            def one(block, total):
                spot = block // (across * along), lax.rem(block // along, across), lax.rem(block, along)
                both = jnp.concatenate([raw_ref[spot + (half,)].astype(f32) for half in range(2)], axis=0)
                w_ref[pl.ds(pl.multiple_of(block * height, height), height), :] = both.astype(bf16)
                return total + small_ref[spot + (0,)].astype(f32) + small_ref[spot + (1,)].astype(f32)

            vec_ref[...] = lax.fori_loop(0, depth * across * along, one, jnp.zeros((16, width), f32))

        run_steps(gather, exchange, plan, dealt, time, steps, 1)

    @pl.when(pair == 0)
    def _():
        tokens = x_ref[0]
        step = 2 * PAIR
        for start in range(0, 3 * width, step):
            part = start // width
            projected = nn(tokens, w_ref[:, start : start + step])
            if part != 1:
                cols = slice(start - part * width, start - part * width + step)
                projected = projected + vec_ref[part // 2 : part // 2 + 1, cols]
            projected = projected.astype(bf16)
            if part == 0:
                projected = projected * jnp.asarray(1.0 / math.sqrt(HEAD_DIM), bf16)
            for half in range(2):
                qkv_ref[0, start // PAIR + half] = projected[:, half * PAIR : (half + 1) * PAIR]

    key = qkv_ref[0, PAIRS + pair]
    value = qkv_ref[0, 2 * PAIRS + pair]
    unusable = lax.broadcasted_iota(jnp.int32, (count, 1), 0) >= length
    mask = jnp.where(unusable, masked_fill, 0.0).astype(bf16)
    keys = [jnp.where(lane == spare, mask, key) for spare in (PAIR - 1, 0)]
    for start in range(0, count, ROWS):
        rows = slice(start, start + ROWS)
        query = qkv_ref[0, pair, rows, :]
        outs = []
        for head in range(2):
            mine = (lane < HEAD_DIM) if head == 0 else (lane >= HEAD_DIM)
            spare = jnp.where(lane == (PAIR - 1 if head == 0 else 0), 1.0, 0.0).astype(bf16)
            scores = nt(jnp.where(mine, query, spare), keys[head])
            top = jnp.max(scores, axis=1, keepdims=True)
            powers = jnp.exp(scores - top)
            total = jnp.sum(powers, axis=1, keepdims=True)
            probs = (powers * (1.0 / total)).astype(bf16)
            probs_ref[0, 0, head, rows, :] = probs
            outs.append(nn(probs, value))
        ctx_ref[0, rows, :] = jnp.where(lane < HEAD_DIM, outs[0], outs[1]).astype(bf16)

    if axes is not None:

        @pl.when(time == steps - 1)
        def _():
            run_rest(gather, exchange, plan, steps)


def attention_forward(axes, lengths, choice, tokens, operands, cotangent, shards):
    seqs, rows, width = tokens.shape
    out_shape = [
        jax.ShapeDtypeStruct((seqs, 3 * PAIRS, rows, PAIR), bf16),
        jax.ShapeDtypeStruct((seqs, rows, width), bf16),
        jax.ShapeDtypeStruct((seqs, PAIRS, 2, rows, rows), bf16),
    ]
    in_specs = [pl.BlockSpec((1, rows, width), lambda s, p, *_: (s, 0, 0))]
    out_specs = [
        pl.BlockSpec((1, 3 * PAIRS, rows, PAIR), lambda s, p, *_: (s, 0, 0, 0)),
        pl.BlockSpec((1, rows, PAIR), lambda s, p, *_: (s, 0, p)),
        pl.BlockSpec((1, 1, 2, rows, rows), lambda s, p, *_: (s, p, 0, 0, 0)),
    ]
    scratch, parts, early, plan, dealt, talk = [], [], [], {}, [], {}
    extra = list(operands)
    if axes is None:
        in_specs += [whole(array.shape) for array in operands]
    else:
        orders = ((0, 2, 1), (0, 2, 1), (1, 0, 2))
        first, small, *later = operands
        parts.append((1, EVERY, orders[0]))
        for cut in tiles(first.shape, (first.shape[0], first.shape[1] // 6)):
            parts.append((0, cut, orders[(len(parts) - 1) % 3]))
        early = range(len(parts))
        for array, shard in enumerate(later, 2):
            parts += [(array, cut, (2, 0, 1)) for cut in tiles(shard.shape, (first.shape[0], width))]
        for place in range(len(parts) - len(early)):
            at = max(0, place - 2)
            plan[place + len(early)] = [0, at, at + (1 if place < 2 else 2), at + (3 if place < 2 else 4)]
        dealt = [max(0, piece - 1) for piece in range(PIECES)]
        extra += [cotangent]
        in_specs += [ANY] * len(extra)
        sizes = tuple(size for _, _, size in axes)
        out_shape += [jax.ShapeDtypeStruct(sizes + shard.shape, bf16) for shard in operands]
        out_shape += [jax.ShapeDtypeStruct((shards, rows, width), bf16), jax.ShapeDtypeStruct(small.shape, f32)]
        out_specs += [ANY] * (len(operands) + 1) + [whole(small.shape)]
        scratch = [
            pltpu.VMEM((width, first.shape[1]), bf16),
            pltpu.VMEM(sizes + first.shape, bf16),
            pltpu.VMEM(sizes + small.shape, bf16),
            pltpu.VMEM(cotangent.shape, bf16),
            pltpu.VMEM((shards, rows, width), bf16),
            sems(3),
        ]
        scratch += gather_sems(axes, parts, len(operands)) + exchange_sems(shards - 1)
        talk = {"collective_id": 3, "has_side_effects": True}
    return pl.pallas_call(
        functools.partial(forward_kernel, axes, seqs, parts, early, plan, dealt),
        out_shape=tuple(out_shape),
        grid_spec=pltpu.PrefetchScalarGridSpec(
            num_scalar_prefetch=2,
            grid=(seqs, PAIRS),
            in_specs=in_specs,
            out_specs=tuple(out_specs),
            scratch_shapes=scratch,
        ),
        compiler_params=pltpu.CompilerParams(vmem_limit_bytes=60 << 20, **talk),
        cost_estimate=pl.CostEstimate(flops=60_000_000_000, transcendentals=30_000_000, bytes_accessed=80_000_000),
        name="attention_forward",
    )(lengths, choice, tokens, *extra)


def normal_tail(values):
    size = jnp.abs(values)
    bell = jnp.exp(-0.5 * values * values)
    t = 1.0 / (1.0 + (0.3275911 / math.sqrt(2.0)) * size)
    poly = t * (
        0.5 * 0.254829592
        + t * (0.5 * -0.284496736 + t * (0.5 * 1.421413741 + t * (0.5 * -1.453152027 + t * (0.5 * 1.061405429))))
    )
    tail = poly * bell
    return jnp.where(values >= 0, 1.0 - tail, tail), bell


def row_mean(values):
    return jnp.mean(values, axis=-1, keepdims=True)


def middle_kernel(
    len_ref, in_slot, out_slot, x_ref, ctx_ref, cot_ref, wo_ref, wu_ref, wd_ref, vec_ref,
    out_ref, gres_ref, gctx_ref, dwo_ref, dwu_ref, dwd_ref, dvec_ref, rms_ref,
    acc_o, acc_u, acc_d, active, slope, sums, stage, sems,
):
    seq, index = pl.program_id(0), pl.program_id(1)
    first = jnp.logical_and(seq == 0, index == 0)
    final = jnp.logical_and(seq == pl.num_programs(0) - 1, index == pl.num_programs(1) - 1)
    length = len_ref[seq]
    width = x_ref.shape[2]
    chunks = wu_ref.shape[1] // width
    tile = lambda place: slice(place * width, (place + 1) * width)

    @pl.when(first)
    def _():
        acc_o[...] = jnp.zeros_like(acc_o)
        acc_u[...] = jnp.zeros_like(acc_u)
        acc_d[...] = jnp.zeros_like(acc_d)
        dvec_ref[...] = jnp.zeros_like(dvec_ref)

    @pl.when(index == 0)
    def _():
        sums[...] = jnp.zeros_like(sums)

    @pl.when(index * BLOCK >= length)
    def _():
        out_ref[...] = jnp.zeros_like(out_ref)
        gres_ref[...] = jnp.zeros_like(gres_ref)
        gctx_ref[...] = jnp.zeros_like(gctx_ref)

    @pl.when(index * BLOCK < length)
    def _():
        vec = lambda place: vec_ref[place : place + 1, :]
        bias_out, gain_a, shift_a, bias_down, gain_f, shift_f = (vec(place) for place in range(2, 8))
        valid = (lax.broadcasted_iota(jnp.int32, (BLOCK, 1), 0) + index * BLOCK < length).astype(f32)
        tokens = x_ref[0].astype(f32)
        context = ctx_ref[0]
        branch_a = nn(context, wo_ref[...]) + bias_out
        mixed = tokens + branch_a
        center = mixed - row_mean(mixed)
        scale_a = lax.rsqrt(row_mean(center * center) + norm_eps)
        hat_a = center * scale_a
        hidden = hat_a * gain_a + shift_a
        hidden_low = hidden.astype(bf16)
        branch_f = bias_down
        for chunk in range(chunks):
            cols = tile(chunk)
            gate = nn(hidden_low, wu_ref[:, cols]) + vec(8 + chunk)
            share, bell = normal_tail(gate)
            act = (gate * share).astype(bf16)
            active[:, cols] = act
            slope[:, cols] = share + gate * bell * (1.0 / math.sqrt(2.0 * math.pi))
            branch_f = branch_f + nn(act, wd_ref[cols, :])
        mixed_f = hidden + branch_f
        center = mixed_f - row_mean(mixed_f)
        scale_f = lax.rsqrt(row_mean(center * center) + norm_eps)
        hat_f = center * scale_f
        out_ref[0] = ((hat_f * gain_f + shift_f) * valid).astype(bf16)
        g_result = cot_ref[0].astype(f32) * valid
        g_hat = g_result * gain_f
        g_res2 = scale_f * (g_hat - row_mean(g_hat) - hat_f * row_mean(g_hat * hat_f))
        g_ffn = g_res2.astype(bf16)
        g_hidden = g_res2
        for chunk in range(chunks):
            cols = tile(chunk)
            g_gate = nt(g_ffn, wd_ref[cols, :]) * slope[:, cols]
            g_low = g_gate.astype(bf16)
            acc_d[cols, :] += tn(active[:, cols], g_ffn)
            acc_u[:, cols] += tn(hidden_low, g_low)
            dvec_ref[8 + chunk : 9 + chunk, :] += jnp.sum(g_low.astype(f32), axis=0, keepdims=True)
            g_hidden = g_hidden + nt(g_low, wu_ref[:, cols])
        g_hat = g_hidden * gain_a
        g_res1 = scale_a * (g_hat - row_mean(g_hat) - hat_a * row_mean(g_hat * hat_a))
        g_attn = g_res1.astype(bf16)
        gres_ref[0] = g_res1
        gctx_ref[0] = nt(g_attn, wo_ref[...]).astype(bf16)
        acc_o[...] += tn(context, g_attn)
        column = lambda values: jnp.sum(values, axis=0, keepdims=True)
        dvec_ref[2:3, :] += column(g_attn.astype(f32))
        dvec_ref[3:4, :] += column(g_hidden * hat_a)
        dvec_ref[4:5, :] += column(g_hidden)
        dvec_ref[5:6, :] += column(g_ffn.astype(f32))
        dvec_ref[6:7, :] += column(g_result * hat_f)
        dvec_ref[7:8, :] += column(g_result)
        sums[0:1, :] += column(tokens * tokens * valid)
        sums[1:2, :] += column(branch_a * branch_a * valid)
        sums[2:3, :] += column(branch_f * branch_f * valid)

    @pl.when(index == pl.num_programs(1) - 1)
    def _():
        mean = jnp.sum(sums[...], axis=1, keepdims=True) / (length * width).astype(f32)
        rms_ref[0] = jnp.broadcast_to(jnp.sqrt(mean), rms_ref.shape[1:])

    @pl.when(final)
    def _():
        pieces = [(acc_o, dwo_ref, EVERY)]
        pieces += [(acc_u, dwu_ref, (ALL, tile(chunk))) for chunk in range(chunks)]
        pieces += [(acc_d, dwd_ref, (tile(chunk), ALL)) for chunk in range(chunks)]
        copies = []
        for place, (acc, out, cut) in enumerate(pieces):
            slot = place % 2
            if place >= 2:
                copies[place - 2].wait()
            stage[slot] = acc[cut].astype(bf16)
            copies.append(pltpu.make_async_copy(stage.at[slot], out.at[cut], sems.at[slot]))
            copies[-1].start()
        copies[-2].wait()
        copies[-1].wait()


def middle(lengths, in_slot, out_slot, tokens, context, cots, w_out, w_up, w_down, vectors):
    seqs, rows, width = tokens.shape
    slots = cots.shape[0]
    hidden = w_up.shape[1]
    inside = lambda s, i, lens: jnp.minimum(i, block_count(lens[s]) - 1)
    here = pl.BlockSpec((1, BLOCK, width), lambda s, i, lens, a, b: (s, inside(s, i, lens), 0))
    there = pl.BlockSpec((1, BLOCK, width), lambda s, i, *_: (s, i, 0))
    flops = 6 * seqs * rows * (width * width + 2 * width * hidden)
    return pl.pallas_call(
        middle_kernel,
        out_shape=(
            jax.ShapeDtypeStruct((slots, rows, width), bf16),
            jax.ShapeDtypeStruct((seqs, rows, width), f32),
            jax.ShapeDtypeStruct((seqs, rows, width), bf16),
            jax.ShapeDtypeStruct(w_out.shape, bf16),
            jax.ShapeDtypeStruct(w_up.shape, bf16),
            jax.ShapeDtypeStruct(w_down.shape, bf16),
            jax.ShapeDtypeStruct((16, width), f32),
            jax.ShapeDtypeStruct((seqs, 8, 128), f32),
        ),
        grid_spec=pltpu.PrefetchScalarGridSpec(
            num_scalar_prefetch=3,
            grid=(seqs, rows // BLOCK),
            in_specs=[
                here,
                here,
                pl.BlockSpec((1, BLOCK, width), lambda s, i, lens, a, b: (a[s], inside(s, i, lens), 0)),
                whole(w_out.shape),
                whole(w_up.shape),
                whole(w_down.shape),
                whole(vectors.shape),
            ],
            out_specs=[
                pl.BlockSpec((1, BLOCK, width), lambda s, i, lens, a, b: (b[s], i, 0)),
                there,
                there,
                ANY,
                ANY,
                ANY,
                whole((16, width)),
                pl.BlockSpec((1, 8, 128), lambda s, i, *_: (s, 0, 0)),
            ],
            scratch_shapes=[
                pltpu.VMEM(w_out.shape, f32),
                pltpu.VMEM(w_up.shape, f32),
                pltpu.VMEM(w_down.shape, f32),
                pltpu.VMEM((BLOCK, hidden), bf16),
                pltpu.VMEM((BLOCK, hidden), f32),
                pltpu.VMEM((8, width), f32),
                pltpu.VMEM((2, width, width), bf16),
                pltpu.SemaphoreType.DMA((2,)),
            ],
        ),
        compiler_params=pltpu.CompilerParams(vmem_limit_bytes=60 << 20),
        cost_estimate=pl.CostEstimate(flops=flops, transcendentals=seqs * rows * hidden, bytes_accessed=60_000_000),
        name="middle",
    )(lengths, in_slot, out_slot, tokens, context, cots, w_out, w_up, w_down, vectors)


def backward_kernel(axes, seqs, parts, plan, dealt, x_ref, qkv_in, ctx_ref, gctx_ref, probs_ref, gres_ref, w_ref, *refs):
    if axes is None:
        gin_ref, dw_ref, dvec_ref = refs[:3]
        mixed, acc_w, stage, copy_sems = refs[3:]
    else:
        grads, result_ref, gin_ref, dw_ref, dvec_ref = refs[:3], refs[3], refs[4], refs[5], refs[6]
        summed, arrived_ref = refs[7:10], refs[10]
        mixed, acc_w, stage, copy_sems = refs[11:15]
        place = Place(axes)
        bufs = {parts[0][2]: refs[15:20]}
        scatter = Scatter(place, parts, grads, summed, bufs, *refs[20:23])
        exchange = Exchange(place, result_ref, arrived_ref, PIECES, *refs[23:26])
    seq, pair = pl.program_id(0), pl.program_id(1)
    time = seq * PAIRS + pair
    steps = seqs * PAIRS
    count, width = x_ref.shape[1], x_ref.shape[2]
    lane = lax.broadcasted_iota(jnp.int32, (1, PAIR), 1)

    if axes is not None:

        @pl.when(time == 0)
        def _():
            meet(place, place.friends(result_ref.shape[0]))

        run_steps(scatter, exchange, plan, dealt, time, steps)

    @pl.when(time == 0)
    def _():
        acc_w[...] = jnp.zeros_like(acc_w)
        dvec_ref[...] = jnp.zeros_like(dvec_ref)

    key = qkv_in[0, 1, 0]
    value = qkv_in[0, 2, 0]
    g_key, g_value = [0.0, 0.0], [0.0, 0.0]
    for start in range(0, count, ROWS):
        rows = slice(start, start + ROWS)
        query = qkv_in[0, 0, 0, rows, :]
        grad = gctx_ref[0, rows, :]
        agree = grad.astype(f32) * ctx_ref[0, rows, :].astype(f32)
        query_t, grad_t = query.T, grad.T
        g_query = jnp.zeros((ROWS, PAIR), f32)
        for head in range(2):
            mine = (lane < HEAD_DIM) if head == 0 else (lane >= HEAD_DIM)
            only = lambda values: jnp.where(mine, values, jnp.zeros_like(values))
            lanes = slice(head * HEAD_DIM, (head + 1) * HEAD_DIM)
            delta = jnp.sum(only(agree), axis=1, keepdims=True)
            probs = probs_ref[0, 0, head, rows, :]
            g_probs = nt(only(grad), value)
            g_scores = (probs.astype(f32) * (g_probs - delta)).astype(bf16)
            g_query = g_query + nn(g_scores, only(key))
            g_key[head] = g_key[head] + nn(query_t[lanes], g_scores)
            g_value[head] = g_value[head] + nn(grad_t[lanes], probs)
        mixed[pair, rows, :] = (g_query * (1.0 / math.sqrt(HEAD_DIM))).astype(bf16)
    mixed[PAIRS + pair] = jnp.concatenate(g_key, axis=0).T.astype(bf16)
    mixed[2 * PAIRS + pair] = jnp.concatenate(g_value, axis=0).T.astype(bf16)

    @pl.when(pair == PAIRS - 1)
    def _():
        @pl.loop(0, count // BLOCK)
        def _(index):
            rows = pl.ds(pl.multiple_of(index * BLOCK, BLOCK), BLOCK)
            tokens = x_ref[0, rows, :]
            g_in = gres_ref[0, rows, :]
            for part in range(3):
                cols = slice(part * width, (part + 1) * width)
                piece = jnp.concatenate([mixed[part * PAIRS + head, rows, :] for head in range(PAIRS)], axis=1)
                g_in = g_in + nt(piece, w_ref[:, cols])
                acc_w[:, cols] += tn(tokens, piece)
                if part != 1:
                    dvec_ref[part // 2 : part // 2 + 1, :] += jnp.sum(piece.astype(f32), axis=0, keepdims=True)
            gin_ref[0, rows, :] = g_in.astype(bf16)

    @pl.when(time == steps - 1)
    def _():
        copies = []
        for part in range(3):
            cols = slice(part * width, (part + 1) * width)
            slot = part % 2
            if part >= 2:
                copies[part - 2].wait()
            stage[slot] = acc_w[:, cols].astype(bf16)
            copies.append(pltpu.make_async_copy(stage.at[slot], dw_ref.at[:, cols], copy_sems.at[slot]))
            copies[-1].start()
        copies[-2].wait()
        copies[-1].wait()
        if axes is not None:
            run_rest(scatter, exchange, plan, steps)


def attention_backward(axes, tokens, qkv, context, g_context, probs, g_res1, w_qkv, grads, results):
    seqs, rows, width = tokens.shape
    pair_cols = pl.BlockSpec((1, rows, PAIR), lambda s, p: (s, 0, p))
    seq_rows = pl.BlockSpec((1, rows, width), lambda s, p: (s, 0, 0))
    in_specs = [
        seq_rows,
        pl.BlockSpec((1, 3, 1, rows, PAIR), lambda s, p: (s, 0, p, 0, 0)),
        pair_cols,
        pair_cols,
        pl.BlockSpec((1, 1, 2, rows, rows), lambda s, p: (s, p, 0, 0, 0)),
        seq_rows,
        whole(w_qkv.shape),
    ]
    out_shape = [
        jax.ShapeDtypeStruct((seqs, rows, width), bf16),
        jax.ShapeDtypeStruct(w_qkv.shape, bf16),
        jax.ShapeDtypeStruct((8, width), f32),
    ]
    out_specs = [seq_rows, ANY, whole((8, width))]
    scratch = [
        pltpu.VMEM((3 * PAIRS, rows, PAIR), bf16),
        pltpu.VMEM(w_qkv.shape, f32),
        pltpu.VMEM((2, width, width), bf16),
        sems(2),
    ]
    extra, parts, plan, dealt, talk = [], [], {}, [], {}
    if axes is not None:
        sizes = tuple(size for _, _, size in axes)
        order = (1, 0, 2)
        grads = [grad.reshape(sizes + (-1, grad.shape[1])) for grad in grads]
        block = (grads[0].shape[4], width)
        for array, grad in enumerate(grads):
            parts += [(array, cut, order, len(parts) + i) for i, cut in enumerate(tiles(grad.shape[4:], block))]
        for place in range(len(parts)):
            at = max(0, place - 2)
            plan[place] = [at] + [2 * stage - 1 + at for stage in range(1, 5)]
        dealt = [piece for piece in range(PIECES)]
        extra = grads + [results]
        in_specs += [ANY] * len(extra)
        out_shape += [jax.ShapeDtypeStruct(grad.shape[4:], f32) for grad in grads]
        out_shape += [jax.ShapeDtypeStruct(results.shape, bf16)]
        out_specs += [whole(grad.shape[4:]) for grad in grads] + [ANY]
        friends = results.shape[0] - 1
        scratch += scatter_buffers(axes, order, len(parts), len(parts), block, bf16)
        scratch += scatter_sems(axes, len(parts)) + exchange_sems(friends)
        talk = {"collective_id": 4, "has_side_effects": True}
    return pl.pallas_call(
        functools.partial(backward_kernel, axes, seqs, parts, plan, dealt),
        out_shape=tuple(out_shape),
        grid_spec=pltpu.PrefetchScalarGridSpec(
            num_scalar_prefetch=0,
            grid=(seqs, PAIRS),
            in_specs=in_specs,
            out_specs=tuple(out_specs),
            scratch_shapes=scratch,
        ),
        compiler_params=pltpu.CompilerParams(vmem_limit_bytes=62 << 20, **talk),
        cost_estimate=pl.CostEstimate(flops=120_000_000_000, transcendentals=1, bytes_accessed=100_000_000),
        name="attention_backward",
    )(tokens, qkv.reshape(seqs, 3, PAIRS, rows, PAIR), context, g_context, probs, g_res1, w_qkv, *extra)


def scatter_kernel(axes, parts, orders, *refs):
    grad_ref, small_ref, note_ref, out_ref, out_small, notes_ref = refs[:6]
    place = Place(axes)
    member = place.at["fsdp"]
    friends = place.friends(notes_ref.shape[0])
    bufs = {order: refs[6 + 5 * i : 11 + 5 * i] for i, order in enumerate(orders + (None,))}
    rest = refs[6 + 5 * (len(orders) + 1) :]
    scatter = Scatter(place, parts, [grad_ref, small_ref], [out_ref, out_small], bufs, *rest[:3])
    meet(place, friends)
    told = [
        push(note_ref, notes_ref.at[member], rest[3].at[step], rest[4].at[step], (place.at["dp"], friend))
        for step, friend in enumerate(friends)
    ]
    for copy in told:
        copy.start()
    notes_ref[member] = note_ref[...]
    for stage in range(place.core + 2):
        for part in range(len(parts)):
            scatter.advance(part, stage)
    for copy in told:
        copy.wait()
    for part in range(len(parts)):
        scatter.finish(part)


def scatter_sums(axes, grad, small, note, shards):
    sizes = tuple(size for _, _, size in axes)
    grad = grad.reshape(sizes + (-1, grad.shape[1]))
    small = small.reshape(sizes + (-1, small.shape[1]))
    block = grad.shape[4:]
    orders = ((2, 1, 0), (1, 2, 0))
    cut = block[1] // 6
    parts = [(0, (ALL, pl.ds(place * cut, cut)), orders[place % 2], place // 2) for place in range(6)]
    parts.insert(0, (1, None, orders[0], 0))
    bufs = [buf for order in orders for buf in scatter_buffers(axes, order, 3, 3, (block[0], cut), bf16)]
    bufs += scatter_buffers(axes, orders[0], 1, 1, small.shape[4:], f32)
    return pl.pallas_call(
        functools.partial(scatter_kernel, axes, parts, orders),
        out_shape=(
            jax.ShapeDtypeStruct(block, f32),
            jax.ShapeDtypeStruct(small.shape[4:], f32),
            jax.ShapeDtypeStruct((shards,) + note.shape, f32),
        ),
        in_specs=[ANY, ANY, VMEM],
        out_specs=(VMEM, VMEM, VMEM),
        scratch_shapes=bufs + scatter_sems(axes, len(parts)) + [sems(shards - 1), sems(shards - 1)],
        compiler_params=pltpu.CompilerParams(collective_id=2, has_side_effects=True, vmem_limit_bytes=56 << 20),
        name="scatter_sums",
    )(grad, small, note)


def body(
    tokens, lengths, deal_order, qkv_weight, query_bias, value_bias, out_weight, out_bias, attn_gain, attn_shift,
    up_weight, up_bias, down_weight, down_bias, ffn_gain, ffn_shift, cotangent,
):
    shards = lax.axis_size("fsdp")
    axes = mesh_axes(lax.axis_size("dp"), shards)
    devices = lax.axis_size("dp") * shards
    seqs, rows, width = tokens.shape
    hidden = up_weight.shape[1]
    chunks = hidden // width
    per = width // devices
    column = shards * seqs
    base = lax.axis_index("dp") * column
    member = lax.axis_index("fsdp")
    order = lax.dynamic_slice_in_dim(deal_order, base, column) - base
    mine = member * seqs
    own_lengths = lax.dynamic_slice_in_dim(lengths, base + mine, seqs)
    target = lax.dynamic_slice_in_dim(order, mine, seqs) // seqs
    dealt_here = mine + jnp.arange(seqs, dtype=jnp.int32)
    matches = order[None, :] == dealt_here[:, None]
    source = jnp.sum(jnp.where(matches, jnp.arange(column, dtype=jnp.int32)[None, :], 0), axis=1)
    peers = jnp.arange(shards, dtype=jnp.int32)

    choice = jnp.sum(jnp.where(source[:, None] // seqs == peers[None, :], jnp.arange(seqs, dtype=jnp.int32)[:, None], 0), axis=0)

    rank = lax.axis_index("dp") * shards + member
    vectors = [query_bias, value_bias, out_bias, attn_gain, attn_shift, down_bias, ffn_gain, ffn_shift]
    small = lax.dynamic_update_slice(jnp.zeros((16, width), bf16), jnp.stack(vectors), (0, rank * per))
    start = rank * (chunks * per)
    small = lax.dynamic_update_slice(small, up_bias[None], (8 + start // width, lax.rem(start, width)))
    if axes is None:
        gather = lambda shard: lax.all_gather(shard, BOTH, axis=0, tiled=True)
        vectors = jnp.sum(lax.all_gather(small, BOTH, axis=0, tiled=False).astype(f32), axis=0)
        w_qkv, w_out, w_up, w_down = gather(qkv_weight), gather(out_weight), gather(up_weight), gather(down_weight)
        outgoing = jnp.stack([lax.dynamic_index_in_dim(cotangent, choice[j], 0, keepdims=False) for j in range(shards)])
        cots = lax.all_to_all(outgoing, "fsdp", split_axis=0, concat_axis=0, tiled=True)
        qkv, context, probs = attention_forward(axes, own_lengths, choice, tokens, [w_qkv, vectors], None, shards)
    else:
        qkv, context, probs, w_qkv, _, w_out, w_up, w_down, cots, vectors = attention_forward(
            axes, own_lengths, choice, tokens, [qkv_weight, small, out_weight, up_weight, down_weight], cotangent, shards
        )
        w_qkv, w_out, w_up, w_down = (array.reshape(-1, array.shape[-1]) for array in (w_qkv, w_out, w_up, w_down))
    results, g_res1, g_context, dw_out, dw_up, dw_down, dvec, rms = middle(
        own_lengths, target, target, tokens, context, cots, w_out, w_up, w_down, vectors
    )
    grads = [dw_out, dw_up, dw_down]
    outs = attention_backward(axes, tokens, qkv, context, g_context, probs, g_res1, w_qkv, grads, results)
    input_grad, dw_qkv, dqv = outs[:3]
    if axes is None:
        arrived = lax.all_to_all(results, "fsdp", split_axis=0, concat_axis=0, tiled=True)
    else:
        outw_grad, upw_grad, downw_grad, arrived = outs[3:]
    layer_out = jnp.stack(
        [lax.dynamic_index_in_dim(arrived, source[t] // seqs, 0, keepdims=False) for t in range(seqs)]
    )

    packed = (dvec[:8] + dqv).reshape(8, devices, per).transpose(1, 0, 2).reshape(devices, 8 * per)
    packed = jnp.concatenate([packed, dvec[8 : 8 + chunks].reshape(devices, chunks * per)], axis=1)
    packed = jnp.pad(packed, ((0, 0), (0, 8 * 128 - packed.shape[1])))
    rms = rms.reshape(seqs * 8, 128)
    if axes is None:
        scatter = lambda array: lax.psum_scatter(array, BOTH, scatter_dimension=0, tiled=True)
        qkvw_grad = scatter(dw_qkv).astype(f32)
        outw_grad, upw_grad, downw_grad = (scatter(grad).astype(f32) for grad in grads)
        packed = scatter(packed)
        rms = lax.all_gather(rms, "fsdp", axis=0, tiled=False)
    else:
        qkvw_grad, packed, rms = scatter_sums(axes, dw_qkv, packed.reshape(devices * 8, 128), rms, shards)
    packed = packed.reshape(-1)
    vector = [packed[place * per : (place + 1) * per] for place in range(8)]
    rms = rms.reshape(column, 8, 128)[:, :3, 0]
    branch_rms = jnp.sum(jnp.where((source[:, None] == jnp.arange(column))[:, :, None], rms[None], 0.0), axis=1)
    return (
        layer_out, input_grad, qkvw_grad, vector[0], vector[1], outw_grad, vector[2], vector[3], vector[4], upw_grad,
        packed[8 * per : (8 + chunks) * per], downw_grad, vector[5], vector[6], vector[7], branch_rms,
    )


def solution(mesh):
    rows3, rows2, rows1 = P(BOTH, None, None), P(BOTH, None), P(BOTH)
    in_specs = (
        rows3, P(), P(), rows2, rows1, rows1, rows2, rows1, rows1, rows1, rows2, rows1, rows2, rows1, rows1, rows1, rows3,
    )
    out_specs = (
        rows3, rows3, rows2, rows1, rows1, rows2, rows1, rows1, rows1, rows2, rows1, rows2, rows1, rows1, rows1, rows2,
    )
    return jax.shard_map(body, mesh=mesh, in_specs=in_specs, out_specs=out_specs, check_vma=False)
```

```python
import functools
import math

import jax
import jax.numpy as jnp
from jax import lax
from jax.experimental import pallas as pl
from jax.experimental.pallas import tpu as pltpu
from jax.sharding import PartitionSpec as P

HEADS = 12
HEAD_DIM = 64
PAIR = 2 * HEAD_DIM
PAIRS = HEADS // 2
BLOCK = 256
ROWS = 512
PIECES = 8
ALL = slice(None)
EVERY = (ALL, ALL)

f32 = jnp.float32
bf16 = jnp.bfloat16
norm_eps = 1e-05
masked_fill = -1e30
BOTH = ("dp", "fsdp")
MESH = pl.DeviceIdType.MESH


def nn(left, right):
    return lax.dot_general(left, right, (((1,), (0,)), ((), ())), preferred_element_type=f32)


def nt(left, right):
    return lax.dot_general(left, right, (((1,), (1,)), ((), ())), preferred_element_type=f32)


def tn(left, right):
    return lax.dot_general(left, right, (((0,), (0,)), ((), ())), preferred_element_type=f32)


def block_count(length):
    return (length + (BLOCK - 1)) // BLOCK


def whole(shape):
    return pl.BlockSpec(shape, lambda *_: (0,) * len(shape), pipeline_mode=pl.Buffered(1))


def sems(*shape):
    return pltpu.SemaphoreType.DMA(shape)


def tiles(shape, block):
    return [
        (pl.ds(top, block[0]), pl.ds(left, block[1]))
        for top in range(0, shape[0], block[0])
        for left in range(0, shape[1], block[1])
    ]


ANY = pl.BlockSpec(memory_space=pl.ANY)
VMEM = pl.BlockSpec(memory_space=pltpu.VMEM)


def mesh_axes(dp, fsdp):
    if (dp, fsdp) == (8, 4):
        return (("dp", 2, 4), ("dp", 1, 2), ("fsdp", 2, 2), ("fsdp", 1, 2))
    return None


class Place:
    def __init__(self, axes):
        self.axes = axes
        self.core = len(axes) - 1
        self.at = {name: lax.axis_index(name) for name in BOTH}
        self.own = [lax.rem(self.at[name] // stride, size) for name, stride, size in axes]

    def shifted(self, dim, step):
        size = self.axes[dim][2]
        return lax.rem(self.own[dim] + step + size, size)

    def device(self, dim, step):
        name, stride, _ = self.axes[dim]
        moved = self.at[name] + (self.shifted(dim, step) - self.own[dim]) * stride
        return tuple(moved if name == axis else self.at[axis] for axis in BOTH)

    def steps(self, dim):
        return range(1, self.axes[dim][2])

    def friends(self, count):
        member = self.at["fsdp"]
        return [lax.rem(member + step, count) for step in range(1, count)]


def meet(place, friends=()):
    barrier = pltpu.get_barrier_semaphore()
    peers = [place.device(dim, step) for dim in range(len(place.axes)) for step in place.steps(dim)]
    peers += [(place.at["dp"], friend) for friend in friends]
    for peer in peers:
        pl.semaphore_signal(barrier, inc=1, device_id=peer, device_id_type=MESH)
    pl.semaphore_wait(barrier, len(peers))


def push(source, target, send, recv, device):
    return pltpu.make_async_remote_copy(source, target, send, recv, device_id=device, device_id_type=MESH)


class Exchange:
    def __init__(self, place, mine, theirs, pieces, send, recv, local):
        self.place, self.mine, self.theirs, self.pieces = place, mine, theirs, pieces
        self.send, self.recv, self.local = send, recv, local

    def copies(self, piece):
        member = self.place.at["fsdp"]
        height = self.mine.shape[1] // self.pieces
        rows = pl.ds(piece * height, height)
        made = [
            push(
                self.mine.at[friend, rows],
                self.theirs.at[member, rows],
                self.send.at[step, piece],
                self.recv.at[step, piece],
                (self.place.at["dp"], friend),
            )
            for step, friend in enumerate(self.place.friends(self.mine.shape[0]))
        ]
        return made + [pltpu.make_async_copy(self.mine.at[member, rows], self.theirs.at[member, rows], self.local.at[piece])]

    def start(self, piece):
        for copy in self.copies(piece):
            copy.start()

    def fill(self, source, choice):
        for slot in range(self.mine.shape[0]):
            self.mine[slot] = source[choice[slot]]

    def wait(self):
        for piece in range(self.pieces):
            for copy in self.copies(piece):
                copy.wait()


def exchange_sems(friends):
    return [sems(friends, PIECES), sems(friends, PIECES), sems(PIECES)]


class Gather:
    def __init__(self, place, parts, shards, outs, send, recv, core_send, core_recv, local):
        self.place, self.parts, self.shards, self.outs = place, parts, shards, outs
        self.sems = send, recv
        self.core_sems = core_send, core_recv
        self.mine = [
            pltpu.make_async_copy(shard, out.at[tuple(place.own)], local.at[i])
            for i, (shard, out) in enumerate(zip(shards, outs))
        ]

    def start(self):
        for copy in self.mine:
            copy.start()

    def local(self):
        for copy in self.mine:
            copy.wait()

    def view(self, number, spot):
        array, cut, _ = self.parts[number]
        return self.outs[array].at[tuple(spot) + cut]

    def shard(self, number):
        array, cut, _ = self.parts[number]
        return self.shards[array].at[cut]

    def known(self, number, stage):
        order = self.parts[number][2]
        return [slice(None) if dim in order[:stage] else own for dim, own in enumerate(self.place.own)]

    def link(self, number, stage):
        order = self.parts[number][2]
        spot = self.known(number, stage)
        source = self.view(number, spot) if stage else self.shard(number)
        first = sum(self.place.axes[dim][2] - 1 for dim in order[:stage])
        send, recv = self.sems
        return [
            push(
                source,
                self.view(number, spot),
                send.at[number, first + step - 1],
                recv.at[number, first + step - 1],
                self.place.device(order[stage], step),
            )
            for step in self.place.steps(order[stage])
        ]

    def across(self, number, stage):
        order = self.parts[number][2]
        core_send, core_recv = self.core_sems
        peer = self.place.device(self.place.core, 1)
        if stage == 0:
            spot = self.known(number, 0)
            return [push(self.shard(number), self.view(number, spot), core_send.at[number, 0], core_recv.at[number, 0], peer)]
        first = sum(self.place.axes[dim][2] - 1 for dim in order[: stage - 1])
        dim = order[stage - 1]
        copies = []
        for step in self.place.steps(dim):
            spot = self.known(number, stage - 1)
            spot[dim] = self.place.shifted(dim, -step)
            view, piece = self.view(number, spot), first + step
            copies.append(push(view, view, core_send.at[number, piece], core_recv.at[number, piece], peer))
        return copies

    def advance(self, number, stage):
        if stage:
            for copy in self.link(number, stage - 1):
                copy.wait_recv()
        if stage < self.place.core:
            for copy in self.link(number, stage):
                copy.start()
        for copy in self.across(number, stage):
            copy.start()

    def finish(self, number):
        for stage in range(self.place.core + 1):
            if stage < self.place.core:
                for copy in self.link(number, stage):
                    copy.wait_send()
            for copy in self.across(number, stage):
                copy.wait()


def gather_sems(axes, parts, count):
    hops = sum(size - 1 for _, _, size in axes[:-1])
    shapes = (len(parts), hops), (len(parts), hops), (len(parts), hops + 1), (len(parts), hops + 1), (count,)
    return [sems(*shape) for shape in shapes]


class Scatter:
    def __init__(self, place, parts, grads, outs, bufs, send, recv, local):
        self.place, self.parts, self.grads, self.outs = place, parts, grads, outs
        self.bufs = bufs
        self.send, self.recv, self.local = send, recv, local

    def refs(self, number):
        _, _, order, slot = self.parts[number]
        own, *came = self.bufs[order if self.parts[number][1] is not None else None]
        held = own.shape[0]
        return [own.at[slot % held]] + [buf.at[slot] for buf in came]

    def first(self, number, stage):
        order = self.parts[number][2]
        return 1 + sum(self.place.axes[dim][2] - 1 for dim in order[:stage])

    def block(self, number, core):
        array, cut, _, _ = self.parts[number]
        lead = (slice(None),) * self.place.core + (core,)
        return self.grads[array].at[lead + (EVERY if cut is None else cut)]

    def across(self, number):
        place = self.place
        return push(
            self.block(number, place.shifted(place.core, 1)),
            self.refs(number)[1],
            self.send.at[number, 0],
            self.recv.at[number, 0],
            place.device(place.core, 1),
        )

    def own(self, number):
        return pltpu.make_async_copy(
            self.block(number, self.place.own[self.place.core]), self.refs(number)[0], self.local.at[number]
        )

    def spot(self, number, stage, at):
        order = self.parts[number][2]
        dims = [slice(None)] * self.place.core
        for dim in order[:stage]:
            dims[dim] = self.place.own[dim]
        if at is not None:
            dims[order[stage]] = at
        return dims

    def link(self, number, stage, step):
        dim = self.parts[number][2][stage]
        place, refs = self.place, self.refs(number)
        piece = self.first(number, stage) + step - 1
        return push(
            refs[0].at[tuple(self.spot(number, stage, place.shifted(dim, step)))],
            refs[2 + stage].at[step - 1],
            self.send.at[number, piece],
            self.recv.at[number, piece],
            place.device(dim, step),
        )

    def add(self, number, spot, extras):
        acc = self.refs(number)[0]
        free = [dim for dim, index in enumerate(spot) if isinstance(index, slice)]
        sizes = [self.place.axes[dim][2] for dim in free]
        total = math.prod(sizes)

        def one(place, carry):
            index, where = list(spot), []
            rest = place
            for dim, size in zip(reversed(free), reversed(sizes)):
                index[dim] = lax.rem(rest, size)
                where.insert(0, index[dim])
                rest = rest // size
            index = tuple(index)
            value = acc[index].astype(f32)
            for extra in extras:
                value = value + extra[tuple(where)].astype(f32)
            acc[index] = value.astype(acc.dtype)
            return carry

        if total == 1:
            one(0, 0)
        else:
            lax.fori_loop(0, total, one, 0)

    def advance(self, number, stage):
        array, cut, order, _ = self.parts[number]
        place, refs = self.place, self.refs(number)
        if stage == 0:
            self.across(number).start()
            self.own(number).start()
            return
        if stage == 1:
            self.own(number).wait()
            self.across(number).wait_recv()
            came = [refs[1]]
        else:
            dim = order[stage - 2]
            for step in place.steps(dim):
                self.link(number, stage - 2, step).wait_recv()
            came = [refs[stage].at[step - 1] for step in place.steps(dim)]
        if stage <= place.core:
            dim = order[stage - 1]
            for step in list(place.steps(dim)) + [0]:
                at = place.shifted(dim, step)
                spot = self.spot(number, stage - 1, at)
                where = self.within(number, stage - 1, at)
                self.add(number, spot, [extra.at[where] for extra in came])
                if step:
                    self.link(number, stage - 1, step).start()
        else:
            total = refs[0][tuple(place.own[:-1])].astype(f32)
            for extra in came:
                total = total + extra[...].astype(f32)
            self.outs[array][EVERY if cut is None else cut] = total

    def within(self, number, stage, at):
        order = self.parts[number][2]
        rest = [dim for dim in range(self.place.core) if dim not in order[:stage]]
        return tuple(at if dim == order[stage] else slice(None) for dim in rest)

    def finish(self, number):
        self.across(number).wait_send()
        order = self.parts[number][2]
        for stage, dim in enumerate(order):
            for step in self.place.steps(dim):
                self.link(number, stage, step).wait_send()


def scatter_buffers(axes, order, tiles, held, block, dtype):
    sizes = [size for _, _, size in axes[:-1]]
    leads = [(held,) + tuple(sizes), (tiles,) + tuple(sizes)]
    left = list(range(len(sizes)))
    for dim in order:
        left.remove(dim)
        leads.append((tiles, sizes[dim] - 1) + tuple(sizes[other] for other in left))
    return [pltpu.VMEM(lead + tuple(block), dtype) for lead in leads]


def scatter_sems(axes, count):
    hops = 1 + sum(size - 1 for _, _, size in axes[:-1])
    return [sems(count, hops), sems(count, hops), sems(count)]


def run_steps(mover, exchange, plan, dealt, time, steps, first=0):
    for step in range(first, steps):
        todo = [(part, stage) for part, row in plan.items() for stage, at in enumerate(row) if at == step]
        pieces = [piece for piece, at in enumerate(dealt) if at == step]

        @pl.when(time == step)
        def _(todo=todo, pieces=pieces):
            for part, stage in todo:
                mover.advance(part, stage)
            for piece in pieces:
                exchange.start(piece)


def run_rest(mover, exchange, plan, steps):
    for part, row in plan.items():
        for stage, at in enumerate(row):
            if at >= steps:
                mover.advance(part, stage)
    for part in plan:
        mover.finish(part)
    exchange.wait()


def forward_kernel(axes, seqs, parts, early, plan, dealt, len_ref, choice_ref, x_ref, *refs):
    seq, pair = pl.program_id(0), pl.program_id(1)
    time = seq * PAIRS + pair
    steps = seqs * PAIRS
    length = len_ref[seq]
    count, width = x_ref.shape[1], x_ref.shape[2]
    lane = lax.broadcasted_iota(jnp.int32, (1, PAIR), 1)
    if axes is None:
        w_ref, vec_ref, qkv_ref, ctx_ref, probs_ref = refs
    else:
        shards, cot_ref, qkv_ref, ctx_ref, probs_ref = refs[:5], refs[5], refs[6], refs[7], refs[8]
        gathered, cots_ref, vec_ref = refs[9:14], refs[14], refs[15]
        w_ref, raw_ref, small_ref, held_ref, going_ref, copy_sems = refs[16:22]
        place = Place(axes)
        gather = Gather(place, parts, shards, gathered, *refs[22:27])
        exchange = Exchange(place, going_ref, cots_ref, PIECES, *refs[27:30])

        @pl.when(time == 0)
        def _():
            now = [
                pltpu.make_async_copy(cot_ref, held_ref, copy_sems.at[0]),
                pltpu.make_async_copy(gathered[0], raw_ref, copy_sems.at[1]),
                pltpu.make_async_copy(gathered[1], small_ref, copy_sems.at[2]),
            ]
            now[0].start()
            meet(place, place.friends(cots_ref.shape[0]))
            gather.start()
            for part in list(early) + list(plan):
                gather.advance(part, 0)
            now[0].wait()
            exchange.fill(held_ref, choice_ref)
            gather.local()
            for stage in range(1, place.core + 1):
                for part in early:
                    gather.advance(part, stage)
                for part, row in plan.items():
                    if stage == 1 and row[1] == 0:
                        gather.advance(part, 1)
                for piece, at in enumerate(dealt):
                    if stage == 2 and at == 0:
                        exchange.start(piece)
            for part in early:
                gather.finish(part)
            for copy in now[1:]:
                copy.start()
            for copy in now[1:]:
                copy.wait()
            depth, across, along, _ = raw_ref.shape[:4]
            height = 2 * raw_ref.shape[4]

            def one(block, total):
                spot = block // (across * along), lax.rem(block // along, across), lax.rem(block, along)
                both = jnp.concatenate([raw_ref[spot + (half,)].astype(f32) for half in range(2)], axis=0)
                w_ref[pl.ds(pl.multiple_of(block * height, height), height), :] = both.astype(bf16)
                return total + small_ref[spot + (0,)].astype(f32) + small_ref[spot + (1,)].astype(f32)

            vec_ref[...] = lax.fori_loop(0, depth * across * along, one, jnp.zeros((16, width), f32))

        run_steps(gather, exchange, plan, dealt, time, steps, 1)

    @pl.when(pair == 0)
    def _():
        tokens = x_ref[0]
        step = 2 * PAIR
        for start in range(0, 3 * width, step):
            part = start // width
            projected = nn(tokens, w_ref[:, start : start + step])
            if part != 1:
                cols = slice(start - part * width, start - part * width + step)
                projected = projected + vec_ref[part // 2 : part // 2 + 1, cols]
            projected = projected.astype(bf16)
            if part == 0:
                projected = projected * jnp.asarray(1.0 / math.sqrt(HEAD_DIM), bf16)
            for half in range(2):
                qkv_ref[0, start // PAIR + half] = projected[:, half * PAIR : (half + 1) * PAIR]

    key = qkv_ref[0, PAIRS + pair]
    value = qkv_ref[0, 2 * PAIRS + pair]
    unusable = lax.broadcasted_iota(jnp.int32, (count, 1), 0) >= length
    mask = jnp.where(unusable, masked_fill, 0.0).astype(bf16)
    keys = [jnp.where(lane == spare, mask, key) for spare in (PAIR - 1, 0)]
    for start in range(0, count, ROWS):
        rows = slice(start, start + ROWS)
        query = qkv_ref[0, pair, rows, :]
        outs = []
        for head in range(2):
            mine = (lane < HEAD_DIM) if head == 0 else (lane >= HEAD_DIM)
            spare = jnp.where(lane == (PAIR - 1 if head == 0 else 0), 1.0, 0.0).astype(bf16)
            scores = nt(jnp.where(mine, query, spare), keys[head])
            top = jnp.max(scores, axis=1, keepdims=True)
            powers = jnp.exp(scores - top)
            total = jnp.sum(powers, axis=1, keepdims=True)
            probs = (powers * (1.0 / total)).astype(bf16)
            probs_ref[0, 0, head, rows, :] = probs
            outs.append(nn(probs, value))
        ctx_ref[0, rows, :] = jnp.where(lane < HEAD_DIM, outs[0], outs[1]).astype(bf16)

    if axes is not None:

        @pl.when(time == steps - 1)
        def _():
            run_rest(gather, exchange, plan, steps)


def attention_forward(axes, lengths, choice, tokens, operands, cotangent, shards):
    seqs, rows, width = tokens.shape
    out_shape = [
        jax.ShapeDtypeStruct((seqs, 3 * PAIRS, rows, PAIR), bf16),
        jax.ShapeDtypeStruct((seqs, rows, width), bf16),
        jax.ShapeDtypeStruct((seqs, PAIRS, 2, rows, rows), bf16),
    ]
    in_specs = [pl.BlockSpec((1, rows, width), lambda s, p, *_: (s, 0, 0))]
    out_specs = [
        pl.BlockSpec((1, 3 * PAIRS, rows, PAIR), lambda s, p, *_: (s, 0, 0, 0)),
        pl.BlockSpec((1, rows, PAIR), lambda s, p, *_: (s, 0, p)),
        pl.BlockSpec((1, 1, 2, rows, rows), lambda s, p, *_: (s, p, 0, 0, 0)),
    ]
    scratch, parts, early, plan, dealt, talk = [], [], [], {}, [], {}
    extra = list(operands)
    if axes is None:
        in_specs += [whole(array.shape) for array in operands]
    else:
        orders = ((0, 2, 1), (0, 2, 1), (1, 0, 2))
        first, small, *later = operands
        parts.append((1, EVERY, orders[0]))
        for cut in tiles(first.shape, (first.shape[0], first.shape[1] // 6)):
            parts.append((0, cut, orders[(len(parts) - 1) % 3]))
        early = range(len(parts))
        for array, shard in enumerate(later, 2):
            parts += [(array, cut, (2, 0, 1)) for cut in tiles(shard.shape, (first.shape[0], width))]
        for place in range(len(parts) - len(early)):
            at = max(0, place - 2)
            plan[place + len(early)] = [0, at, at + (1 if place < 2 else 2), at + (3 if place < 2 else 4)]
        dealt = [max(0, piece - 1) for piece in range(PIECES)]
        extra += [cotangent]
        in_specs += [ANY] * len(extra)
        sizes = tuple(size for _, _, size in axes)
        out_shape += [jax.ShapeDtypeStruct(sizes + shard.shape, bf16) for shard in operands]
        out_shape += [jax.ShapeDtypeStruct((shards, rows, width), bf16), jax.ShapeDtypeStruct(small.shape, f32)]
        out_specs += [ANY] * (len(operands) + 1) + [whole(small.shape)]
        scratch = [
            pltpu.VMEM((width, first.shape[1]), bf16),
            pltpu.VMEM(sizes + first.shape, bf16),
            pltpu.VMEM(sizes + small.shape, bf16),
            pltpu.VMEM(cotangent.shape, bf16),
            pltpu.VMEM((shards, rows, width), bf16),
            sems(3),
        ]
        scratch += gather_sems(axes, parts, len(operands)) + exchange_sems(shards - 1)
        talk = {"collective_id": 3, "has_side_effects": True}
    return pl.pallas_call(
        functools.partial(forward_kernel, axes, seqs, parts, early, plan, dealt),
        out_shape=tuple(out_shape),
        grid_spec=pltpu.PrefetchScalarGridSpec(
            num_scalar_prefetch=2,
            grid=(seqs, PAIRS),
            in_specs=in_specs,
            out_specs=tuple(out_specs),
            scratch_shapes=scratch,
        ),
        compiler_params=pltpu.CompilerParams(vmem_limit_bytes=60 << 20, **talk),
        cost_estimate=pl.CostEstimate(flops=60_000_000_000, transcendentals=30_000_000, bytes_accessed=80_000_000),
        name="attention_forward",
    )(lengths, choice, tokens, *extra)


def normal_tail(values):
    size = jnp.abs(values)
    bell = jnp.exp(-0.5 * values * values)
    t = 1.0 / (1.0 + (0.3275911 / math.sqrt(2.0)) * size)
    poly = t * (
        0.5 * 0.254829592
        + t * (0.5 * -0.284496736 + t * (0.5 * 1.421413741 + t * (0.5 * -1.453152027 + t * (0.5 * 1.061405429))))
    )
    tail = poly * bell
    return jnp.where(values >= 0, 1.0 - tail, tail), bell


def row_mean(values):
    return jnp.mean(values, axis=-1, keepdims=True)


def middle_kernel(
    len_ref, in_slot, out_slot, x_ref, ctx_ref, cot_ref, wo_ref, wu_ref, wd_ref, vec_ref,
    out_ref, gres_ref, gctx_ref, dwo_ref, dwu_ref, dwd_ref, dvec_ref, rms_ref,
    acc_o, acc_u, acc_d, active, slope, sums, stage, sems,
):
    seq, index = pl.program_id(0), pl.program_id(1)
    first = jnp.logical_and(seq == 0, index == 0)
    final = jnp.logical_and(seq == pl.num_programs(0) - 1, index == pl.num_programs(1) - 1)
    length = len_ref[seq]
    width = x_ref.shape[2]
    chunks = wu_ref.shape[1] // width
    tile = lambda place: slice(place * width, (place + 1) * width)

    @pl.when(first)
    def _():
        acc_o[...] = jnp.zeros_like(acc_o)
        acc_u[...] = jnp.zeros_like(acc_u)
        acc_d[...] = jnp.zeros_like(acc_d)
        dvec_ref[...] = jnp.zeros_like(dvec_ref)

    @pl.when(index == 0)
    def _():
        sums[...] = jnp.zeros_like(sums)

    @pl.when(index * BLOCK >= length)
    def _():
        out_ref[...] = jnp.zeros_like(out_ref)
        gres_ref[...] = jnp.zeros_like(gres_ref)
        gctx_ref[...] = jnp.zeros_like(gctx_ref)

    @pl.when(index * BLOCK < length)
    def _():
        vec = lambda place: vec_ref[place : place + 1, :]
        bias_out, gain_a, shift_a, bias_down, gain_f, shift_f = (vec(place) for place in range(2, 8))
        valid = (lax.broadcasted_iota(jnp.int32, (BLOCK, 1), 0) + index * BLOCK < length).astype(f32)
        tokens = x_ref[0].astype(f32)
        context = ctx_ref[0]
        branch_a = nn(context, wo_ref[...]) + bias_out
        mixed = tokens + branch_a
        center = mixed - row_mean(mixed)
        scale_a = lax.rsqrt(row_mean(center * center) + norm_eps)
        hat_a = center * scale_a
        hidden = hat_a * gain_a + shift_a
        hidden_low = hidden.astype(bf16)
        branch_f = bias_down
        for chunk in range(chunks):
            cols = tile(chunk)
            gate = nn(hidden_low, wu_ref[:, cols]) + vec(8 + chunk)
            share, bell = normal_tail(gate)
            act = (gate * share).astype(bf16)
            active[:, cols] = act
            slope[:, cols] = share + gate * bell * (1.0 / math.sqrt(2.0 * math.pi))
            branch_f = branch_f + nn(act, wd_ref[cols, :])
        mixed_f = hidden + branch_f
        center = mixed_f - row_mean(mixed_f)
        scale_f = lax.rsqrt(row_mean(center * center) + norm_eps)
        hat_f = center * scale_f
        out_ref[0] = ((hat_f * gain_f + shift_f) * valid).astype(bf16)
        g_result = cot_ref[0].astype(f32) * valid
        g_hat = g_result * gain_f
        g_res2 = scale_f * (g_hat - row_mean(g_hat) - hat_f * row_mean(g_hat * hat_f))
        g_ffn = g_res2.astype(bf16)
        g_hidden = g_res2
        for chunk in range(chunks):
            cols = tile(chunk)
            g_gate = nt(g_ffn, wd_ref[cols, :]) * slope[:, cols]
            g_low = g_gate.astype(bf16)
            acc_d[cols, :] += tn(active[:, cols], g_ffn)
            acc_u[:, cols] += tn(hidden_low, g_low)
            dvec_ref[8 + chunk : 9 + chunk, :] += jnp.sum(g_low.astype(f32), axis=0, keepdims=True)
            g_hidden = g_hidden + nt(g_low, wu_ref[:, cols])
        g_hat = g_hidden * gain_a
        g_res1 = scale_a * (g_hat - row_mean(g_hat) - hat_a * row_mean(g_hat * hat_a))
        g_attn = g_res1.astype(bf16)
        gres_ref[0] = g_res1
        gctx_ref[0] = nt(g_attn, wo_ref[...]).astype(bf16)
        acc_o[...] += tn(context, g_attn)
        column = lambda values: jnp.sum(values, axis=0, keepdims=True)
        dvec_ref[2:3, :] += column(g_attn.astype(f32))
        dvec_ref[3:4, :] += column(g_hidden * hat_a)
        dvec_ref[4:5, :] += column(g_hidden)
        dvec_ref[5:6, :] += column(g_ffn.astype(f32))
        dvec_ref[6:7, :] += column(g_result * hat_f)
        dvec_ref[7:8, :] += column(g_result)
        sums[0:1, :] += column(tokens * tokens * valid)
        sums[1:2, :] += column(branch_a * branch_a * valid)
        sums[2:3, :] += column(branch_f * branch_f * valid)

    @pl.when(index == pl.num_programs(1) - 1)
    def _():
        mean = jnp.sum(sums[...], axis=1, keepdims=True) / (length * width).astype(f32)
        rms_ref[0] = jnp.broadcast_to(jnp.sqrt(mean), rms_ref.shape[1:])

    @pl.when(final)
    def _():
        pieces = [(acc_o, dwo_ref, EVERY)]
        pieces += [(acc_u, dwu_ref, (ALL, tile(chunk))) for chunk in range(chunks)]
        pieces += [(acc_d, dwd_ref, (tile(chunk), ALL)) for chunk in range(chunks)]
        copies = []
        for place, (acc, out, cut) in enumerate(pieces):
            slot = place % 2
            if place >= 2:
                copies[place - 2].wait()
            stage[slot] = acc[cut].astype(bf16)
            copies.append(pltpu.make_async_copy(stage.at[slot], out.at[cut], sems.at[slot]))
            copies[-1].start()
        copies[-2].wait()
        copies[-1].wait()


def middle(lengths, in_slot, out_slot, tokens, context, cots, w_out, w_up, w_down, vectors):
    seqs, rows, width = tokens.shape
    slots = cots.shape[0]
    hidden = w_up.shape[1]
    inside = lambda s, i, lens: jnp.minimum(i, block_count(lens[s]) - 1)
    here = pl.BlockSpec((1, BLOCK, width), lambda s, i, lens, a, b: (s, inside(s, i, lens), 0))
    there = pl.BlockSpec((1, BLOCK, width), lambda s, i, *_: (s, i, 0))
    flops = 6 * seqs * rows * (width * width + 2 * width * hidden)
    return pl.pallas_call(
        middle_kernel,
        out_shape=(
            jax.ShapeDtypeStruct((slots, rows, width), bf16),
            jax.ShapeDtypeStruct((seqs, rows, width), f32),
            jax.ShapeDtypeStruct((seqs, rows, width), bf16),
            jax.ShapeDtypeStruct(w_out.shape, bf16),
            jax.ShapeDtypeStruct(w_up.shape, bf16),
            jax.ShapeDtypeStruct(w_down.shape, bf16),
            jax.ShapeDtypeStruct((16, width), f32),
            jax.ShapeDtypeStruct((seqs, 8, 128), f32),
        ),
        grid_spec=pltpu.PrefetchScalarGridSpec(
            num_scalar_prefetch=3,
            grid=(seqs, rows // BLOCK),
            in_specs=[
                here,
                here,
                pl.BlockSpec((1, BLOCK, width), lambda s, i, lens, a, b: (a[s], inside(s, i, lens), 0)),
                whole(w_out.shape),
                whole(w_up.shape),
                whole(w_down.shape),
                whole(vectors.shape),
            ],
            out_specs=[
                pl.BlockSpec((1, BLOCK, width), lambda s, i, lens, a, b: (b[s], i, 0)),
                there,
                there,
                ANY,
                ANY,
                ANY,
                whole((16, width)),
                pl.BlockSpec((1, 8, 128), lambda s, i, *_: (s, 0, 0)),
            ],
            scratch_shapes=[
                pltpu.VMEM(w_out.shape, f32),
                pltpu.VMEM(w_up.shape, f32),
                pltpu.VMEM(w_down.shape, f32),
                pltpu.VMEM((BLOCK, hidden), bf16),
                pltpu.VMEM((BLOCK, hidden), f32),
                pltpu.VMEM((8, width), f32),
                pltpu.VMEM((2, width, width), bf16),
                pltpu.SemaphoreType.DMA((2,)),
            ],
        ),
        compiler_params=pltpu.CompilerParams(vmem_limit_bytes=60 << 20),
        cost_estimate=pl.CostEstimate(flops=flops, transcendentals=seqs * rows * hidden, bytes_accessed=60_000_000),
        name="middle",
    )(lengths, in_slot, out_slot, tokens, context, cots, w_out, w_up, w_down, vectors)


def backward_kernel(axes, seqs, parts, plan, dealt, x_ref, qkv_in, ctx_ref, gctx_ref, probs_ref, gres_ref, w_ref, *refs):
    if axes is None:
        gin_ref, dw_ref, dvec_ref = refs[:3]
        mixed, acc_w, stage, copy_sems = refs[3:]
    else:
        grads, result_ref, gin_ref, dw_ref, dvec_ref = refs[:3], refs[3], refs[4], refs[5], refs[6]
        summed, arrived_ref = refs[7:10], refs[10]
        mixed, acc_w, stage, copy_sems = refs[11:15]
        place = Place(axes)
        bufs = {parts[0][2]: refs[15:20]}
        scatter = Scatter(place, parts, grads, summed, bufs, *refs[20:23])
        exchange = Exchange(place, result_ref, arrived_ref, PIECES, *refs[23:26])
    seq, pair = pl.program_id(0), pl.program_id(1)
    time = seq * PAIRS + pair
    steps = seqs * PAIRS
    count, width = x_ref.shape[1], x_ref.shape[2]
    lane = lax.broadcasted_iota(jnp.int32, (1, PAIR), 1)

    if axes is not None:

        @pl.when(time == 0)
        def _():
            meet(place, place.friends(result_ref.shape[0]))

        run_steps(scatter, exchange, plan, dealt, time, steps)

    @pl.when(time == 0)
    def _():
        acc_w[...] = jnp.zeros_like(acc_w)
        dvec_ref[...] = jnp.zeros_like(dvec_ref)

    key = qkv_in[0, 1, 0]
    value = qkv_in[0, 2, 0]
    g_key, g_value = [0.0, 0.0], [0.0, 0.0]
    for start in range(0, count, ROWS):
        rows = slice(start, start + ROWS)
        query = qkv_in[0, 0, 0, rows, :]
        grad = gctx_ref[0, rows, :]
        agree = grad.astype(f32) * ctx_ref[0, rows, :].astype(f32)
        query_t, grad_t = query.T, grad.T
        g_query = jnp.zeros((ROWS, PAIR), f32)
        for head in range(2):
            mine = (lane < HEAD_DIM) if head == 0 else (lane >= HEAD_DIM)
            only = lambda values: jnp.where(mine, values, jnp.zeros_like(values))
            lanes = slice(head * HEAD_DIM, (head + 1) * HEAD_DIM)
            delta = jnp.sum(only(agree), axis=1, keepdims=True)
            probs = probs_ref[0, 0, head, rows, :]
            g_probs = nt(only(grad), value)
            g_scores = (probs.astype(f32) * (g_probs - delta)).astype(bf16)
            g_query = g_query + nn(g_scores, only(key))
            g_key[head] = g_key[head] + nn(query_t[lanes], g_scores)
            g_value[head] = g_value[head] + nn(grad_t[lanes], probs)
        mixed[pair, rows, :] = (g_query * (1.0 / math.sqrt(HEAD_DIM))).astype(bf16)
    mixed[PAIRS + pair] = jnp.concatenate(g_key, axis=0).T.astype(bf16)
    mixed[2 * PAIRS + pair] = jnp.concatenate(g_value, axis=0).T.astype(bf16)

    @pl.when(pair == PAIRS - 1)
    def _():
        @pl.loop(0, count // BLOCK)
        def _(index):
            rows = pl.ds(pl.multiple_of(index * BLOCK, BLOCK), BLOCK)
            tokens = x_ref[0, rows, :]
            g_in = gres_ref[0, rows, :]
            for part in range(3):
                cols = slice(part * width, (part + 1) * width)
                piece = jnp.concatenate([mixed[part * PAIRS + head, rows, :] for head in range(PAIRS)], axis=1)
                g_in = g_in + nt(piece, w_ref[:, cols])
                acc_w[:, cols] += tn(tokens, piece)
                if part != 1:
                    dvec_ref[part // 2 : part // 2 + 1, :] += jnp.sum(piece.astype(f32), axis=0, keepdims=True)
            gin_ref[0, rows, :] = g_in.astype(bf16)

    @pl.when(time == steps - 1)
    def _():
        copies = []
        for part in range(3):
            cols = slice(part * width, (part + 1) * width)
            slot = part % 2
            if part >= 2:
                copies[part - 2].wait()
            stage[slot] = acc_w[:, cols].astype(bf16)
            copies.append(pltpu.make_async_copy(stage.at[slot], dw_ref.at[:, cols], copy_sems.at[slot]))
            copies[-1].start()
        copies[-2].wait()
        copies[-1].wait()
        if axes is not None:
            run_rest(scatter, exchange, plan, steps)


def attention_backward(axes, tokens, qkv, context, g_context, probs, g_res1, w_qkv, grads, results):
    seqs, rows, width = tokens.shape
    pair_cols = pl.BlockSpec((1, rows, PAIR), lambda s, p: (s, 0, p))
    seq_rows = pl.BlockSpec((1, rows, width), lambda s, p: (s, 0, 0))
    in_specs = [
        seq_rows,
        pl.BlockSpec((1, 3, 1, rows, PAIR), lambda s, p: (s, 0, p, 0, 0)),
        pair_cols,
        pair_cols,
        pl.BlockSpec((1, 1, 2, rows, rows), lambda s, p: (s, p, 0, 0, 0)),
        seq_rows,
        whole(w_qkv.shape),
    ]
    out_shape = [
        jax.ShapeDtypeStruct((seqs, rows, width), bf16),
        jax.ShapeDtypeStruct(w_qkv.shape, bf16),
        jax.ShapeDtypeStruct((8, width), f32),
    ]
    out_specs = [seq_rows, ANY, whole((8, width))]
    scratch = [
        pltpu.VMEM((3 * PAIRS, rows, PAIR), bf16),
        pltpu.VMEM(w_qkv.shape, f32),
        pltpu.VMEM((2, width, width), bf16),
        sems(2),
    ]
    extra, parts, plan, dealt, talk = [], [], {}, [], {}
    if axes is not None:
        sizes = tuple(size for _, _, size in axes)
        order = (1, 0, 2)
        grads = [grad.reshape(sizes + (-1, grad.shape[1])) for grad in grads]
        block = (grads[0].shape[4], width)
        for array, grad in enumerate(grads):
            parts += [(array, cut, order, len(parts) + i) for i, cut in enumerate(tiles(grad.shape[4:], block))]
        for place in range(len(parts)):
            at = max(0, place - 2)
            plan[place] = [at] + [2 * stage - 1 + at for stage in range(1, 5)]
        dealt = [piece for piece in range(PIECES)]
        extra = grads + [results]
        in_specs += [ANY] * len(extra)
        out_shape += [jax.ShapeDtypeStruct(grad.shape[4:], f32) for grad in grads]
        out_shape += [jax.ShapeDtypeStruct(results.shape, bf16)]
        out_specs += [whole(grad.shape[4:]) for grad in grads] + [ANY]
        friends = results.shape[0] - 1
        scratch += scatter_buffers(axes, order, len(parts), len(parts), block, bf16)
        scratch += scatter_sems(axes, len(parts)) + exchange_sems(friends)
        talk = {"collective_id": 4, "has_side_effects": True}
    return pl.pallas_call(
        functools.partial(backward_kernel, axes, seqs, parts, plan, dealt),
        out_shape=tuple(out_shape),
        grid_spec=pltpu.PrefetchScalarGridSpec(
            num_scalar_prefetch=0,
            grid=(seqs, PAIRS),
            in_specs=in_specs,
            out_specs=tuple(out_specs),
            scratch_shapes=scratch,
        ),
        compiler_params=pltpu.CompilerParams(vmem_limit_bytes=62 << 20, **talk),
        cost_estimate=pl.CostEstimate(flops=120_000_000_000, transcendentals=1, bytes_accessed=100_000_000),
        name="attention_backward",
    )(tokens, qkv.reshape(seqs, 3, PAIRS, rows, PAIR), context, g_context, probs, g_res1, w_qkv, *extra)


def scatter_kernel(axes, parts, orders, *refs):
    grad_ref, small_ref, note_ref, arrived_ref, pick_ref, out_ref, out_small, notes_ref, layer_ref = refs[:9]
    came, kept, layer_sems = refs[-3:]
    refs = refs[3:-3]
    fetch = pltpu.make_async_copy(arrived_ref, came, layer_sems.at[0])
    store = pltpu.make_async_copy(kept, layer_ref, layer_sems.at[1])
    fetch.start()
    place = Place(axes)
    member = place.at["fsdp"]
    friends = place.friends(notes_ref.shape[0])
    bufs = {order: refs[6 + 5 * i : 11 + 5 * i] for i, order in enumerate(orders + (None,))}
    rest = refs[6 + 5 * (len(orders) + 1) :]
    scatter = Scatter(place, parts, [grad_ref, small_ref], [out_ref, out_small], bufs, *rest[:3])
    meet(place, friends)
    told = [
        push(note_ref, notes_ref.at[member], rest[3].at[step], rest[4].at[step], (place.at["dp"], friend))
        for step, friend in enumerate(friends)
    ]
    for copy in told:
        copy.start()
    notes_ref[member] = note_ref[...]
    for stage in range(place.core + 2):
        for part in range(len(parts)):
            scatter.advance(part, stage)
        if stage == 1:
            fetch.wait()
            for slot in range(kept.shape[0]):
                kept[slot] = came[pick_ref[slot]]
            store.start()
    store.wait()
    for copy in told:
        copy.wait()
    for part in range(len(parts)):
        scatter.finish(part)


def scatter_sums(axes, grad, small, note, shards, arrived, pick):
    sizes = tuple(size for _, _, size in axes)
    grad = grad.reshape(sizes + (-1, grad.shape[1]))
    small = small.reshape(sizes + (-1, small.shape[1]))
    block = grad.shape[4:]
    orders = ((2, 1, 0), (1, 2, 0))
    cut = block[1] // 6
    parts = [(0, (ALL, pl.ds(place * cut, cut)), orders[place % 2], place // 2) for place in range(6)]
    parts.insert(0, (1, None, orders[0], 0))
    bufs = [buf for order in orders for buf in scatter_buffers(axes, order, 3, 3, (block[0], cut), bf16)]
    bufs += scatter_buffers(axes, orders[0], 1, 1, small.shape[4:], f32)
    return pl.pallas_call(
        functools.partial(scatter_kernel, axes, parts, orders),
        out_shape=(
            jax.ShapeDtypeStruct(block, f32),
            jax.ShapeDtypeStruct(small.shape[4:], f32),
            jax.ShapeDtypeStruct((shards,) + note.shape, f32),
            jax.ShapeDtypeStruct(pick.shape + arrived.shape[1:], bf16),
        ),
        in_specs=[ANY, ANY, VMEM, ANY, pl.BlockSpec(memory_space=pltpu.SMEM)],
        out_specs=(VMEM, VMEM, VMEM, ANY),
        scratch_shapes=bufs
        + scatter_sems(axes, len(parts))
        + [sems(shards - 1), sems(shards - 1)]
        + [pltpu.VMEM(arrived.shape, bf16), pltpu.VMEM(pick.shape + arrived.shape[1:], bf16), sems(2)],
        compiler_params=pltpu.CompilerParams(collective_id=2, has_side_effects=True, vmem_limit_bytes=56 << 20),
        name="scatter_sums",
    )(grad, small, note, arrived, pick)


def body(
    tokens, lengths, deal_order, qkv_weight, query_bias, value_bias, out_weight, out_bias, attn_gain, attn_shift,
    up_weight, up_bias, down_weight, down_bias, ffn_gain, ffn_shift, cotangent,
):
    shards = lax.axis_size("fsdp")
    axes = mesh_axes(lax.axis_size("dp"), shards)
    devices = lax.axis_size("dp") * shards
    seqs, rows, width = tokens.shape
    hidden = up_weight.shape[1]
    chunks = hidden // width
    per = width // devices
    column = shards * seqs
    base = lax.axis_index("dp") * column
    member = lax.axis_index("fsdp")
    order = lax.dynamic_slice_in_dim(deal_order, base, column) - base
    mine = member * seqs
    own_lengths = lax.dynamic_slice_in_dim(lengths, base + mine, seqs)
    target = lax.dynamic_slice_in_dim(order, mine, seqs) // seqs
    dealt_here = mine + jnp.arange(seqs, dtype=jnp.int32)
    matches = order[None, :] == dealt_here[:, None]
    source = jnp.sum(jnp.where(matches, jnp.arange(column, dtype=jnp.int32)[None, :], 0), axis=1)
    peers = jnp.arange(shards, dtype=jnp.int32)

    choice = jnp.sum(jnp.where(source[:, None] // seqs == peers[None, :], jnp.arange(seqs, dtype=jnp.int32)[:, None], 0), axis=0)

    rank = lax.axis_index("dp") * shards + member
    vectors = [query_bias, value_bias, out_bias, attn_gain, attn_shift, down_bias, ffn_gain, ffn_shift]
    small = lax.dynamic_update_slice(jnp.zeros((16, width), bf16), jnp.stack(vectors), (0, rank * per))
    start = rank * (chunks * per)
    small = lax.dynamic_update_slice(small, up_bias[None], (8 + start // width, lax.rem(start, width)))
    if axes is None:
        gather = lambda shard: lax.all_gather(shard, BOTH, axis=0, tiled=True)
        vectors = jnp.sum(lax.all_gather(small, BOTH, axis=0, tiled=False).astype(f32), axis=0)
        w_qkv, w_out, w_up, w_down = gather(qkv_weight), gather(out_weight), gather(up_weight), gather(down_weight)
        outgoing = jnp.stack([lax.dynamic_index_in_dim(cotangent, choice[j], 0, keepdims=False) for j in range(shards)])
        cots = lax.all_to_all(outgoing, "fsdp", split_axis=0, concat_axis=0, tiled=True)
        qkv, context, probs = attention_forward(axes, own_lengths, choice, tokens, [w_qkv, vectors], None, shards)
    else:
        qkv, context, probs, w_qkv, _, w_out, w_up, w_down, cots, vectors = attention_forward(
            axes, own_lengths, choice, tokens, [qkv_weight, small, out_weight, up_weight, down_weight], cotangent, shards
        )
        w_qkv, w_out, w_up, w_down = (array.reshape(-1, array.shape[-1]) for array in (w_qkv, w_out, w_up, w_down))
    results, g_res1, g_context, dw_out, dw_up, dw_down, dvec, rms = middle(
        own_lengths, target, target, tokens, context, cots, w_out, w_up, w_down, vectors
    )
    grads = [dw_out, dw_up, dw_down]
    outs = attention_backward(axes, tokens, qkv, context, g_context, probs, g_res1, w_qkv, grads, results)
    input_grad, dw_qkv, dqv = outs[:3]
    if axes is None:
        arrived = lax.all_to_all(results, "fsdp", split_axis=0, concat_axis=0, tiled=True)
    else:
        outw_grad, upw_grad, downw_grad, arrived = outs[3:]
    packed = (dvec[:8] + dqv).reshape(8, devices, per).transpose(1, 0, 2).reshape(devices, 8 * per)
    packed = jnp.concatenate([packed, dvec[8 : 8 + chunks].reshape(devices, chunks * per)], axis=1)
    packed = jnp.pad(packed, ((0, 0), (0, 8 * 128 - packed.shape[1])))
    rms = rms.reshape(seqs * 8, 128)
    if axes is None:
        scatter = lambda array: lax.psum_scatter(array, BOTH, scatter_dimension=0, tiled=True)
        qkvw_grad = scatter(dw_qkv).astype(f32)
        outw_grad, upw_grad, downw_grad = (scatter(grad).astype(f32) for grad in grads)
        packed = scatter(packed)
        rms = lax.all_gather(rms, "fsdp", axis=0, tiled=False)
        picked = [lax.dynamic_index_in_dim(arrived, source[t] // seqs, 0, keepdims=False) for t in range(seqs)]
        layer_out = jnp.stack(picked)
    else:
        qkvw_grad, packed, rms, layer_out = scatter_sums(
            axes, dw_qkv, packed.reshape(devices * 8, 128), rms, shards, arrived, source // seqs
        )
    packed = packed.reshape(-1)
    vector = [packed[place * per : (place + 1) * per] for place in range(8)]
    rms = rms.reshape(column, 8, 128)[:, :3, 0]
    branch_rms = jnp.sum(jnp.where((source[:, None] == jnp.arange(column))[:, :, None], rms[None], 0.0), axis=1)
    return (
        layer_out, input_grad, qkvw_grad, vector[0], vector[1], outw_grad, vector[2], vector[3], vector[4], upw_grad,
        packed[8 * per : (8 + chunks) * per], downw_grad, vector[5], vector[6], vector[7], branch_rms,
    )


def solution(mesh):
    rows3, rows2, rows1 = P(BOTH, None, None), P(BOTH, None), P(BOTH)
    in_specs = (
        rows3, P(), P(), rows2, rows1, rows1, rows2, rows1, rows1, rows1, rows2, rows1, rows2, rows1, rows1, rows1, rows3,
    )
    out_specs = (
        rows3, rows3, rows2, rows1, rows1, rows2, rows1, rows1, rows1, rows2, rows1, rows2, rows1, rows1, rows1, rows2,
    )
    return jax.shard_map(body, mesh=mesh, in_specs=in_specs, out_specs=out_specs, check_vma=False)
```

```python
import functools
import math

import jax
import jax.numpy as jnp
from jax import lax
from jax.experimental import pallas as pl
from jax.experimental.pallas import tpu as pltpu
from jax.sharding import PartitionSpec as P

HEADS = 12
HEAD_DIM = 64
PAIR = 2 * HEAD_DIM
PAIRS = HEADS // 2
BLOCK = 256
ROWS = 512
PIECES = 8
ALL = slice(None)
EVERY = (ALL, ALL)

f32 = jnp.float32
bf16 = jnp.bfloat16
norm_eps = 1e-05
masked_fill = -1e30
BOTH = ("dp", "fsdp")
MESH = pl.DeviceIdType.MESH


def nn(left, right):
    return lax.dot_general(left, right, (((1,), (0,)), ((), ())), preferred_element_type=f32)


def nt(left, right):
    return lax.dot_general(left, right, (((1,), (1,)), ((), ())), preferred_element_type=f32)


def tn(left, right):
    return lax.dot_general(left, right, (((0,), (0,)), ((), ())), preferred_element_type=f32)


def block_count(length):
    return (length + (BLOCK - 1)) // BLOCK


def whole(shape):
    return pl.BlockSpec(shape, lambda *_: (0,) * len(shape), pipeline_mode=pl.Buffered(1))


def sems(*shape):
    return pltpu.SemaphoreType.DMA(shape)


def tiles(shape, block):
    return [
        (pl.ds(top, block[0]), pl.ds(left, block[1]))
        for top in range(0, shape[0], block[0])
        for left in range(0, shape[1], block[1])
    ]


ANY = pl.BlockSpec(memory_space=pl.ANY)
VMEM = pl.BlockSpec(memory_space=pltpu.VMEM)


def mesh_axes(dp, fsdp):
    if (dp, fsdp) == (8, 4):
        return (("dp", 2, 4), ("dp", 1, 2), ("fsdp", 2, 2), ("fsdp", 1, 2))
    return None


class Place:
    def __init__(self, axes):
        self.axes = axes
        self.core = len(axes) - 1
        self.at = {name: lax.axis_index(name) for name in BOTH}
        self.own = [lax.rem(self.at[name] // stride, size) for name, stride, size in axes]

    def shifted(self, dim, step):
        size = self.axes[dim][2]
        return lax.rem(self.own[dim] + step + size, size)

    def device(self, dim, step):
        name, stride, _ = self.axes[dim]
        moved = self.at[name] + (self.shifted(dim, step) - self.own[dim]) * stride
        return tuple(moved if name == axis else self.at[axis] for axis in BOTH)

    def steps(self, dim):
        return range(1, self.axes[dim][2])

    def friends(self, count):
        member = self.at["fsdp"]
        return [lax.rem(member + step, count) for step in range(1, count)]


def meet(place, friends=()):
    barrier = pltpu.get_barrier_semaphore()
    peers = [place.device(dim, step) for dim in range(len(place.axes)) for step in place.steps(dim)]
    peers += [(place.at["dp"], friend) for friend in friends]
    for peer in peers:
        pl.semaphore_signal(barrier, inc=1, device_id=peer, device_id_type=MESH)
    pl.semaphore_wait(barrier, len(peers))


def push(source, target, send, recv, device):
    return pltpu.make_async_remote_copy(source, target, send, recv, device_id=device, device_id_type=MESH)


class Exchange:
    def __init__(self, place, mine, theirs, pieces, send, recv, local):
        self.place, self.mine, self.theirs, self.pieces = place, mine, theirs, pieces
        self.send, self.recv, self.local = send, recv, local

    def copies(self, piece):
        member = self.place.at["fsdp"]
        height = self.mine.shape[1] // self.pieces
        rows = pl.ds(piece * height, height)
        made = [
            push(
                self.mine.at[friend, rows],
                self.theirs.at[member, rows],
                self.send.at[step, piece],
                self.recv.at[step, piece],
                (self.place.at["dp"], friend),
            )
            for step, friend in enumerate(self.place.friends(self.mine.shape[0]))
        ]
        return made + [pltpu.make_async_copy(self.mine.at[member, rows], self.theirs.at[member, rows], self.local.at[piece])]

    def start(self, piece):
        for copy in self.copies(piece):
            copy.start()

    def fill(self, source, choice):
        for slot in range(self.mine.shape[0]):
            self.mine[slot] = source[choice[slot]]

    def wait(self):
        for piece in range(self.pieces):
            for copy in self.copies(piece):
                copy.wait()


def exchange_sems(friends):
    return [sems(friends, PIECES), sems(friends, PIECES), sems(PIECES)]


class Gather:
    def __init__(self, place, parts, shards, outs, send, recv, core_send, core_recv, local):
        self.place, self.parts, self.shards, self.outs = place, parts, shards, outs
        self.sems = send, recv
        self.core_sems = core_send, core_recv
        self.mine = [
            pltpu.make_async_copy(shard, out.at[tuple(place.own)], local.at[i])
            for i, (shard, out) in enumerate(zip(shards, outs))
        ]

    def start(self):
        for copy in self.mine:
            copy.start()

    def local(self):
        for copy in self.mine:
            copy.wait()

    def view(self, number, spot):
        array, cut, _ = self.parts[number]
        return self.outs[array].at[tuple(spot) + cut]

    def shard(self, number):
        array, cut, _ = self.parts[number]
        return self.shards[array].at[cut]

    def known(self, number, stage):
        order = self.parts[number][2]
        return [slice(None) if dim in order[:stage] else own for dim, own in enumerate(self.place.own)]

    def link(self, number, stage):
        order = self.parts[number][2]
        spot = self.known(number, stage)
        source = self.view(number, spot) if stage else self.shard(number)
        first = sum(self.place.axes[dim][2] - 1 for dim in order[:stage])
        send, recv = self.sems
        return [
            push(
                source,
                self.view(number, spot),
                send.at[number, first + step - 1],
                recv.at[number, first + step - 1],
                self.place.device(order[stage], step),
            )
            for step in self.place.steps(order[stage])
        ]

    def across(self, number, stage):
        order = self.parts[number][2]
        core_send, core_recv = self.core_sems
        peer = self.place.device(self.place.core, 1)
        if stage == 0:
            spot = self.known(number, 0)
            return [push(self.shard(number), self.view(number, spot), core_send.at[number, 0], core_recv.at[number, 0], peer)]
        first = sum(self.place.axes[dim][2] - 1 for dim in order[: stage - 1])
        dim = order[stage - 1]
        copies = []
        for step in self.place.steps(dim):
            spot = self.known(number, stage - 1)
            spot[dim] = self.place.shifted(dim, -step)
            view, piece = self.view(number, spot), first + step
            copies.append(push(view, view, core_send.at[number, piece], core_recv.at[number, piece], peer))
        return copies

    def advance(self, number, stage):
        if stage:
            for copy in self.link(number, stage - 1):
                copy.wait_recv()
        if stage < self.place.core:
            for copy in self.link(number, stage):
                copy.start()
        for copy in self.across(number, stage):
            copy.start()

    def finish(self, number):
        for stage in range(self.place.core + 1):
            if stage < self.place.core:
                for copy in self.link(number, stage):
                    copy.wait_send()
            for copy in self.across(number, stage):
                copy.wait()


def gather_sems(axes, parts, count):
    hops = sum(size - 1 for _, _, size in axes[:-1])
    shapes = (len(parts), hops), (len(parts), hops), (len(parts), hops + 1), (len(parts), hops + 1), (count,)
    return [sems(*shape) for shape in shapes]


class Scatter:
    def __init__(self, place, parts, grads, outs, bufs, send, recv, local):
        self.place, self.parts, self.grads, self.outs = place, parts, grads, outs
        self.bufs = bufs
        self.send, self.recv, self.local = send, recv, local

    def refs(self, number):
        _, _, order, slot = self.parts[number]
        own, *came = self.bufs[order if self.parts[number][1] is not None else None]
        held = own.shape[0]
        return [own.at[slot % held]] + [buf.at[slot] for buf in came]

    def first(self, number, stage):
        order = self.parts[number][2]
        return 1 + sum(self.place.axes[dim][2] - 1 for dim in order[:stage])

    def block(self, number, core):
        array, cut, _, _ = self.parts[number]
        lead = (slice(None),) * self.place.core + (core,)
        return self.grads[array].at[lead + (EVERY if cut is None else cut)]

    def across(self, number):
        place = self.place
        return push(
            self.block(number, place.shifted(place.core, 1)),
            self.refs(number)[1],
            self.send.at[number, 0],
            self.recv.at[number, 0],
            place.device(place.core, 1),
        )

    def own(self, number):
        return pltpu.make_async_copy(
            self.block(number, self.place.own[self.place.core]), self.refs(number)[0], self.local.at[number]
        )

    def spot(self, number, stage, at):
        order = self.parts[number][2]
        dims = [slice(None)] * self.place.core
        for dim in order[:stage]:
            dims[dim] = self.place.own[dim]
        if at is not None:
            dims[order[stage]] = at
        return dims

    def link(self, number, stage, step):
        dim = self.parts[number][2][stage]
        place, refs = self.place, self.refs(number)
        piece = self.first(number, stage) + step - 1
        return push(
            refs[0].at[tuple(self.spot(number, stage, place.shifted(dim, step)))],
            refs[2 + stage].at[step - 1],
            self.send.at[number, piece],
            self.recv.at[number, piece],
            place.device(dim, step),
        )

    def add(self, number, spot, extras):
        acc = self.refs(number)[0]
        free = [dim for dim, index in enumerate(spot) if isinstance(index, slice)]
        sizes = [self.place.axes[dim][2] for dim in free]
        total = math.prod(sizes)

        def one(place, carry):
            index, where = list(spot), []
            rest = place
            for dim, size in zip(reversed(free), reversed(sizes)):
                index[dim] = lax.rem(rest, size)
                where.insert(0, index[dim])
                rest = rest // size
            index = tuple(index)
            value = acc[index].astype(f32)
            for extra in extras:
                value = value + extra[tuple(where)].astype(f32)
            acc[index] = value.astype(acc.dtype)
            return carry

        if total == 1:
            one(0, 0)
        else:
            lax.fori_loop(0, total, one, 0)

    def advance(self, number, stage):
        array, cut, order, _ = self.parts[number]
        place, refs = self.place, self.refs(number)
        if stage == 0:
            self.across(number).start()
            self.own(number).start()
            return
        if stage == 1:
            self.own(number).wait()
            self.across(number).wait_recv()
            came = [refs[1]]
        else:
            dim = order[stage - 2]
            for step in place.steps(dim):
                self.link(number, stage - 2, step).wait_recv()
            came = [refs[stage].at[step - 1] for step in place.steps(dim)]
        if stage <= place.core:
            dim = order[stage - 1]
            for step in list(place.steps(dim)) + [0]:
                at = place.shifted(dim, step)
                spot = self.spot(number, stage - 1, at)
                where = self.within(number, stage - 1, at)
                self.add(number, spot, [extra.at[where] for extra in came])
                if step:
                    self.link(number, stage - 1, step).start()
        else:
            total = refs[0][tuple(place.own[:-1])].astype(f32)
            for extra in came:
                total = total + extra[...].astype(f32)
            self.outs[array][EVERY if cut is None else cut] = total

    def within(self, number, stage, at):
        order = self.parts[number][2]
        rest = [dim for dim in range(self.place.core) if dim not in order[:stage]]
        return tuple(at if dim == order[stage] else slice(None) for dim in rest)

    def finish(self, number):
        self.across(number).wait_send()
        order = self.parts[number][2]
        for stage, dim in enumerate(order):
            for step in self.place.steps(dim):
                self.link(number, stage, step).wait_send()


def scatter_buffers(axes, order, tiles, held, block, dtype):
    sizes = [size for _, _, size in axes[:-1]]
    leads = [(held,) + tuple(sizes), (tiles,) + tuple(sizes)]
    left = list(range(len(sizes)))
    for dim in order:
        left.remove(dim)
        leads.append((tiles, sizes[dim] - 1) + tuple(sizes[other] for other in left))
    return [pltpu.VMEM(lead + tuple(block), dtype) for lead in leads]


def scatter_sems(axes, count):
    hops = 1 + sum(size - 1 for _, _, size in axes[:-1])
    return [sems(count, hops), sems(count, hops), sems(count)]


def run_steps(mover, exchange, plan, dealt, time, steps, first=0):
    for step in range(first, steps):
        todo = [(part, stage) for part, row in plan.items() for stage, at in enumerate(row) if at == step]
        pieces = [piece for piece, at in enumerate(dealt) if at == step]

        @pl.when(time == step)
        def _(todo=todo, pieces=pieces):
            for part, stage in todo:
                mover.advance(part, stage)
            for piece in pieces:
                exchange.start(piece)


def run_rest(mover, exchange, plan, steps):
    for part, row in plan.items():
        for stage, at in enumerate(row):
            if at >= steps:
                mover.advance(part, stage)
    for part in plan:
        mover.finish(part)
    exchange.wait()


def forward_kernel(axes, seqs, parts, early, plan, dealt, len_ref, choice_ref, x_ref, *refs):
    seq, pair = pl.program_id(0), pl.program_id(1)
    time = seq * PAIRS + pair
    steps = seqs * PAIRS
    length = len_ref[seq]
    count, width = x_ref.shape[1], x_ref.shape[2]
    lane = lax.broadcasted_iota(jnp.int32, (1, PAIR), 1)
    if axes is None:
        w_ref, vec_ref, qkv_ref, ctx_ref, probs_ref = refs
    else:
        shards, cot_ref, qkv_ref, ctx_ref, probs_ref = refs[:5], refs[5], refs[6], refs[7], refs[8]
        gathered, cots_ref, vec_ref = refs[9:14], refs[14], refs[15]
        w_ref, raw_ref, small_ref, held_ref, going_ref, copy_sems = refs[16:22]
        place = Place(axes)
        gather = Gather(place, parts, shards, gathered, *refs[22:27])
        exchange = Exchange(place, going_ref, cots_ref, PIECES, *refs[27:30])

        @pl.when(time == 0)
        def _():
            now = [
                pltpu.make_async_copy(cot_ref, held_ref, copy_sems.at[0]),
                pltpu.make_async_copy(gathered[0], raw_ref, copy_sems.at[1]),
                pltpu.make_async_copy(gathered[1], small_ref, copy_sems.at[2]),
            ]
            now[0].start()
            meet(place, place.friends(cots_ref.shape[0]))
            gather.start()
            for part in list(early) + list(plan):
                gather.advance(part, 0)
            now[0].wait()
            exchange.fill(held_ref, choice_ref)
            gather.local()
            for stage in range(1, place.core + 1):
                for part in early:
                    gather.advance(part, stage)
                for part, row in plan.items():
                    if stage == 1 and row[1] == 0:
                        gather.advance(part, 1)
                for piece, at in enumerate(dealt):
                    if stage == 2 and at == 0:
                        exchange.start(piece)
            for part in early:
                gather.finish(part)
            for copy in now[1:]:
                copy.start()
            for copy in now[1:]:
                copy.wait()
            depth, across, along, _ = raw_ref.shape[:4]
            height = 2 * raw_ref.shape[4]

            def one(block, total):
                spot = block // (across * along), lax.rem(block // along, across), lax.rem(block, along)
                both = jnp.concatenate([raw_ref[spot + (half,)].astype(f32) for half in range(2)], axis=0)
                w_ref[pl.ds(pl.multiple_of(block * height, height), height), :] = both.astype(bf16)
                return total + small_ref[spot + (0,)].astype(f32) + small_ref[spot + (1,)].astype(f32)

            vec_ref[...] = lax.fori_loop(0, depth * across * along, one, jnp.zeros((16, width), f32))

        run_steps(gather, exchange, plan, dealt, time, steps, 1)

    @pl.when(pair == 0)
    def _():
        tokens = x_ref[0]
        step = 2 * PAIR
        for start in range(0, 3 * width, step):
            part = start // width
            projected = nn(tokens, w_ref[:, start : start + step])
            if part != 1:
                cols = slice(start - part * width, start - part * width + step)
                projected = projected + vec_ref[part // 2 : part // 2 + 1, cols]
            projected = projected.astype(bf16)
            if part == 0:
                projected = projected * jnp.asarray(1.0 / math.sqrt(HEAD_DIM), bf16)
            for half in range(2):
                qkv_ref[0, start // PAIR + half] = projected[:, half * PAIR : (half + 1) * PAIR]

    key = qkv_ref[0, PAIRS + pair]
    value = qkv_ref[0, 2 * PAIRS + pair]
    unusable = lax.broadcasted_iota(jnp.int32, (count, 1), 0) >= length
    mask = jnp.where(unusable, masked_fill, 0.0).astype(bf16)
    keys = [jnp.where(lane == spare, mask, key) for spare in (PAIR - 1, 0)]
    for start in range(0, count, ROWS):
        rows = slice(start, start + ROWS)
        query = qkv_ref[0, pair, rows, :]
        outs = []
        for head in range(2):
            mine = (lane < HEAD_DIM) if head == 0 else (lane >= HEAD_DIM)
            spare = jnp.where(lane == (PAIR - 1 if head == 0 else 0), 1.0, 0.0).astype(bf16)
            scores = nt(jnp.where(mine, query, spare), keys[head])
            top = jnp.max(scores, axis=1, keepdims=True)
            powers = jnp.exp(scores - top)
            total = jnp.sum(powers, axis=1, keepdims=True)
            probs = (powers * (1.0 / total)).astype(bf16)
            probs_ref[0, 0, head, rows, :] = probs
            outs.append(nn(probs, value))
        ctx_ref[0, rows, :] = jnp.where(lane < HEAD_DIM, outs[0], outs[1]).astype(bf16)

    if axes is not None:

        @pl.when(time == steps - 1)
        def _():
            run_rest(gather, exchange, plan, steps)


def attention_forward(axes, lengths, choice, tokens, operands, cotangent, shards):
    seqs, rows, width = tokens.shape
    out_shape = [
        jax.ShapeDtypeStruct((seqs, 3 * PAIRS, rows, PAIR), bf16),
        jax.ShapeDtypeStruct((seqs, rows, width), bf16),
        jax.ShapeDtypeStruct((seqs, PAIRS, 2, rows, rows), bf16),
    ]
    in_specs = [pl.BlockSpec((1, rows, width), lambda s, p, *_: (s, 0, 0))]
    out_specs = [
        pl.BlockSpec((1, 3 * PAIRS, rows, PAIR), lambda s, p, *_: (s, 0, 0, 0)),
        pl.BlockSpec((1, rows, PAIR), lambda s, p, *_: (s, 0, p)),
        pl.BlockSpec((1, 1, 2, rows, rows), lambda s, p, *_: (s, p, 0, 0, 0)),
    ]
    scratch, parts, early, plan, dealt, talk = [], [], [], {}, [], {}
    extra = list(operands)
    if axes is None:
        in_specs += [whole(array.shape) for array in operands]
    else:
        orders = ((0, 2, 1), (0, 2, 1), (1, 0, 2))
        first, small, *later = operands
        parts.append((1, EVERY, orders[0]))
        for cut in tiles(first.shape, (first.shape[0], first.shape[1] // 6)):
            parts.append((0, cut, orders[(len(parts) - 1) % 3]))
        early = range(len(parts))
        for array, shard in enumerate(later, 2):
            parts += [(array, cut, (2, 0, 1)) for cut in tiles(shard.shape, (first.shape[0], width))]
        for place in range(len(parts) - len(early)):
            at = max(0, place - 2)
            plan[place + len(early)] = [0, at, at + (1 if place < 2 else 2), at + (3 if place < 2 else 4)]
        dealt = [max(0, piece - 1) for piece in range(PIECES)]
        extra += [cotangent]
        in_specs += [ANY] * len(extra)
        sizes = tuple(size for _, _, size in axes)
        out_shape += [jax.ShapeDtypeStruct(sizes + shard.shape, bf16) for shard in operands]
        out_shape += [jax.ShapeDtypeStruct((shards, rows, width), bf16), jax.ShapeDtypeStruct(small.shape, f32)]
        out_specs += [ANY] * (len(operands) + 1) + [whole(small.shape)]
        scratch = [
            pltpu.VMEM((width, first.shape[1]), bf16),
            pltpu.VMEM(sizes + first.shape, bf16),
            pltpu.VMEM(sizes + small.shape, bf16),
            pltpu.VMEM(cotangent.shape, bf16),
            pltpu.VMEM((shards, rows, width), bf16),
            sems(3),
        ]
        scratch += gather_sems(axes, parts, len(operands)) + exchange_sems(shards - 1)
        talk = {"collective_id": 3, "has_side_effects": True}
    return pl.pallas_call(
        functools.partial(forward_kernel, axes, seqs, parts, early, plan, dealt),
        out_shape=tuple(out_shape),
        grid_spec=pltpu.PrefetchScalarGridSpec(
            num_scalar_prefetch=2,
            grid=(seqs, PAIRS),
            in_specs=in_specs,
            out_specs=tuple(out_specs),
            scratch_shapes=scratch,
        ),
        compiler_params=pltpu.CompilerParams(vmem_limit_bytes=60 << 20, **talk),
        cost_estimate=pl.CostEstimate(flops=60_000_000_000, transcendentals=30_000_000, bytes_accessed=80_000_000),
        name="attention_forward",
    )(lengths, choice, tokens, *extra)


def normal_tail(values):
    size = jnp.abs(values)
    bell = jnp.exp(-0.5 * values * values)
    t = 1.0 / (1.0 + (0.3275911 / math.sqrt(2.0)) * size)
    poly = t * (
        0.5 * 0.254829592
        + t * (0.5 * -0.284496736 + t * (0.5 * 1.421413741 + t * (0.5 * -1.453152027 + t * (0.5 * 1.061405429))))
    )
    tail = poly * bell
    return jnp.where(values >= 0, 1.0 - tail, tail), bell


def row_mean(values):
    return jnp.mean(values, axis=-1, keepdims=True)


def middle_kernel(
    len_ref, in_slot, out_slot, x_ref, ctx_ref, cot_ref, wo_ref, wu_ref, wd_ref, vec_ref,
    out_ref, gres_ref, gctx_ref, dwo_ref, dwu_ref, dwd_ref, dvec_ref, rms_ref,
    acc_o, acc_u, acc_d, active, slope, sums, stage, sems,
):
    seq, index = pl.program_id(0), pl.program_id(1)
    first = jnp.logical_and(seq == 0, index == 0)
    final = jnp.logical_and(seq == pl.num_programs(0) - 1, index == pl.num_programs(1) - 1)
    length = len_ref[seq]
    width = x_ref.shape[2]
    chunks = wu_ref.shape[1] // width
    tile = lambda place: slice(place * width, (place + 1) * width)

    @pl.when(first)
    def _():
        acc_o[...] = jnp.zeros_like(acc_o)
        acc_u[...] = jnp.zeros_like(acc_u)
        acc_d[...] = jnp.zeros_like(acc_d)
        dvec_ref[...] = jnp.zeros_like(dvec_ref)

    @pl.when(index == 0)
    def _():
        sums[...] = jnp.zeros_like(sums)

    @pl.when(index * BLOCK >= length)
    def _():
        out_ref[...] = jnp.zeros_like(out_ref)
        gres_ref[...] = jnp.zeros_like(gres_ref)
        gctx_ref[...] = jnp.zeros_like(gctx_ref)

    @pl.when(index * BLOCK < length)
    def _():
        vec = lambda place: vec_ref[place : place + 1, :]
        bias_out, gain_a, shift_a, bias_down, gain_f, shift_f = (vec(place) for place in range(2, 8))
        valid = (lax.broadcasted_iota(jnp.int32, (BLOCK, 1), 0) + index * BLOCK < length).astype(f32)
        tokens = x_ref[0].astype(f32)
        context = ctx_ref[0]
        branch_a = nn(context, wo_ref[...]) + bias_out
        mixed = tokens + branch_a
        center = mixed - row_mean(mixed)
        scale_a = lax.rsqrt(row_mean(center * center) + norm_eps)
        hat_a = center * scale_a
        hidden = hat_a * gain_a + shift_a
        hidden_low = hidden.astype(bf16)
        branch_f = bias_down
        for chunk in range(chunks):
            cols = tile(chunk)
            gate = nn(hidden_low, wu_ref[:, cols]) + vec(8 + chunk)
            share, bell = normal_tail(gate)
            act = (gate * share).astype(bf16)
            active[:, cols] = act
            slope[:, cols] = share + gate * bell * (1.0 / math.sqrt(2.0 * math.pi))
            branch_f = branch_f + nn(act, wd_ref[cols, :])
        mixed_f = hidden + branch_f
        center = mixed_f - row_mean(mixed_f)
        scale_f = lax.rsqrt(row_mean(center * center) + norm_eps)
        hat_f = center * scale_f
        out_ref[0] = ((hat_f * gain_f + shift_f) * valid).astype(bf16)
        g_result = cot_ref[0].astype(f32) * valid
        g_hat = g_result * gain_f
        g_res2 = scale_f * (g_hat - row_mean(g_hat) - hat_f * row_mean(g_hat * hat_f))
        g_ffn = g_res2.astype(bf16)
        g_hidden = g_res2
        for chunk in range(chunks):
            cols = tile(chunk)
            g_gate = nt(g_ffn, wd_ref[cols, :]) * slope[:, cols]
            g_low = g_gate.astype(bf16)
            acc_d[cols, :] += tn(active[:, cols], g_ffn)
            acc_u[:, cols] += tn(hidden_low, g_low)
            dvec_ref[8 + chunk : 9 + chunk, :] += jnp.sum(g_low.astype(f32), axis=0, keepdims=True)
            g_hidden = g_hidden + nt(g_low, wu_ref[:, cols])
        g_hat = g_hidden * gain_a
        g_res1 = scale_a * (g_hat - row_mean(g_hat) - hat_a * row_mean(g_hat * hat_a))
        g_attn = g_res1.astype(bf16)
        gres_ref[0] = g_res1
        gctx_ref[0] = nt(g_attn, wo_ref[...]).astype(bf16)
        acc_o[...] += tn(context, g_attn)
        column = lambda values: jnp.sum(values, axis=0, keepdims=True)
        dvec_ref[2:3, :] += column(g_attn.astype(f32))
        dvec_ref[3:4, :] += column(g_hidden * hat_a)
        dvec_ref[4:5, :] += column(g_hidden)
        dvec_ref[5:6, :] += column(g_ffn.astype(f32))
        dvec_ref[6:7, :] += column(g_result * hat_f)
        dvec_ref[7:8, :] += column(g_result)
        sums[0:1, :] += column(tokens * tokens * valid)
        sums[1:2, :] += column(branch_a * branch_a * valid)
        sums[2:3, :] += column(branch_f * branch_f * valid)

    @pl.when(index == pl.num_programs(1) - 1)
    def _():
        mean = jnp.sum(sums[...], axis=1, keepdims=True) / (length * width).astype(f32)
        rms_ref[0] = jnp.broadcast_to(jnp.sqrt(mean), rms_ref.shape[1:])

    @pl.when(final)
    def _():
        pieces = [(acc_o, dwo_ref, EVERY)]
        pieces += [(acc_u, dwu_ref, (ALL, tile(chunk))) for chunk in range(chunks)]
        pieces += [(acc_d, dwd_ref, (tile(chunk), ALL)) for chunk in range(chunks)]
        copies = []
        for place, (acc, out, cut) in enumerate(pieces):
            slot = place % 2
            if place >= 2:
                copies[place - 2].wait()
            stage[slot] = acc[cut].astype(bf16)
            copies.append(pltpu.make_async_copy(stage.at[slot], out.at[cut], sems.at[slot]))
            copies[-1].start()
        copies[-2].wait()
        copies[-1].wait()


def middle(lengths, in_slot, out_slot, tokens, context, cots, w_out, w_up, w_down, vectors):
    seqs, rows, width = tokens.shape
    slots = cots.shape[0]
    hidden = w_up.shape[1]
    inside = lambda s, i, lens: jnp.minimum(i, block_count(lens[s]) - 1)
    here = pl.BlockSpec((1, BLOCK, width), lambda s, i, lens, a, b: (s, inside(s, i, lens), 0))
    there = pl.BlockSpec((1, BLOCK, width), lambda s, i, *_: (s, i, 0))
    flops = 6 * seqs * rows * (width * width + 2 * width * hidden)
    return pl.pallas_call(
        middle_kernel,
        out_shape=(
            jax.ShapeDtypeStruct((slots, rows, width), bf16),
            jax.ShapeDtypeStruct((seqs, rows, width), f32),
            jax.ShapeDtypeStruct((seqs, rows, width), bf16),
            jax.ShapeDtypeStruct(w_out.shape, bf16),
            jax.ShapeDtypeStruct(w_up.shape, bf16),
            jax.ShapeDtypeStruct(w_down.shape, bf16),
            jax.ShapeDtypeStruct((16, width), f32),
            jax.ShapeDtypeStruct((seqs, 8, 128), f32),
        ),
        grid_spec=pltpu.PrefetchScalarGridSpec(
            num_scalar_prefetch=3,
            grid=(seqs, rows // BLOCK),
            in_specs=[
                here,
                here,
                pl.BlockSpec((1, BLOCK, width), lambda s, i, lens, a, b: (a[s], inside(s, i, lens), 0)),
                whole(w_out.shape),
                whole(w_up.shape),
                whole(w_down.shape),
                whole(vectors.shape),
            ],
            out_specs=[
                pl.BlockSpec((1, BLOCK, width), lambda s, i, lens, a, b: (b[s], i, 0)),
                there,
                there,
                ANY,
                ANY,
                ANY,
                whole((16, width)),
                pl.BlockSpec((1, 8, 128), lambda s, i, *_: (s, 0, 0)),
            ],
            scratch_shapes=[
                pltpu.VMEM(w_out.shape, f32),
                pltpu.VMEM(w_up.shape, f32),
                pltpu.VMEM(w_down.shape, f32),
                pltpu.VMEM((BLOCK, hidden), bf16),
                pltpu.VMEM((BLOCK, hidden), f32),
                pltpu.VMEM((8, width), f32),
                pltpu.VMEM((2, width, width), bf16),
                pltpu.SemaphoreType.DMA((2,)),
            ],
        ),
        compiler_params=pltpu.CompilerParams(vmem_limit_bytes=60 << 20),
        cost_estimate=pl.CostEstimate(flops=flops, transcendentals=seqs * rows * hidden, bytes_accessed=60_000_000),
        name="middle",
    )(lengths, in_slot, out_slot, tokens, context, cots, w_out, w_up, w_down, vectors)


def backward_kernel(axes, seqs, parts, plan, dealt, x_ref, qkv_in, ctx_ref, gctx_ref, probs_ref, gres_ref, w_ref, *refs):
    if axes is None:
        gin_ref, dw_ref, dvec_ref = refs[:3]
        mixed, acc_w, stage, copy_sems = refs[3:]
    else:
        grads, result_ref, gin_ref, dw_ref, dvec_ref = refs[:3], refs[3], refs[4], refs[5], refs[6]
        summed, arrived_ref = refs[7:10], refs[10]
        mixed, acc_w, stage, copy_sems = refs[11:15]
        place = Place(axes)
        bufs = {parts[0][2]: refs[15:20]}
        scatter = Scatter(place, parts, grads, summed, bufs, *refs[20:23])
        exchange = Exchange(place, result_ref, arrived_ref, PIECES, *refs[23:26])
    seq, pair = pl.program_id(0), pl.program_id(1)
    time = seq * PAIRS + pair
    steps = seqs * PAIRS
    count, width = x_ref.shape[1], x_ref.shape[2]
    lane = lax.broadcasted_iota(jnp.int32, (1, PAIR), 1)

    if axes is not None:

        @pl.when(time == 0)
        def _():
            meet(place, place.friends(result_ref.shape[0]))

        run_steps(scatter, exchange, plan, dealt, time, steps)

    @pl.when(time == 0)
    def _():
        acc_w[...] = jnp.zeros_like(acc_w)
        dvec_ref[...] = jnp.zeros_like(dvec_ref)

    key = qkv_in[0, 1, 0]
    value = qkv_in[0, 2, 0]
    g_key, g_value = [0.0, 0.0], [0.0, 0.0]
    for start in range(0, count, ROWS):
        rows = slice(start, start + ROWS)
        query = qkv_in[0, 0, 0, rows, :]
        grad = gctx_ref[0, rows, :]
        agree = grad.astype(f32) * ctx_ref[0, rows, :].astype(f32)
        query_t, grad_t = query.T, grad.T
        g_query = jnp.zeros((ROWS, PAIR), f32)
        for head in range(2):
            mine = (lane < HEAD_DIM) if head == 0 else (lane >= HEAD_DIM)
            only = lambda values: jnp.where(mine, values, jnp.zeros_like(values))
            lanes = slice(head * HEAD_DIM, (head + 1) * HEAD_DIM)
            delta = jnp.sum(only(agree), axis=1, keepdims=True)
            probs = probs_ref[0, 0, head, rows, :]
            g_probs = nt(only(grad), value)
            g_scores = (probs.astype(f32) * (g_probs - delta)).astype(bf16)
            g_query = g_query + nn(g_scores, only(key))
            g_key[head] = g_key[head] + nn(query_t[lanes], g_scores)
            g_value[head] = g_value[head] + nn(grad_t[lanes], probs)
        mixed[pair, rows, :] = (g_query * (1.0 / math.sqrt(HEAD_DIM))).astype(bf16)
    mixed[PAIRS + pair] = jnp.concatenate(g_key, axis=0).T.astype(bf16)
    mixed[2 * PAIRS + pair] = jnp.concatenate(g_value, axis=0).T.astype(bf16)

    @pl.when(pair == PAIRS - 1)
    def _():
        @pl.loop(0, count // BLOCK)
        def _(index):
            rows = pl.ds(pl.multiple_of(index * BLOCK, BLOCK), BLOCK)
            tokens = x_ref[0, rows, :]
            g_in = gres_ref[0, rows, :]
            for part in range(3):
                cols = slice(part * width, (part + 1) * width)
                piece = jnp.concatenate([mixed[part * PAIRS + head, rows, :] for head in range(PAIRS)], axis=1)
                g_in = g_in + nt(piece, w_ref[:, cols])
                acc_w[:, cols] += tn(tokens, piece)
                if part != 1:
                    dvec_ref[part // 2 : part // 2 + 1, :] += jnp.sum(piece.astype(f32), axis=0, keepdims=True)
            gin_ref[0, rows, :] = g_in.astype(bf16)

    @pl.when(time == steps - 1)
    def _():
        copies = []
        for part in range(3):
            cols = slice(part * width, (part + 1) * width)
            slot = part % 2
            if part >= 2:
                copies[part - 2].wait()
            stage[slot] = acc_w[:, cols].astype(bf16)
            copies.append(pltpu.make_async_copy(stage.at[slot], dw_ref.at[:, cols], copy_sems.at[slot]))
            copies[-1].start()
        copies[-2].wait()
        copies[-1].wait()
        if axes is not None:
            run_rest(scatter, exchange, plan, steps)


def attention_backward(axes, tokens, qkv, context, g_context, probs, g_res1, w_qkv, grads, results):
    seqs, rows, width = tokens.shape
    pair_cols = pl.BlockSpec((1, rows, PAIR), lambda s, p: (s, 0, p))
    seq_rows = pl.BlockSpec((1, rows, width), lambda s, p: (s, 0, 0))
    in_specs = [
        seq_rows,
        pl.BlockSpec((1, 3, 1, rows, PAIR), lambda s, p: (s, 0, p, 0, 0)),
        pair_cols,
        pair_cols,
        pl.BlockSpec((1, 1, 2, rows, rows), lambda s, p: (s, p, 0, 0, 0)),
        seq_rows,
        whole(w_qkv.shape),
    ]
    out_shape = [
        jax.ShapeDtypeStruct((seqs, rows, width), bf16),
        jax.ShapeDtypeStruct(w_qkv.shape, bf16),
        jax.ShapeDtypeStruct((8, width), f32),
    ]
    out_specs = [seq_rows, ANY, whole((8, width))]
    scratch = [
        pltpu.VMEM((3 * PAIRS, rows, PAIR), bf16),
        pltpu.VMEM(w_qkv.shape, f32),
        pltpu.VMEM((2, width, width), bf16),
        sems(2),
    ]
    extra, parts, plan, dealt, talk = [], [], {}, [], {}
    if axes is not None:
        sizes = tuple(size for _, _, size in axes)
        order = (1, 0, 2)
        grads = [grad.reshape(sizes + (-1, grad.shape[1])) for grad in grads]
        block = (grads[0].shape[4], width)
        for array, grad in enumerate(grads):
            parts += [(array, cut, order, len(parts) + i) for i, cut in enumerate(tiles(grad.shape[4:], block))]
        for place in range(len(parts)):
            at = max(0, place - 2)
            plan[place] = [at] + [2 * stage - 1 + at for stage in range(1, 5)]
        dealt = [piece + 2 for piece in range(PIECES)]
        extra = grads + [results]
        in_specs += [ANY] * len(extra)
        out_shape += [jax.ShapeDtypeStruct(grad.shape[4:], f32) for grad in grads]
        out_shape += [jax.ShapeDtypeStruct(results.shape, bf16)]
        out_specs += [whole(grad.shape[4:]) for grad in grads] + [ANY]
        friends = results.shape[0] - 1
        scratch += scatter_buffers(axes, order, len(parts), len(parts), block, bf16)
        scratch += scatter_sems(axes, len(parts)) + exchange_sems(friends)
        talk = {"collective_id": 4, "has_side_effects": True}
    return pl.pallas_call(
        functools.partial(backward_kernel, axes, seqs, parts, plan, dealt),
        out_shape=tuple(out_shape),
        grid_spec=pltpu.PrefetchScalarGridSpec(
            num_scalar_prefetch=0,
            grid=(seqs, PAIRS),
            in_specs=in_specs,
            out_specs=tuple(out_specs),
            scratch_shapes=scratch,
        ),
        compiler_params=pltpu.CompilerParams(vmem_limit_bytes=62 << 20, **talk),
        cost_estimate=pl.CostEstimate(flops=120_000_000_000, transcendentals=1, bytes_accessed=100_000_000),
        name="attention_backward",
    )(tokens, qkv.reshape(seqs, 3, PAIRS, rows, PAIR), context, g_context, probs, g_res1, w_qkv, *extra)


def scatter_kernel(axes, parts, orders, *refs):
    grad_ref, small_ref, note_ref, arrived_ref, pick_ref, out_ref, out_small, notes_ref, layer_ref = refs[:9]
    came, kept, layer_sems = refs[-3:]
    refs = refs[3:-3]
    fetch = pltpu.make_async_copy(arrived_ref, came, layer_sems.at[0])
    store = pltpu.make_async_copy(kept, layer_ref, layer_sems.at[1])
    fetch.start()
    place = Place(axes)
    member = place.at["fsdp"]
    friends = place.friends(notes_ref.shape[0])
    bufs = {order: refs[6 + 5 * i : 11 + 5 * i] for i, order in enumerate(orders + (None,))}
    rest = refs[6 + 5 * (len(orders) + 1) :]
    scatter = Scatter(place, parts, [grad_ref, small_ref], [out_ref, out_small], bufs, *rest[:3])
    meet(place, friends)
    told = [
        push(note_ref, notes_ref.at[member], rest[3].at[step], rest[4].at[step], (place.at["dp"], friend))
        for step, friend in enumerate(friends)
    ]
    for copy in told:
        copy.start()
    notes_ref[member] = note_ref[...]
    for stage in range(place.core + 2):
        for part in range(len(parts)):
            scatter.advance(part, stage)
        if stage == 1:
            fetch.wait()
            for slot in range(kept.shape[0]):
                kept[slot] = came[pick_ref[slot]]
            store.start()
    store.wait()
    for copy in told:
        copy.wait()
    for part in range(len(parts)):
        scatter.finish(part)


def scatter_sums(axes, grad, small, note, shards, arrived, pick):
    sizes = tuple(size for _, _, size in axes)
    grad = grad.reshape(sizes + (-1, grad.shape[1]))
    small = small.reshape(sizes + (-1, small.shape[1]))
    block = grad.shape[4:]
    orders = ((2, 1, 0), (1, 2, 0))
    cut = block[1] // 6
    parts = [(0, (ALL, pl.ds(place * cut, cut)), orders[place % 2], place // 2) for place in range(6)]
    parts.insert(0, (1, None, orders[0], 0))
    bufs = [buf for order in orders for buf in scatter_buffers(axes, order, 3, 3, (block[0], cut), bf16)]
    bufs += scatter_buffers(axes, orders[0], 1, 1, small.shape[4:], f32)
    return pl.pallas_call(
        functools.partial(scatter_kernel, axes, parts, orders),
        out_shape=(
            jax.ShapeDtypeStruct(block, f32),
            jax.ShapeDtypeStruct(small.shape[4:], f32),
            jax.ShapeDtypeStruct((shards,) + note.shape, f32),
            jax.ShapeDtypeStruct(pick.shape + arrived.shape[1:], bf16),
        ),
        in_specs=[ANY, ANY, VMEM, ANY, pl.BlockSpec(memory_space=pltpu.SMEM)],
        out_specs=(VMEM, VMEM, VMEM, ANY),
        scratch_shapes=bufs
        + scatter_sems(axes, len(parts))
        + [sems(shards - 1), sems(shards - 1)]
        + [pltpu.VMEM(arrived.shape, bf16), pltpu.VMEM(pick.shape + arrived.shape[1:], bf16), sems(2)],
        compiler_params=pltpu.CompilerParams(collective_id=2, has_side_effects=True, vmem_limit_bytes=56 << 20),
        name="scatter_sums",
    )(grad, small, note, arrived, pick)


def body(
    tokens, lengths, deal_order, qkv_weight, query_bias, value_bias, out_weight, out_bias, attn_gain, attn_shift,
    up_weight, up_bias, down_weight, down_bias, ffn_gain, ffn_shift, cotangent,
):
    shards = lax.axis_size("fsdp")
    axes = mesh_axes(lax.axis_size("dp"), shards)
    devices = lax.axis_size("dp") * shards
    seqs, rows, width = tokens.shape
    hidden = up_weight.shape[1]
    chunks = hidden // width
    per = width // devices
    column = shards * seqs
    base = lax.axis_index("dp") * column
    member = lax.axis_index("fsdp")
    order = lax.dynamic_slice_in_dim(deal_order, base, column) - base
    mine = member * seqs
    own_lengths = lax.dynamic_slice_in_dim(lengths, base + mine, seqs)
    target = lax.dynamic_slice_in_dim(order, mine, seqs) // seqs
    dealt_here = mine + jnp.arange(seqs, dtype=jnp.int32)
    matches = order[None, :] == dealt_here[:, None]
    source = jnp.sum(jnp.where(matches, jnp.arange(column, dtype=jnp.int32)[None, :], 0), axis=1)
    peers = jnp.arange(shards, dtype=jnp.int32)

    choice = jnp.sum(jnp.where(source[:, None] // seqs == peers[None, :], jnp.arange(seqs, dtype=jnp.int32)[:, None], 0), axis=0)

    rank = lax.axis_index("dp") * shards + member
    vectors = [query_bias, value_bias, out_bias, attn_gain, attn_shift, down_bias, ffn_gain, ffn_shift]
    small = lax.dynamic_update_slice(jnp.zeros((16, width), bf16), jnp.stack(vectors), (0, rank * per))
    start = rank * (chunks * per)
    small = lax.dynamic_update_slice(small, up_bias[None], (8 + start // width, lax.rem(start, width)))
    if axes is None:
        gather = lambda shard: lax.all_gather(shard, BOTH, axis=0, tiled=True)
        vectors = jnp.sum(lax.all_gather(small, BOTH, axis=0, tiled=False).astype(f32), axis=0)
        w_qkv, w_out, w_up, w_down = gather(qkv_weight), gather(out_weight), gather(up_weight), gather(down_weight)
        outgoing = jnp.stack([lax.dynamic_index_in_dim(cotangent, choice[j], 0, keepdims=False) for j in range(shards)])
        cots = lax.all_to_all(outgoing, "fsdp", split_axis=0, concat_axis=0, tiled=True)
        qkv, context, probs = attention_forward(axes, own_lengths, choice, tokens, [w_qkv, vectors], None, shards)
    else:
        qkv, context, probs, w_qkv, _, w_out, w_up, w_down, cots, vectors = attention_forward(
            axes, own_lengths, choice, tokens, [qkv_weight, small, out_weight, up_weight, down_weight], cotangent, shards
        )
        w_qkv, w_out, w_up, w_down = (array.reshape(-1, array.shape[-1]) for array in (w_qkv, w_out, w_up, w_down))
    results, g_res1, g_context, dw_out, dw_up, dw_down, dvec, rms = middle(
        own_lengths, target, target, tokens, context, cots, w_out, w_up, w_down, vectors
    )
    grads = [dw_out, dw_up, dw_down]
    outs = attention_backward(axes, tokens, qkv, context, g_context, probs, g_res1, w_qkv, grads, results)
    input_grad, dw_qkv, dqv = outs[:3]
    if axes is None:
        arrived = lax.all_to_all(results, "fsdp", split_axis=0, concat_axis=0, tiled=True)
    else:
        outw_grad, upw_grad, downw_grad, arrived = outs[3:]
    packed = (dvec[:8] + dqv).reshape(8, devices, per).transpose(1, 0, 2).reshape(devices, 8 * per)
    packed = jnp.concatenate([packed, dvec[8 : 8 + chunks].reshape(devices, chunks * per)], axis=1)
    packed = jnp.pad(packed, ((0, 0), (0, 8 * 128 - packed.shape[1])))
    rms = rms.reshape(seqs * 8, 128)
    if axes is None:
        scatter = lambda array: lax.psum_scatter(array, BOTH, scatter_dimension=0, tiled=True)
        qkvw_grad = scatter(dw_qkv).astype(f32)
        outw_grad, upw_grad, downw_grad = (scatter(grad).astype(f32) for grad in grads)
        packed = scatter(packed)
        rms = lax.all_gather(rms, "fsdp", axis=0, tiled=False)
        picked = [lax.dynamic_index_in_dim(arrived, source[t] // seqs, 0, keepdims=False) for t in range(seqs)]
        layer_out = jnp.stack(picked)
    else:
        qkvw_grad, packed, rms, layer_out = scatter_sums(
            axes, dw_qkv, packed.reshape(devices * 8, 128), rms, shards, arrived, source // seqs
        )
    packed = packed.reshape(-1)
    vector = [packed[place * per : (place + 1) * per] for place in range(8)]
    rms = rms.reshape(column, 8, 128)[:, :3, 0]
    branch_rms = jnp.sum(jnp.where((source[:, None] == jnp.arange(column))[:, :, None], rms[None], 0.0), axis=1)
    return (
        layer_out, input_grad, qkvw_grad, vector[0], vector[1], outw_grad, vector[2], vector[3], vector[4], upw_grad,
        packed[8 * per : (8 + chunks) * per], downw_grad, vector[5], vector[6], vector[7], branch_rms,
    )


def solution(mesh):
    rows3, rows2, rows1 = P(BOTH, None, None), P(BOTH, None), P(BOTH)
    in_specs = (
        rows3, P(), P(), rows2, rows1, rows1, rows2, rows1, rows1, rows1, rows2, rows1, rows2, rows1, rows1, rows1, rows3,
    )
    out_specs = (
        rows3, rows3, rows2, rows1, rows1, rows2, rows1, rows1, rows1, rows2, rows1, rows2, rows1, rows1, rows1, rows2,
    )
    return jax.shard_map(body, mesh=mesh, in_specs=in_specs, out_specs=out_specs, check_vma=False)
```
